256 devices in a mesh: rve: 32 (over z, x), mic: 4 (over y), mac: 2 (over core).
Axes of the slice: x: 4, y: 4, z: 8, core: 2. Of those that a mesh axis runs over, the one named last changes fastest.
Arguments:
- displacement: float32 [3, 32, 8, 8], P(None, 'rve', ('mic', 'mac')), may hold values from -3 to 3
- plastic: float32 [2048, 6, 16, 256], P(('rve', 'mic', 'mac')), may hold values from -0.3 to 0.3
- bulk_modulus: float32 [16, 256], replicated, may hold values from 1 to 3
- shear_modulus: float32 [16, 256], replicated, may hold values from 0.5 to 1.5
- yield_radius: float32 [16, 256], replicated, may hold values from 0.05 to 0.3
- counts: int32 [2048], P(('rve', 'mic', 'mac')), may hold values from 0 to 3
- migration_plan: int32 [2048], P(('rve', 'mic', 'mac')), may hold values from 0 to 2047, as said below
Outputs:
- nodal_force: float32 [3, 32, 8, 8], P(None, 'rve', ('mic', 'mac'))
- plastic_new: float32 [2048, 6, 16, 256], P(('rve', 'mic', 'mac'))
The draws below stay inside these ranges and needn't reach their ends.
Inputs may be any that keep to these rules, and one draw needn't show every extreme that they name: migration_plan is a permutation of 0 .. 2047. It keeps an RVE within the devices that share its mic and mac index; each device sends exactly 2 of its RVEs to each of 4 devices along rve and none to the others, so that every device receives 8. At each receiving device the RVEs are placed in order of rising iteration count.
All inputs are finite; a program needn't handle non-finite values.
Results may differ from the reference program's by a relative error of at most 0.0003.
Values sent between devices are 32-bit elements; how exact they have to be, the bound alone decides.
A program may use at most 128 MiB of HBM per device.

```python
import math
import jax
import jax.numpy as jnp
from jax import lax

G = 16
ITER_PEAK = 3
RBLK = 4
NZ = 8
R_LOC = 8
NX = 32
NY = 8
NE = 2048
PEERS = 4
CAP = 2
N_RVE = 32
N_MIC = 4
N_MAC = 2


def plan_parts(key):
    folded = jax.random.fold_in(key, 4242)
    subkeys = jax.random.split(folded, 7)
    columns = N_MIC * N_MAC
    groups_total = N_RVE * columns
    loaded = jax.random.randint(subkeys[0], (N_RVE, columns), 0, 4) == 0
    forced = jax.random.randint(subkeys[1], (), 0, groups_total)
    loaded = loaded | (jnp.arange(groups_total).reshape(N_RVE, columns) == forced)
    upper_draw = jax.random.randint(subkeys[2], (N_RVE, columns, R_LOC), 1, ITER_PEAK + 1)
    lower_draw = jax.random.randint(subkeys[3], (N_RVE, columns, R_LOC), 0, 2)
    iterations = jnp.where(loaded[:, :, None], upper_draw, lower_draw)
    first_slot = (jnp.arange(R_LOC) == 0)[None, None, :]
    iterations = jnp.where(loaded[:, :, None] & first_slot, ITER_PEAK, iterations)
    offset_index = jnp.arange(N_RVE)
    offset_score = jax.random.randint(subkeys[4], (N_RVE,), 0, 2 ** 16) * N_RVE + offset_index
    required = (offset_index == 1) | (offset_index == N_RVE // 2)
    offset_score = jnp.where(required, offset_index - 2 * N_RVE, offset_score)
    offsets = jnp.argsort(offset_score)[:PEERS].astype(jnp.int32)
    shuffle = jax.random.randint(subkeys[5], (N_RVE, columns, R_LOC), 0, 2 ** 16) * R_LOC + jnp.arange(R_LOC)[None, None, :]
    position = jnp.argsort(jnp.argsort(shuffle, axis=-1), axis=-1)
    bundle = position // CAP
    target = (jnp.arange(N_RVE)[:, None, None] + offsets[bundle]) % N_RVE
    flat_index = jnp.arange(N_RVE)[:, None, None] * R_LOC + jnp.arange(R_LOC)[None, None, :]
    tiebreak = jax.random.randint(subkeys[6], (N_RVE, columns, R_LOC), 0, 2 ** 12) * (N_RVE * R_LOC) + flat_index
    ordering = iterations * (2 ** 12 * N_RVE * R_LOC) + tiebreak
    target_cols = jnp.transpose(target, (1, 0, 2)).reshape(columns, N_RVE * R_LOC)
    ordering_cols = jnp.transpose(ordering, (1, 0, 2)).reshape(columns, N_RVE * R_LOC)
    shared = target_cols[:, :, None] == target_cols[:, None, :]
    smaller = ordering_cols[:, None, :] < ordering_cols[:, :, None]
    arrival = jnp.sum((shared & smaller).astype(jnp.int32), axis=2)
    arrival = jnp.transpose(arrival.reshape(columns, N_RVE, R_LOC), (1, 0, 2))
    destination = (target * columns + jnp.arange(columns)[None, :, None]) * R_LOC + arrival
    return (iterations.reshape(-1).astype(jnp.int32), destination.reshape(-1).astype(jnp.int32))


def draw_counts(key, part):
    return plan_parts(key)[0]


def draw_migration_plan(key, part):
    return plan_parts(key)[1]


def block_levels(own_key, shape, shards, low, high):
    def one(axis_at, blocks):
        heights = jax.random.uniform(jax.random.fold_in(jax.random.fold_in(own_key, 6), axis_at), (blocks,), jnp.float32, low / len(shards), high / len(shards))
        return jnp.repeat(jnp.exp(heights), shape[axis_at] // blocks).reshape((-1,) + (1,) * (len(shape) - axis_at - 1))

    level = one(*shards[0])
    for cut in shards[1:]:
        level = level * one(*cut)
    return level


def normal_values(stream_key, shape, scale, bound, cuts=(), kind=jnp.bfloat16):
    factor_of = block_levels(stream_key, shape, cuts, -0.22, 0.18) if cuts else 1.0
    drawn = jax.random.normal(stream_key, shape, jnp.float32) * scale * factor_of
    return jnp.minimum(jnp.maximum(drawn, -bound), bound).astype(kind)


def setup_inputs(seed: int = 0) -> dict:
    key_list = jax.random.split(jax.random.key(seed), 8)
    return {
        "displacement": normal_values(key_list[0], (3, NX, NY, NZ), 0.5, 3.0, ((1, 32), (2, 8)), jnp.float32),
        "plastic": normal_values(key_list[1], (NE, 6, G, G * G), 0.05, 0.3, ((0, 256),), jnp.float32),
        "bulk_modulus": jnp.clip(jax.random.uniform(key_list[2], (G, G * G), jnp.float32, 1.0, 3.0), 1.0, 3.0),
        "shear_modulus": jnp.clip(jax.random.uniform(key_list[3], (G, G * G), jnp.float32, 0.5, 1.5), 0.5, 1.5),
        "yield_radius": jnp.clip(jnp.exp(jax.random.uniform(key_list[4], (G, G * G), jnp.float32, math.log(0.05), math.log(0.3))), 0.05, 0.3),
        "counts": draw_counts(jax.random.fold_in(key_list[7], 71), 0),
        "migration_plan": draw_migration_plan(jax.random.fold_in(key_list[7], 71), 0),
    }


REF_COUPLING = 0.7

def material_response(strain, plastic, bulk_modulus, shear_modulus, yield_radius):
    elastic = strain - plastic
    volumetric = elastic[..., 0, :, :, :] + elastic[..., 1, :, :, :] + elastic[..., 2, :, :, :]
    mean_normal = volumetric / 3.0
    deviator = jnp.stack([elastic[..., 0, :, :, :] - mean_normal, elastic[..., 1, :, :, :] - mean_normal, elastic[..., 2, :, :, :] - mean_normal, elastic[..., 3, :, :, :], elastic[..., 4, :, :, :], elastic[..., 5, :, :, :]], axis=-4)
    trial_deviator = 2.0 * shear_modulus * deviator
    weights = jnp.array([1.0, 1.0, 1.0, 2.0, 2.0, 2.0], jnp.float32).reshape(6, 1, 1, 1)
    squared = lax.optimization_barrier(jnp.sum(weights * trial_deviator * trial_deviator, axis=-4))
    factor = yield_radius / jnp.sqrt(jnp.maximum(squared, yield_radius * yield_radius))
    relaxed = factor[..., None, :, :, :] * trial_deviator
    normal_mask = jnp.array([1.0, 1.0, 1.0, 0.0, 0.0, 0.0], jnp.float32).reshape(6, 1, 1, 1)
    stress = relaxed + normal_mask * (bulk_modulus * volumetric)[..., None, :, :, :]
    increment = (trial_deviator - relaxed) / (2.0 * shear_modulus)
    return (stress, increment)

def green_apply(real_part, imag_part):
    extent = real_part.shape[-1]
    wavenumber = ((jnp.arange(extent) + extent // 2) % extent - extent // 2).astype(jnp.float32)
    freq_a = wavenumber[:, None, None]
    freq_b = wavenumber[None, :, None]
    freq_c = wavenumber[None, None, :]
    magnitude = freq_a * freq_a + freq_b * freq_b + freq_c * freq_c
    nonzero = magnitude > 0.0
    guarded = jnp.maximum(magnitude, 1.0)
    linear_term = jnp.where(nonzero, 1.0 / (2.0 * guarded), 0.0)
    cubic_term = jnp.where(nonzero, REF_COUPLING / (guarded * guarded), 0.0)

    def single(tau):
        tau_aa, tau_bb, tau_cc = (tau[:, 0], tau[:, 1], tau[:, 2])
        tau_bc, tau_ac, tau_ab = (tau[:, 3], tau[:, 4], tau[:, 5])
        traction_a = tau_aa * freq_a + tau_ab * freq_b + tau_ac * freq_c
        traction_b = tau_ab * freq_a + tau_bb * freq_b + tau_bc * freq_c
        traction_c = tau_ac * freq_a + tau_bc * freq_b + tau_cc * freq_c
        normal_part = freq_a * traction_a + freq_b * traction_b + freq_c * traction_c
        result_list = [linear_term * 2.0 * freq_a * traction_a - cubic_term * freq_a * freq_a * normal_part, linear_term * 2.0 * freq_b * traction_b - cubic_term * freq_b * freq_b * normal_part, linear_term * 2.0 * freq_c * traction_c - cubic_term * freq_c * freq_c * normal_part, linear_term * (freq_b * traction_c + freq_c * traction_b) - cubic_term * freq_b * freq_c * normal_part, linear_term * (freq_a * traction_c + freq_c * traction_a) - cubic_term * freq_a * freq_c * normal_part, linear_term * (freq_a * traction_b + freq_b * traction_a) - cubic_term * freq_a * freq_b * normal_part]
        return jnp.stack(result_list, axis=1)
    return (single(real_part), single(imag_part))

def polarization_update(stress):
    spectrum = jnp.fft.fftn(stress, axes=(-3, -2, -1))
    real_part, imag_part = green_apply(jnp.real(spectrum), jnp.imag(spectrum))
    return jnp.real(jnp.fft.ifftn(lax.complex(real_part, imag_part), axes=(-3, -2, -1)))

def element_strain(displacement):
    padded = jnp.pad(displacement, ((0, 0), (0, 1), (0, 1), (0, 1)))
    gradient = [[0.0, 0.0, 0.0], [0.0, 0.0, 0.0], [0.0, 0.0, 0.0]]
    for shift_a in (0, 1):
        for shift_b in (0, 1):
            for shift_c in (0, 1):
                corner_values = padded[:, shift_a:shift_a + NX, shift_b:shift_b + NY, shift_c:shift_c + NZ]
                signs = ((2 * shift_a - 1) / 4.0, (2 * shift_b - 1) / 4.0, (2 * shift_c - 1) / 4.0)
                for component in range(3):
                    for direction in range(3):
                        gradient[component][direction] = gradient[component][direction] + corner_values[component] * signs[direction]
    return jnp.stack([gradient[0][0], gradient[1][1], gradient[2][2], 0.5 * (gradient[1][2] + gradient[2][1]), 0.5 * (gradient[0][2] + gradient[2][0]), 0.5 * (gradient[0][1] + gradient[1][0])], axis=0)

def nodal_forces(stress_field):
    padded = jnp.pad(stress_field, ((0, 0), (1, 0), (1, 0), (1, 0)))
    pairs = [[0, 5, 4], [5, 1, 3], [4, 3, 2]]
    forces = [0.0, 0.0, 0.0]
    for shift_a in (0, 1):
        for shift_b in (0, 1):
            for shift_c in (0, 1):
                corner_values = padded[:, 1 - shift_a:1 - shift_a + NX, 1 - shift_b:1 - shift_b + NY, 1 - shift_c:1 - shift_c + NZ]
                signs = ((2 * shift_a - 1) / 4.0, (2 * shift_b - 1) / 4.0, (2 * shift_c - 1) / 4.0)
                for component in range(3):
                    for direction in range(3):
                        forces[component] = forces[component] + corner_values[pairs[component][direction]] * signs[direction]
    return jnp.stack(forces, axis=0)

def reference(displacement, plastic, bulk_modulus, shear_modulus, yield_radius, counts, migration_plan):
    strain_field = element_strain(displacement)
    strain_rows = strain_field.reshape(6, NE).T
    bulk_grid = bulk_modulus.reshape(G, G, G)
    shear_grid = shear_modulus.reshape(G, G, G)
    radius_grid = yield_radius.reshape(G, G, G)
    plastic_blocks = plastic.reshape(NE // RBLK, RBLK, 6, G, G, G)
    strain_blocks = strain_rows.reshape(NE // RBLK, RBLK, 6)
    count_blocks = counts.reshape(NE // RBLK, RBLK)

    def solve_block(inputs):
        plastic_block, strain_block, count_block = inputs
        strain = jnp.broadcast_to(strain_block[:, :, None, None, None], plastic_block.shape)
        previous_map = strain
        previous_update = jnp.zeros_like(strain)
        for step_index in range(ITER_PEAK):
            stress, unused = material_response(strain, plastic_block, bulk_grid, shear_grid, radius_grid)
            update = polarization_update(stress)
            mapped = strain - update
            change = update - previous_update
            numerator = lax.optimization_barrier(jnp.mean(change * update, axis=(1, 2, 3, 4)))
            denominator = lax.optimization_barrier(jnp.mean(change * change, axis=(1, 2, 3, 4))) + 1e-06
            weight = numerator / denominator if step_index > 0 else jnp.zeros_like(numerator)
            candidate = mapped - weight[:, None, None, None, None] * (mapped - previous_map)
            active = step_index < count_block
            strain = jnp.where(active[:, None, None, None, None], candidate, strain)
            previous_map = mapped
            previous_update = update
        stress, increment = material_response(strain, plastic_block, bulk_grid, shear_grid, radius_grid)
        return (lax.optimization_barrier(jnp.mean(stress, axis=(2, 3, 4))), plastic_block + increment)
    averages, updated = lax.map(solve_block, (plastic_blocks, strain_blocks, count_blocks))
    stress_field = averages.reshape(NE, 6).T.reshape(6, NX, NY, NZ)
    force = nodal_forces(stress_field)
    updated = updated.reshape(NE, 6, G, G * G)
    moved = jnp.zeros_like(updated).at[migration_plan].set(updated)
    return (force, moved)
```

```python
import math

import jax
import jax.numpy as jnp
import numpy as np
from jax import lax
from jax.experimental import pallas as pl
from jax.experimental.pallas import tpu as pltpu
from jax.sharding import Mesh
from jax.sharding import PartitionSpec as P

RVE = ("rve_0", "rve_1")
RVE_MIC_MAC = ("rve_0", "rve_1", "mic", "mac")


COUPLING = 0.7
PAIRS = ((0, 0), (1, 1), (2, 2), (1, 2), (0, 2), (0, 1))


def transform_tables(n):
    plane = np.arange(n * n)
    b, c = plane // n, plane % n
    angle = 2.0 * np.pi / n * ((np.outer(b, b) + np.outer(c, c)) % n)
    table = np.concatenate([np.cos(angle), np.sin(angle)], axis=1).astype(np.float32)
    high = table.astype(jnp.bfloat16)
    low = (table - high.astype(np.float32)).astype(jnp.bfloat16)
    return np.concatenate([high, high, low], axis=0)


def green_table(n):
    index = np.stack(np.meshgrid(np.arange(n), np.arange(n), np.arange(n), indexing="ij"))

    def operator(i):
        k = ((i + n // 2) % n - n // 2).astype(np.float64)
        q = np.sum(k * k, axis=0)
        safe = np.maximum(q, 1.0)
        rows = []
        for m, r in PAIRS:
            row = []
            for p, s in PAIRS:
                eye = lambda u, v: 1.0 if u == v else 0.0
                first = (
                    eye(m, p) * k[r] * k[s] + eye(m, s) * k[r] * k[p] + eye(r, p) * k[m] * k[s] + eye(r, s) * k[m] * k[p]
                ) / (4.0 * safe)
                row.append(first - COUPLING * k[m] * k[r] * k[p] * k[s] / (safe * safe))
            rows.append(row)
        return np.where(q > 0, np.array(rows), 0.0)

    even = 0.5 * (operator(index) + operator((-index) % n)) / float(n**3)
    even = even[:, :, : n // 2 + 1]
    rows = [even[i, j].reshape(n // 2 + 1, n * n) for i in range(6) for j in range(i, 6)]
    table = np.stack(rows, axis=1).reshape(-1, n * n).astype(np.float32)
    return np.pad(table, ((0, -table.shape[0] % 8), (0, 0)))


def turn(k, n, value, sign):
    re, im = value
    if k == 0:
        return value
    if 4 * k == n:
        return (im, -re) if sign < 0 else (-im, re)
    if 8 * k == n:
        r = math.sqrt(0.5)
        return ((re + im) * r, (im - re) * r) if sign < 0 else ((re - im) * r, (re + im) * r)
    c, s = math.cos(2 * math.pi * k / n), sign * math.sin(2 * math.pi * k / n)
    return (re * c - im * s, re * s + im * c)


def real_forward(x):
    n = len(x)
    if n == 2:
        return [(x[0] + x[1], None), (x[0] - x[1], None)]
    even, odd = real_forward(x[0::2]), real_forward(x[1::2])
    out = [None] * (n // 2 + 1)
    out[0] = (even[0][0] + odd[0][0], None)
    out[n // 2] = (even[0][0] - odd[0][0], None)
    for k in range(1, n // 4 + 1):
        if 4 * k == n:
            out[k] = (even[k][0], -odd[k][0])
        else:
            t = turn(k, n, odd[k], -1)
            out[k] = (even[k][0] + t[0], even[k][1] + t[1])
            out[n // 2 - k] = (even[k][0] - t[0], t[1] - even[k][1])
    return out


def real_backward(y):
    n = 2 * (len(y) - 1)
    if n == 2:
        return [y[0][0] + y[1][0], y[0][0] - y[1][0]]
    even, odd = [None] * (n // 4 + 1), [None] * (n // 4 + 1)
    even[0] = (y[0][0] + y[n // 2][0], None)
    odd[0] = (y[0][0] - y[n // 2][0], None)
    for k in range(1, n // 4 + 1):
        if 4 * k == n:
            even[k] = (2.0 * y[k][0], None)
            odd[k] = (-2.0 * y[k][1], None)
        else:
            o = y[n // 2 - k]
            even[k] = (y[k][0] + o[0], y[k][1] - o[1])
            odd[k] = turn(k, n, (y[k][0] - o[0], y[k][1] + o[1]), 1)
    out = [None] * n
    out[0::2] = real_backward(even)
    out[1::2] = real_backward(odd)
    return out


def flow_rule(elastic, shear2, radius):
    volume = elastic[0] + elastic[1] + elastic[2]
    mean = volume * (1.0 / 3.0)
    deviator = [elastic[i] - mean for i in range(3)] + list(elastic[3:])
    trial = [shear2 * d for d in deviator]
    normal = trial[0] * trial[0] + trial[1] * trial[1] + trial[2] * trial[2]
    mixed = trial[3] * trial[3] + trial[4] * trial[4] + trial[5] * trial[5]
    squared = normal + (mixed + mixed)
    factor = radius * lax.rsqrt(jnp.maximum(squared, radius * radius))
    return volume, deviator, trial, factor


HALVES = (slice(0, 128), slice(128, 256))


def solve_kernel(
    plastic_ref, macro_ref, counts_ref, bulk_ref, shear_ref, radius_ref, dft_ref, green_ref,
    next_ref, mean_ref,
    halves_s, copy_sem, material_s, green_s, plastic_s, strain_s, stress_s, update_s, mapped_s, left_s, product_s, left2_s, product2_s,
):
    f32, bf16 = jnp.float32, jnp.bfloat16
    counts = counts_ref[...]
    incoming = [
        pltpu.make_async_copy(plastic_ref.at[:, lanes], halves_s.at[h], copy_sem.at[h]) for h, lanes in enumerate(HALVES)
    ]
    for copy in incoming:
        copy.start()
    for a in range(16):
        shear2 = 2.0 * shear_ref[a : a + 1, :]
        for i, row in enumerate((shear2, bulk_ref[a : a + 1, :], radius_ref[a : a + 1, :])):
            material_s[a, i] = jnp.broadcast_to(row, (8, 256))

    @pl.loop(0, 24)
    def _(block):
        rows = green_ref[pl.ds(pl.multiple_of(block * 8, 8), 8), :]
        for r in range(8):
            green_s[block * 8 + r] = jnp.broadcast_to(rows[r : r + 1, :], (8, 256))

    for copy in incoming:
        copy.wait()

    @pl.loop(0, 96, unroll=4)
    def _(row):
        for h, lanes in enumerate(HALVES):
            plastic_s[row, :, lanes] = halves_s[h, pl.ds(row, 8, stride=96), :]

    for c in range(6):
        start = jnp.broadcast_to(macro_ref[:, c : c + 1], (8, 256))

        @pl.loop(0, 16)
        def _(a):
            strain_s[c * 16 + a] = start

    def split(value):
        high = value.astype(bf16)
        low = (value - high.astype(f32)).astype(bf16)
        return high, low

    def polarization():
        @pl.loop(0, 16)
        def _(a):
            for lanes in HALVES:
                shear2 = material_s[a, 0, :, lanes]
                bulk = material_s[a, 1, :, lanes]
                radius = material_s[a, 2, :, lanes]
                elastic = [strain_s[c * 16 + a, :, lanes] - plastic_s[c * 16 + a, :, lanes] for c in range(6)]
                volume, _, trial, factor = flow_rule(elastic, shear2, radius)
                pressure = bulk * volume
                for c in range(6):
                    value = factor * trial[c]
                    stress_s[c * 16 + a, :, lanes] = value + pressure if c < 3 else value

        @pl.loop(0, 3)
        def _(pair):
            for lanes in HALVES:
                sets = []
                for half in range(2):
                    y = real_forward([stress_s[pair * 32 + half * 16 + a, :, lanes] for a in range(16)])
                    sets.append([y[0][0], y[8][0]] + [part for k in range(1, 8) for part in y[k]])
                rows = pl.ds(pl.multiple_of(pair * 16, 16), 16)
                for r in range(16):
                    high, low = split(jnp.concatenate([sets[0][r], sets[1][r]], axis=0))
                    left_s[r, rows, lanes] = high
                    left_s[r, rows, slice(256 + lanes.start, 256 + lanes.stop)] = low

        left = left_s[...].reshape(768, 512)
        product_s[...] = jnp.dot(
            jnp.concatenate([left, left[:, :256]], axis=1), dft_ref[...], preferred_element_type=f32
        ).reshape(16, 48, 512)

        def operate(k, re, im, lanes):
            for t, value in ((2 * k, re), (2 * k + 1, im)):
                value = value[:3] + [v + v for v in value[3:]]
                out = [None] * 6
                j = 0
                for i in range(6):
                    for m in range(i, 6):
                        g = green_s[k * 21 + j, :, lanes]
                        j += 1
                        out[i] = g * value[m] if out[i] is None else out[i] + g * value[m]
                        if m != i:
                            out[m] = g * value[i] if out[m] is None else out[m] + g * value[i]
                for pair in range(3):
                    high, low = split(jnp.concatenate([out[2 * pair], out[2 * pair + 1]], axis=0))
                    left2_s[t, slice(pair * 16, pair * 16 + 16), lanes] = high
                    left2_s[t, slice(pair * 16, pair * 16 + 16), slice(256 + lanes.start, 256 + lanes.stop)] = low

        for k, row in ((0, 0), (8, 1)):
            for lanes in HALVES:
                wide = slice(256 + lanes.start, 256 + lanes.stop)
                re = [product_s[row, slice(c * 8, c * 8 + 8), lanes] for c in range(6)]
                im = [-product_s[row, slice(c * 8, c * 8 + 8), wide] for c in range(6)]
                operate(k, re, im, lanes)

        @pl.loop(1, 8)
        def _(k):
            for lanes in HALVES:
                wide = slice(256 + lanes.start, 256 + lanes.stop)
                re, im = [], []
                for c in range(6):
                    rows = slice(c * 8, c * 8 + 8)
                    re.append(product_s[2 * k, rows, lanes] + product_s[2 * k + 1, rows, wide])
                    im.append(product_s[2 * k + 1, rows, lanes] - product_s[2 * k, rows, wide])
                operate(k, re, im, lanes)

        left2 = left2_s[...].reshape(864, 512)
        product2_s[...] = jnp.dot(
            jnp.concatenate([left2, left2[:, :256]], axis=1), dft_ref[...], preferred_element_type=f32
        ).reshape(18, 48, 512)

    def update_of(c, lanes):
        wide = slice(256 + lanes.start, 256 + lanes.stop)
        rows = pl.ds(pl.multiple_of(c * 8, 8), 8)
        y = []
        for k in range(9):
            re = product2_s[2 * k, rows, lanes] - product2_s[2 * k + 1, rows, wide]
            im = None if k in (0, 8) else product2_s[2 * k, rows, wide] + product2_s[2 * k + 1, rows, lanes]
            y.append((re, im))
        return real_backward(y)

    polarization()
    active = counts > 0

    @pl.loop(0, 6)
    def _(c):
        for lanes in HALVES:
            update = update_of(c, lanes)
            for a in range(16):
                strain = strain_s[c * 16 + a, :, lanes]
                strain_s[c * 16 + a, :, lanes] = jnp.where(active, strain - update[a], strain)
                update_s[c * 16 + a, :, lanes] = update[a]
                mapped_s[c * 16 + a, :, lanes] = strain - update[a]

    @pl.loop(1, 3)
    def _(step):
        polarization()
        zero = jnp.zeros((8, 128), f32)

        def gather(c, carry):
            numerator, denominator = carry
            for lanes in HALVES:
                update = update_of(c, lanes)
                for a in range(16):
                    change = update[a] - update_s[c * 16 + a, :, lanes]
                    numerator = numerator + change * update[a]
                    denominator = denominator + change * change
                    update_s[c * 16 + a, :, lanes] = update[a]
            return numerator, denominator

        numerator, denominator = lax.fori_loop(0, 6, gather, (zero, zero))
        scale = 1.0 / float(6 * 16**3)
        numerator = jnp.sum(numerator, axis=1, keepdims=True) * scale
        denominator = jnp.sum(denominator, axis=1, keepdims=True) * scale + 1e-06
        weight = jnp.broadcast_to(numerator / denominator, (8, 256))
        active = jnp.broadcast_to(step < counts, (8, 256))

        @pl.loop(0, 96, unroll=4)
        def _(row):
            strain = strain_s[row]
            mapped = strain - update_s[row]
            candidate = mapped - weight * (mapped - mapped_s[row])
            mapped_s[row] = mapped
            strain_s[row] = jnp.where(active, candidate, strain)

    def finish(a, sums):
        sums = list(sums)
        for lanes in HALVES:
            shear2 = material_s[a, 0, :, lanes]
            bulk = material_s[a, 1, :, lanes]
            radius = material_s[a, 2, :, lanes]
            plastic = [plastic_s[c * 16 + a, :, lanes] for c in range(6)]
            elastic = [strain_s[c * 16 + a, :, lanes] - plastic[c] for c in range(6)]
            volume, deviator, trial, factor = flow_rule(elastic, shear2, radius)
            pressure = bulk * volume
            for c in range(6):
                value = factor * trial[c]
                sums[c] = sums[c] + (value + pressure if c < 3 else value)
                plastic_s[c * 16 + a, :, lanes] = plastic[c] + (deviator[c] - factor * deviator[c])
        return tuple(sums)

    zero = jnp.zeros((8, 128), f32)
    sums = lax.fori_loop(0, 16, finish, (zero,) * 6)
    lane = lax.broadcasted_iota(jnp.int32, (8, 128), 1)
    means = zero
    for c in range(6):
        means = jnp.where(lane == c, jnp.sum(sums[c], axis=1, keepdims=True) * (1.0 / 4096.0), means)
    mean_ref[...] = means

    @pl.loop(0, 96, unroll=4)
    def _(row):
        for h, lanes in enumerate(HALVES):
            halves_s[h, pl.ds(row, 8, stride=96), :] = plastic_s[row, :, lanes]

    outgoing = [
        pltpu.make_async_copy(halves_s.at[h], next_ref.at[:, lanes], copy_sem.at[h]) for h, lanes in enumerate(HALVES)
    ]
    for copy in outgoing:
        copy.start()
    for copy in outgoing:
        copy.wait()


def solve(plastic, macro, counts, bulk, shear, radius):
    f32, bf16 = jnp.float32, jnp.bfloat16
    vm = pl.BlockSpec(memory_space=pltpu.VMEM)
    updated, means = pl.pallas_call(
        solve_kernel,
        out_shape=(jax.ShapeDtypeStruct((768, 256), f32), jax.ShapeDtypeStruct((8, 128), f32)),
        in_specs=[pl.BlockSpec(memory_space=pl.ANY)] + [vm] * 7,
        out_specs=(pl.BlockSpec(memory_space=pl.ANY), vm),
        scratch_shapes=[
            pltpu.VMEM((2, 768, 128), f32),
            pltpu.SemaphoreType.DMA((2,)),
            pltpu.VMEM((16, 3, 8, 256), f32),
            pltpu.VMEM((192, 8, 256), f32),
            pltpu.VMEM((96, 8, 256), f32),
            pltpu.VMEM((96, 8, 256), f32),
            pltpu.VMEM((96, 8, 256), f32),
            pltpu.VMEM((96, 8, 256), f32),
            pltpu.VMEM((96, 8, 256), f32),
            pltpu.VMEM((16, 48, 512), bf16),
            pltpu.VMEM((16, 48, 512), f32),
            pltpu.VMEM((18, 48, 512), bf16),
            pltpu.VMEM((18, 48, 512), f32),
        ],
        compiler_params=pltpu.CompilerParams(vmem_limit_bytes=48 << 20),
        name="solve",
    )(
        plastic.reshape(768, 256),
        macro,
        counts[:, None],
        bulk,
        shear,
        radius,
        jnp.asarray(transform_tables(16)),
        jnp.asarray(green_table(16)),
    )
    return updated, means


def shifted(value, axis, steps):
    count = lax.axis_size(axis)
    first, last = (max(0, -steps), min(count, count - steps))
    return lax.ppermute(value, axis, [(source, source + steps) for source in range(first, last)])


def element_strain(displacement):
    rows_y = displacement.shape[2]
    depth = displacement.shape[3]
    upper_layer = shifted(displacement, RVE, -1)
    extended = jnp.concatenate([displacement, upper_layer], axis=1)
    upper_row = shifted(extended, ("mic", "mac"), -1)
    extended = jnp.concatenate([extended, upper_row], axis=2)
    extended = jnp.pad(extended, ((0, 0), (0, 0), (0, 0), (0, 1)))
    gradient = [[0.0, 0.0, 0.0], [0.0, 0.0, 0.0], [0.0, 0.0, 0.0]]
    for shift_a in (0, 1):
        for shift_b in (0, 1):
            for shift_c in (0, 1):
                corner_values = extended[
                    :, shift_a : shift_a + 1, shift_b : shift_b + rows_y, shift_c : shift_c + depth
                ]
                signs = ((2 * shift_a - 1) / 4.0, (2 * shift_b - 1) / 4.0, (2 * shift_c - 1) / 4.0)
                for component in range(3):
                    for direction in range(3):
                        gradient[component][direction] = (
                            gradient[component][direction]
                            + corner_values[component] * signs[direction]
                        )
    strain_field = jnp.stack(
        [
            gradient[0][0],
            gradient[1][1],
            gradient[2][2],
            0.5 * (gradient[1][2] + gradient[2][1]),
            0.5 * (gradient[0][2] + gradient[2][0]),
            0.5 * (gradient[0][1] + gradient[1][0]),
        ],
        axis=0,
    )
    return strain_field.reshape(6, rows_y * depth).T


def nodal_forces(averages, rows_y, depth):
    macro_stress = averages.T.reshape(6, 1, rows_y, depth)
    lower_layer = shifted(macro_stress, RVE, 1)
    extended = jnp.concatenate([lower_layer, macro_stress], axis=1)
    lower_row = shifted(extended, ("mic", "mac"), 1)
    extended = jnp.concatenate([lower_row, extended], axis=2)
    extended = jnp.pad(extended, ((0, 0), (0, 0), (0, 0), (1, 0)))
    pairs = [[0, 5, 4], [5, 1, 3], [4, 3, 2]]
    forces = [0.0, 0.0, 0.0]
    for shift_a in (0, 1):
        for shift_b in (0, 1):
            for shift_c in (0, 1):
                corner_values = extended[
                    :,
                    1 - shift_a : 2 - shift_a,
                    1 - shift_b : 1 - shift_b + rows_y,
                    1 - shift_c : 1 - shift_c + depth,
                ]
                signs = ((2 * shift_a - 1) / 4.0, (2 * shift_b - 1) / 4.0, (2 * shift_c - 1) / 4.0)
                for component in range(3):
                    for direction in range(3):
                        forces[component] = (
                            forces[component]
                            + corner_values[pairs[component][direction]] * signs[direction]
                        )
    return jnp.stack(forces, axis=0)


def route_slots(migration_plan, width_rows, capacity):
    columns = lax.axis_size("mic") * lax.axis_size("mac")
    target = migration_plan // width_rows
    partner = target // columns
    target_row = migration_plan % width_rows
    shared = partner[:, None] == partner[None, :]
    positions = jnp.arange(width_rows)
    earlier = positions[:, None] > positions[None, :]
    order_within = jnp.sum((shared & earlier).astype(jnp.int32), axis=1)
    return (partner * capacity + order_within, target_row)


def pack_rows(payload, slot_index, total_slots):
    matches = slot_index[None, :] == jnp.arange(total_slots)[:, None]
    source = jnp.sum(jnp.where(matches, jnp.arange(payload.shape[0])[None, :], 0), axis=1)
    filled = jnp.any(matches, axis=1)
    picked = jnp.take(payload, source, axis=0)
    return jnp.where(
        filled.reshape((-1,) + (1,) * (payload.ndim - 1)), picked, jnp.zeros_like(picked)
    )


def unpack_rows(received, labels, width_rows):
    wanted = labels.astype(jnp.int32) - 1
    matches = wanted[None, :] == jnp.arange(width_rows)[:, None]
    source = jnp.sum(jnp.where(matches, jnp.arange(received.shape[0])[None, :], 0), axis=1)
    return jnp.take(received, source, axis=0)


def on_device(
    displacement, plastic, bulk_modulus, shear_modulus, yield_radius, counts, migration_plan
):
    width_rows, depth = plastic.shape[0], displacement.shape[3]
    strain_rows = element_strain(displacement)
    updated, means = solve(
        plastic, strain_rows, counts, bulk_modulus, shear_modulus, yield_radius
    )
    devices_along = lax.axis_size(RVE)
    capacity = 2
    total_slots = devices_along * capacity
    slot_index, target_row = route_slots(migration_plan, width_rows, capacity)
    labels = (target_row + 1)[:, None]
    outgoing = pack_rows(updated.reshape(plastic.shape), slot_index, total_slots)
    outgoing_labels = pack_rows(labels, slot_index, total_slots)
    arrived = lax.all_to_all(outgoing, RVE, split_axis=0, concat_axis=0, tiled=True)
    arrived_labels = lax.all_to_all(
        outgoing_labels, RVE, split_axis=0, concat_axis=0, tiled=True
    )
    plastic_new = unpack_rows(arrived, arrived_labels[:, 0], width_rows)
    force = nodal_forces(means[:, :6], displacement.shape[2], depth)
    return (force, plastic_new)


def solution(mesh):
    finer = Mesh(
        mesh.devices.reshape(8, 4, mesh.shape["mic"], mesh.shape["mac"]),
        ("rve_0", "rve_1", "mic", "mac"),
    )
    placed = (
        P(None, RVE, ("mic", "mac"), None),
        P(RVE_MIC_MAC, None, None, None),
        P(),
        P(),
        P(),
        P(RVE_MIC_MAC),
        P(RVE_MIC_MAC),
    )
    return jax.shard_map(
        on_device,
        mesh=finer,
        in_specs=placed,
        out_specs=(P(None, RVE, ("mic", "mac"), None), P(RVE_MIC_MAC, None, None, None)),
        check_vma=False,
    )
```

```python
import functools
import math

import jax
import jax.numpy as jnp
import numpy as np
from jax import lax
from jax.experimental import pallas as pl
from jax.experimental.pallas import tpu as pltpu
from jax.sharding import Mesh
from jax.sharding import PartitionSpec as P

RVE = ("rve_0", "rve_1")
RVE_MIC_MAC = ("rve_0", "rve_1", "mic", "mac")


COUPLING = 0.7
PAIRS = ((0, 0), (1, 1), (2, 2), (1, 2), (0, 2), (0, 1))


def transform_tables(n):
    plane = np.arange(n * n)
    b, c = plane // n, plane % n
    angle = 2.0 * np.pi / n * ((np.outer(b, b) + np.outer(c, c)) % n)
    table = np.concatenate([np.cos(angle), np.sin(angle)], axis=1).astype(np.float32)
    high = table.astype(jnp.bfloat16)
    low = (table - high.astype(np.float32)).astype(jnp.bfloat16)
    return np.concatenate([high, high, low], axis=0)


def green_table(n):
    index = np.stack(np.meshgrid(np.arange(n), np.arange(n), np.arange(n), indexing="ij"))

    def operator(i):
        k = ((i + n // 2) % n - n // 2).astype(np.float64)
        q = np.sum(k * k, axis=0)
        safe = np.maximum(q, 1.0)
        rows = []
        for m, r in PAIRS:
            row = []
            for p, s in PAIRS:
                eye = lambda u, v: 1.0 if u == v else 0.0
                first = (
                    eye(m, p) * k[r] * k[s] + eye(m, s) * k[r] * k[p] + eye(r, p) * k[m] * k[s] + eye(r, s) * k[m] * k[p]
                ) / (4.0 * safe)
                row.append(first - COUPLING * k[m] * k[r] * k[p] * k[s] / (safe * safe))
            rows.append(row)
        return np.where(q > 0, np.array(rows), 0.0)

    even = 0.5 * (operator(index) + operator((-index) % n)) / float(n**3)
    even = even[:, :, : n // 2 + 1]
    rows = [even[i, j].reshape(n // 2 + 1, n * n) for i in range(6) for j in range(i, 6)]
    table = np.stack(rows, axis=1).reshape(-1, n * n).astype(np.float32)
    return np.pad(table, ((0, -table.shape[0] % 8), (0, 0)))


def turn(k, n, value, sign):
    re, im = value
    if k == 0:
        return value
    if 4 * k == n:
        return (im, -re) if sign < 0 else (-im, re)
    if 8 * k == n:
        r = math.sqrt(0.5)
        return ((re + im) * r, (im - re) * r) if sign < 0 else ((re - im) * r, (re + im) * r)
    c, s = math.cos(2 * math.pi * k / n), sign * math.sin(2 * math.pi * k / n)
    return (re * c - im * s, re * s + im * c)


def real_forward(x):
    n = len(x)
    if n == 2:
        return [(x[0] + x[1], None), (x[0] - x[1], None)]
    even, odd = real_forward(x[0::2]), real_forward(x[1::2])
    out = [None] * (n // 2 + 1)
    out[0] = (even[0][0] + odd[0][0], None)
    out[n // 2] = (even[0][0] - odd[0][0], None)
    for k in range(1, n // 4 + 1):
        if 4 * k == n:
            out[k] = (even[k][0], -odd[k][0])
        else:
            t = turn(k, n, odd[k], -1)
            out[k] = (even[k][0] + t[0], even[k][1] + t[1])
            out[n // 2 - k] = (even[k][0] - t[0], t[1] - even[k][1])
    return out


def real_backward(y):
    n = 2 * (len(y) - 1)
    if n == 2:
        return [y[0][0] + y[1][0], y[0][0] - y[1][0]]
    even, odd = [None] * (n // 4 + 1), [None] * (n // 4 + 1)
    even[0] = (y[0][0] + y[n // 2][0], None)
    odd[0] = (y[0][0] - y[n // 2][0], None)
    for k in range(1, n // 4 + 1):
        if 4 * k == n:
            even[k] = (2.0 * y[k][0], None)
            odd[k] = (-2.0 * y[k][1], None)
        else:
            o = y[n // 2 - k]
            even[k] = (y[k][0] + o[0], y[k][1] - o[1])
            odd[k] = turn(k, n, (y[k][0] - o[0], y[k][1] + o[1]), 1)
    out = [None] * n
    out[0::2] = real_backward(even)
    out[1::2] = real_backward(odd)
    return out


def flow_rule(elastic, shear2, radius):
    volume = elastic[0] + elastic[1] + elastic[2]
    mean = volume * (1.0 / 3.0)
    deviator = [elastic[i] - mean for i in range(3)] + list(elastic[3:])
    trial = [shear2 * d for d in deviator]
    normal = trial[0] * trial[0] + trial[1] * trial[1] + trial[2] * trial[2]
    mixed = trial[3] * trial[3] + trial[4] * trial[4] + trial[5] * trial[5]
    squared = normal + (mixed + mixed)
    factor = radius * lax.rsqrt(jnp.maximum(squared, radius * radius))
    return volume, deviator, trial, factor


HALVES = (slice(0, 128), slice(128, 256))


def solve_kernel(
    plastic_ref, macro_ref, counts_ref, bulk_ref, shear_ref, radius_ref, dft_ref, green_ref,
    next_ref, mean_ref,
    halves_s, copy_sem, material_s, green_s, plastic_s, strain_s, stress_s, update_s, mapped_s, left_s, product_s, left2_s, product2_s,
):
    f32, bf16 = jnp.float32, jnp.bfloat16
    counts = counts_ref[...]
    incoming = [
        pltpu.make_async_copy(plastic_ref.at[:, lanes], halves_s.at[h], copy_sem.at[h]) for h, lanes in enumerate(HALVES)
    ]
    for copy in incoming:
        copy.start()
    for a in range(16):
        shear2 = 2.0 * shear_ref[a : a + 1, :]
        for i, row in enumerate((shear2, bulk_ref[a : a + 1, :], radius_ref[a : a + 1, :])):
            material_s[a, i] = jnp.broadcast_to(row, (8, 256))

    @pl.loop(0, 24)
    def _(block):
        rows = green_ref[pl.ds(pl.multiple_of(block * 8, 8), 8), :]
        for r in range(8):
            green_s[block * 8 + r] = jnp.broadcast_to(rows[r : r + 1, :], (8, 256))

    for copy in incoming:
        copy.wait()

    @pl.loop(0, 96, unroll=4)
    def _(row):
        for h, lanes in enumerate(HALVES):
            plastic_s[row, :, lanes] = halves_s[h, pl.ds(row, 8, stride=96), :]

    for c in range(6):
        start = jnp.broadcast_to(macro_ref[:, c : c + 1], (8, 256))

        @pl.loop(0, 16)
        def _(a):
            strain_s[c * 16 + a] = start

    def split(value):
        high = value.astype(bf16)
        low = (value - high.astype(f32)).astype(bf16)
        return high, low

    def polarization():
        @pl.loop(0, 16)
        def _(a):
            for lanes in HALVES:
                shear2 = material_s[a, 0, :, lanes]
                bulk = material_s[a, 1, :, lanes]
                radius = material_s[a, 2, :, lanes]
                elastic = [strain_s[c * 16 + a, :, lanes] - plastic_s[c * 16 + a, :, lanes] for c in range(6)]
                volume, _, trial, factor = flow_rule(elastic, shear2, radius)
                pressure = bulk * volume
                for c in range(6):
                    value = factor * trial[c]
                    stress_s[c * 16 + a, :, lanes] = value + pressure if c < 3 else value

        @pl.loop(0, 3)
        def _(pair):
            for lanes in HALVES:
                sets = []
                for half in range(2):
                    y = real_forward([stress_s[pair * 32 + half * 16 + a, :, lanes] for a in range(16)])
                    sets.append([y[0][0], y[8][0]] + [part for k in range(1, 8) for part in y[k]])
                rows = pl.ds(pl.multiple_of(pair * 16, 16), 16)
                for r in range(16):
                    high, low = split(jnp.concatenate([sets[0][r], sets[1][r]], axis=0))
                    left_s[r, rows, lanes] = high
                    left_s[r, rows, slice(256 + lanes.start, 256 + lanes.stop)] = low

        left = left_s[...].reshape(768, 512)
        product_s[...] = jnp.dot(
            jnp.concatenate([left, left[:, :256]], axis=1), dft_ref[...], preferred_element_type=f32
        ).reshape(16, 48, 512)

        def operate(k, re, im, lanes):
            for t, value in ((2 * k, re), (2 * k + 1, im)):
                value = value[:3] + [v + v for v in value[3:]]
                out = [None] * 6
                j = 0
                for i in range(6):
                    for m in range(i, 6):
                        g = green_s[k * 21 + j, :, lanes]
                        j += 1
                        out[i] = g * value[m] if out[i] is None else out[i] + g * value[m]
                        if m != i:
                            out[m] = g * value[i] if out[m] is None else out[m] + g * value[i]
                for pair in range(3):
                    high, low = split(jnp.concatenate([out[2 * pair], out[2 * pair + 1]], axis=0))
                    left2_s[t, slice(pair * 16, pair * 16 + 16), lanes] = high
                    left2_s[t, slice(pair * 16, pair * 16 + 16), slice(256 + lanes.start, 256 + lanes.stop)] = low

        for k, row in ((0, 0), (8, 1)):
            for lanes in HALVES:
                wide = slice(256 + lanes.start, 256 + lanes.stop)
                re = [product_s[row, slice(c * 8, c * 8 + 8), lanes] for c in range(6)]
                im = [-product_s[row, slice(c * 8, c * 8 + 8), wide] for c in range(6)]
                operate(k, re, im, lanes)

        @pl.loop(1, 8)
        def _(k):
            for lanes in HALVES:
                wide = slice(256 + lanes.start, 256 + lanes.stop)
                re, im = [], []
                for c in range(6):
                    rows = slice(c * 8, c * 8 + 8)
                    re.append(product_s[2 * k, rows, lanes] + product_s[2 * k + 1, rows, wide])
                    im.append(product_s[2 * k + 1, rows, lanes] - product_s[2 * k, rows, wide])
                operate(k, re, im, lanes)

        left2 = left2_s[...].reshape(864, 512)
        product2_s[...] = jnp.dot(
            jnp.concatenate([left2, left2[:, :256]], axis=1), dft_ref[...], preferred_element_type=f32
        ).reshape(18, 48, 512)

    def update_of(c, lanes):
        wide = slice(256 + lanes.start, 256 + lanes.stop)
        rows = pl.ds(pl.multiple_of(c * 8, 8), 8)
        y = []
        for k in range(9):
            re = product2_s[2 * k, rows, lanes] - product2_s[2 * k + 1, rows, wide]
            im = None if k in (0, 8) else product2_s[2 * k, rows, wide] + product2_s[2 * k + 1, rows, lanes]
            y.append((re, im))
        return real_backward(y)

    polarization()
    active = counts > 0

    @pl.loop(0, 6)
    def _(c):
        for lanes in HALVES:
            update = update_of(c, lanes)
            for a in range(16):
                strain = strain_s[c * 16 + a, :, lanes]
                strain_s[c * 16 + a, :, lanes] = jnp.where(active, strain - update[a], strain)
                update_s[c * 16 + a, :, lanes] = update[a]
                mapped_s[c * 16 + a, :, lanes] = strain - update[a]

    @pl.loop(1, 3)
    def _(step):
        polarization()
        zero = jnp.zeros((8, 128), f32)

        def gather(c, carry):
            numerator, denominator = carry
            for lanes in HALVES:
                update = update_of(c, lanes)
                for a in range(16):
                    change = update[a] - update_s[c * 16 + a, :, lanes]
                    numerator = numerator + change * update[a]
                    denominator = denominator + change * change
                    update_s[c * 16 + a, :, lanes] = update[a]
            return numerator, denominator

        numerator, denominator = lax.fori_loop(0, 6, gather, (zero, zero))
        scale = 1.0 / float(6 * 16**3)
        numerator = jnp.sum(numerator, axis=1, keepdims=True) * scale
        denominator = jnp.sum(denominator, axis=1, keepdims=True) * scale + 1e-06
        weight = jnp.broadcast_to(numerator / denominator, (8, 256))
        active = jnp.broadcast_to(step < counts, (8, 256))

        @pl.loop(0, 96, unroll=4)
        def _(row):
            strain = strain_s[row]
            mapped = strain - update_s[row]
            candidate = mapped - weight * (mapped - mapped_s[row])
            mapped_s[row] = mapped
            strain_s[row] = jnp.where(active, candidate, strain)

    def finish(a, sums):
        sums = list(sums)
        for lanes in HALVES:
            shear2 = material_s[a, 0, :, lanes]
            bulk = material_s[a, 1, :, lanes]
            radius = material_s[a, 2, :, lanes]
            plastic = [plastic_s[c * 16 + a, :, lanes] for c in range(6)]
            elastic = [strain_s[c * 16 + a, :, lanes] - plastic[c] for c in range(6)]
            volume, deviator, trial, factor = flow_rule(elastic, shear2, radius)
            pressure = bulk * volume
            for c in range(6):
                value = factor * trial[c]
                sums[c] = sums[c] + (value + pressure if c < 3 else value)
                plastic_s[c * 16 + a, :, lanes] = plastic[c] + (deviator[c] - factor * deviator[c])
        return tuple(sums)

    zero = jnp.zeros((8, 128), f32)
    sums = lax.fori_loop(0, 16, finish, (zero,) * 6)
    lane = lax.broadcasted_iota(jnp.int32, (8, 128), 1)
    means = zero
    for c in range(6):
        means = jnp.where(lane == c, jnp.sum(sums[c], axis=1, keepdims=True) * (1.0 / 4096.0), means)
    mean_ref[...] = means

    @pl.loop(0, 96, unroll=4)
    def _(row):
        for h, lanes in enumerate(HALVES):
            halves_s[h, pl.ds(row, 8, stride=96), :] = plastic_s[row, :, lanes]

    outgoing = [
        pltpu.make_async_copy(halves_s.at[h], next_ref.at[:, lanes], copy_sem.at[h]) for h, lanes in enumerate(HALVES)
    ]
    for copy in outgoing:
        copy.start()
    for copy in outgoing:
        copy.wait()


def solve(plastic, macro, counts, bulk, shear, radius):
    f32, bf16 = jnp.float32, jnp.bfloat16
    vm = pl.BlockSpec(memory_space=pltpu.VMEM)
    updated, means = pl.pallas_call(
        solve_kernel,
        out_shape=(jax.ShapeDtypeStruct((768, 256), f32), jax.ShapeDtypeStruct((8, 128), f32)),
        in_specs=[pl.BlockSpec(memory_space=pl.ANY)] + [vm] * 7,
        out_specs=(pl.BlockSpec(memory_space=pl.ANY), vm),
        scratch_shapes=[
            pltpu.VMEM((2, 768, 128), f32),
            pltpu.SemaphoreType.DMA((2,)),
            pltpu.VMEM((16, 3, 8, 256), f32),
            pltpu.VMEM((192, 8, 256), f32),
            pltpu.VMEM((96, 8, 256), f32),
            pltpu.VMEM((96, 8, 256), f32),
            pltpu.VMEM((96, 8, 256), f32),
            pltpu.VMEM((96, 8, 256), f32),
            pltpu.VMEM((96, 8, 256), f32),
            pltpu.VMEM((16, 48, 512), bf16),
            pltpu.VMEM((16, 48, 512), f32),
            pltpu.VMEM((18, 48, 512), bf16),
            pltpu.VMEM((18, 48, 512), f32),
        ],
        compiler_params=pltpu.CompilerParams(vmem_limit_bytes=48 << 20),
        name="solve",
    )(
        plastic.reshape(768, 256),
        macro,
        counts[:, None],
        bulk,
        shear,
        radius,
        jnp.asarray(transform_tables(16)),
        jnp.asarray(green_table(16)),
    )
    return updated, means


MESH_ID = pl.DeviceIdType.MESH
GROUP, COLUMNS, SLOTS, PACK = 32, 8, 8, 2


def place(layer, column):
    return {"rve_0": layer // 4, "rve_1": layer % 4, "mic": column // 2, "mac": column % 2}


def own_place():
    layer = lax.axis_index("rve_0") * 4 + lax.axis_index("rve_1")
    return layer, lax.axis_index("mic") * 2 + lax.axis_index("mac")


def gossip_kernel(
    row_ref, rows_ref, columns_ref, used_ref, sent, group, second, across, send_a, recv_a, send_b, recv_b
):
    layer, column = own_place()
    barrier = pltpu.get_barrier_semaphore()

    @pl.loop(1, GROUP)
    def _(step):
        peer = lax.rem(layer + step, GROUP)
        pl.semaphore_signal(barrier, inc=1, device_id=place(peer, column), device_id_type=MESH_ID)

    @pl.loop(1, COLUMNS)
    def _(step):
        peer = lax.rem(column + step, COLUMNS)
        pl.semaphore_signal(barrier, inc=1, device_id=place(layer, peer), device_id_type=MESH_ID)

    sent[...] = row_ref[...]
    group[layer] = row_ref[0]
    pl.semaphore_wait(barrier, GROUP + COLUMNS - 2)

    def to_layer(step):
        peer = lax.rem(layer + step, GROUP)
        return pltpu.make_async_remote_copy(
            src_ref=sent.at[0],
            dst_ref=group.at[layer],
            send_sem=send_a.at[step],
            recv_sem=recv_a.at[step],
            device_id=place(peer, column),
            device_id_type=MESH_ID,
        )

    def to_column(step):
        peer = lax.rem(column + step, COLUMNS)
        return pltpu.make_async_remote_copy(
            src_ref=second.at[0],
            dst_ref=across.at[column],
            send_sem=send_b.at[step],
            recv_sem=recv_b.at[step],
            device_id=place(layer, peer),
            device_id_type=MESH_ID,
        )

    pl.loop(1, GROUP)(lambda step: to_layer(step).start())
    pl.loop(1, GROUP)(lambda step: to_layer(step).wait())
    lane = lax.broadcasted_iota(jnp.int32, (1, 128), 1)
    used = group[0]
    for i in range(1, GROUP):
        used = jnp.maximum(used, group[i])
    upper = pltpu.roll(group[lax.rem(layer + 1, GROUP)], 32, 1)
    upper = jnp.where(layer < GROUP - 1, upper, jnp.zeros_like(upper))
    mixed = jnp.where(lane < 64, used, jnp.where(lane < 96, row_ref[0], upper))
    second[0] = mixed
    across[column] = mixed
    pl.loop(1, COLUMNS)(lambda step: to_column(step).start())
    pl.loop(1, COLUMNS)(lambda step: to_column(step).wait())
    used = across[0]
    for i in range(1, COLUMNS):
        used = jnp.maximum(used, across[i])
    used_ref[...] = used
    rows_ref[...] = group[...]
    right = across[lax.rem(column + 1, COLUMNS)]
    columns_ref[0] = across[column]
    columns_ref[1] = jnp.where(column < COLUMNS - 1, right, jnp.zeros_like(right))


def gossip(row):
    vm = pl.BlockSpec(memory_space=pltpu.VMEM)
    f32 = jnp.float32
    return pl.pallas_call(
        gossip_kernel,
        out_shape=(
            jax.ShapeDtypeStruct((GROUP, 1, 128), f32),
            jax.ShapeDtypeStruct((2, 1, 128), f32),
            jax.ShapeDtypeStruct((1, 128), f32),
        ),
        in_specs=[vm],
        out_specs=(vm, vm, vm),
        scratch_shapes=[
            pltpu.VMEM((1, 1, 128), f32),
            pltpu.VMEM((GROUP, 1, 128), f32),
            pltpu.VMEM((1, 1, 128), f32),
            pltpu.VMEM((COLUMNS, 1, 128), f32),
            pltpu.SemaphoreType.DMA((GROUP,)),
            pltpu.SemaphoreType.DMA((GROUP,)),
            pltpu.SemaphoreType.DMA((COLUMNS,)),
            pltpu.SemaphoreType.DMA((COLUMNS,)),
        ],
        compiler_params=pltpu.CompilerParams(collective_id=0, has_side_effects=True),
        name="gossip",
    )(row)


def agenda_kernel(here_ref, plan_ref, used_ref, total_ref, shift_ref, pick_ref, land_ref):
    layer = here_ref[0]
    total_ref[0] = 0

    @pl.loop(0, GROUP)
    def _(d):
        shift_ref[d] = 0
        pick_ref[d, 0] = 0
        pick_ref[d, 1] = 0
        land_ref[d, 0] = SLOTS
        land_ref[d, 1] = SLOTS

    @pl.loop(0, GROUP)
    def _(d):
        @pl.when(used_ref[32 + d] > 0)
        def _():
            step = total_ref[0]
            shift_ref[step] = d
            total_ref[0] = step + 1
            target, source = lax.rem(layer + d, GROUP), lax.rem(layer - d + GROUP, GROUP)
            out_rank, in_rank = jnp.int32(0), jnp.int32(0)
            for i in range(SLOTS):
                goes = plan_ref[layer, i] // (SLOTS * COLUMNS) == target
                value = plan_ref[source, i]
                comes = value // (SLOTS * COLUMNS) == layer

                @pl.when(goes & (out_rank < PACK))
                def _():
                    pick_ref[step, out_rank] = i

                @pl.when(comes & (in_rank < PACK))
                def _():
                    land_ref[step, in_rank] = lax.rem(value, SLOTS)

                out_rank = out_rank + goes.astype(jnp.int32)
                in_rank = in_rank + comes.astype(jnp.int32)


def agenda(here, plan, used):
    sm = pl.BlockSpec(memory_space=pltpu.SMEM)
    i32 = jnp.int32
    return pl.pallas_call(
        agenda_kernel,
        out_shape=(
            jax.ShapeDtypeStruct((1,), i32),
            jax.ShapeDtypeStruct((GROUP,), i32),
            jax.ShapeDtypeStruct((GROUP, PACK), i32),
            jax.ShapeDtypeStruct((GROUP, PACK), i32),
        ),
        in_specs=[sm] * 3,
        out_specs=(sm,) * 4,
        name="agenda",
    )(here, plan, used)


def rotate_kernel(shift, sent_ref, got_ref, arrival, send_sem, recv_sem):
    layer, column = own_place()
    target, source = lax.rem(layer + shift, GROUP), lax.rem(layer + GROUP - shift, GROUP)
    barrier = pltpu.get_barrier_semaphore()
    pl.semaphore_signal(barrier, inc=1, device_id=place(source, column), device_id_type=MESH_ID)
    pl.semaphore_wait(barrier, 1)
    copy = pltpu.make_async_remote_copy(
        src_ref=sent_ref,
        dst_ref=arrival,
        send_sem=send_sem,
        recv_sem=recv_sem,
        device_id=place(target, column),
        device_id_type=MESH_ID,
    )
    copy.start()
    copy.wait()
    got_ref[...] = arrival[...]


def rotate(shift, packets):
    vm = pl.BlockSpec(memory_space=pltpu.VMEM)
    return pl.pallas_call(
        functools.partial(rotate_kernel, shift),
        out_shape=jax.ShapeDtypeStruct(packets.shape, packets.dtype),
        in_specs=[vm],
        out_specs=vm,
        scratch_shapes=[
            pltpu.VMEM(packets.shape, packets.dtype),
            pltpu.SemaphoreType.DMA,
            pltpu.SemaphoreType.DMA,
        ],
        compiler_params=pltpu.CompilerParams(collective_id=shift, has_side_effects=True),
        name=f"rotate{shift}",
    )(packets)


def land_kernel(step_ref, land_ref, got_ref, held_ref, out_ref, sems):
    step = step_ref[0]
    for j in range(PACK):
        row = land_ref[step, j]

        @pl.when(row < SLOTS)
        def _():
            pltpu.make_async_copy(got_ref.at[j], out_ref.at[row], sems.at[j]).start()

    for j in range(PACK):
        row = land_ref[step, j]

        @pl.when(row < SLOTS)
        def _():
            pltpu.make_async_copy(got_ref.at[j], out_ref.at[row], sems.at[j]).wait()


def land(step, rows, got, held):
    vm, sm = pl.BlockSpec(memory_space=pltpu.VMEM), pl.BlockSpec(memory_space=pltpu.SMEM)
    anywhere = pl.BlockSpec(memory_space=pl.ANY)
    return pl.pallas_call(
        land_kernel,
        out_shape=jax.ShapeDtypeStruct(held.shape, held.dtype),
        in_specs=[sm, sm, vm, anywhere],
        out_specs=anywhere,
        scratch_shapes=[pltpu.SemaphoreType.DMA((PACK,))],
        input_output_aliases={3: 0},
        name="land",
    )(step, rows, got, held)


def migrate(updated, total, shifts, picks, rows):
    branches = [lambda packets: packets] + [functools.partial(rotate, d) for d in range(1, GROUP)]

    def step(state):
        i, held = state
        pick = lax.dynamic_slice(picks, (i, 0), (1, PACK))[0]
        packets = jnp.concatenate(
            [lax.dynamic_slice(updated, (pick[j], 0, 0), (1, 96, 256)) for j in range(PACK)], axis=0
        )
        got = lax.switch(shifts[i], branches, packets)
        return i + 1, land(i.reshape(1), rows, got, held)

    start = (jnp.int32(0), jnp.zeros_like(updated))
    return lax.while_loop(lambda state: state[0] < total, step, start)[1]


def shifted(value, axis, steps):
    count = lax.axis_size(axis)
    first, last = (max(0, -steps), min(count, count - steps))
    return lax.ppermute(value, axis, [(source, source + steps) for source in range(first, last)])


def element_strain(extended):
    rows_y, depth = extended.shape[2] - 1, extended.shape[3]
    extended = jnp.pad(extended, ((0, 0), (0, 0), (0, 0), (0, 1)))
    gradient = [[0.0, 0.0, 0.0], [0.0, 0.0, 0.0], [0.0, 0.0, 0.0]]
    for shift_a in (0, 1):
        for shift_b in (0, 1):
            for shift_c in (0, 1):
                corner_values = extended[
                    :, shift_a : shift_a + 1, shift_b : shift_b + rows_y, shift_c : shift_c + depth
                ]
                signs = ((2 * shift_a - 1) / 4.0, (2 * shift_b - 1) / 4.0, (2 * shift_c - 1) / 4.0)
                for component in range(3):
                    for direction in range(3):
                        gradient[component][direction] = (
                            gradient[component][direction]
                            + corner_values[component] * signs[direction]
                        )
    strain_field = jnp.stack(
        [
            gradient[0][0],
            gradient[1][1],
            gradient[2][2],
            0.5 * (gradient[1][2] + gradient[2][1]),
            0.5 * (gradient[0][2] + gradient[2][0]),
            0.5 * (gradient[0][1] + gradient[1][0]),
        ],
        axis=0,
    )
    return strain_field.reshape(6, rows_y * depth).T


def nodal_forces(averages, rows_y, depth):
    macro_stress = averages.T.reshape(6, 1, rows_y, depth)
    lower_layer = shifted(macro_stress, RVE, 1)
    extended = jnp.concatenate([lower_layer, macro_stress], axis=1)
    lower_row = shifted(extended, ("mic", "mac"), 1)
    extended = jnp.concatenate([lower_row, extended], axis=2)
    extended = jnp.pad(extended, ((0, 0), (0, 0), (0, 0), (1, 0)))
    pairs = [[0, 5, 4], [5, 1, 3], [4, 3, 2]]
    forces = [0.0, 0.0, 0.0]
    for shift_a in (0, 1):
        for shift_b in (0, 1):
            for shift_c in (0, 1):
                corner_values = extended[
                    :,
                    1 - shift_a : 2 - shift_a,
                    1 - shift_b : 1 - shift_b + rows_y,
                    1 - shift_c : 1 - shift_c + depth,
                ]
                signs = ((2 * shift_a - 1) / 4.0, (2 * shift_b - 1) / 4.0, (2 * shift_c - 1) / 4.0)
                for component in range(3):
                    for direction in range(3):
                        forces[component] = (
                            forces[component]
                            + corner_values[pairs[component][direction]] * signs[direction]
                        )
    return jnp.stack(forces, axis=0)


def on_device(
    displacement, plastic, bulk_modulus, shear_modulus, yield_radius, counts, migration_plan
):
    depth = displacement.shape[3]
    layer, column = own_place()
    shift = (migration_plan // (SLOTS * COLUMNS) - layer + GROUP) % GROUP
    seen = jnp.any(shift[:, None] == jnp.arange(GROUP)[None, :], axis=0)
    row = jnp.concatenate(
        [
            jnp.pad(migration_plan, (0, 24)).astype(jnp.float32),
            seen.astype(jnp.float32),
            jnp.pad(displacement.reshape(3 * depth), (0, 64 - 3 * depth)),
        ]
    )
    rows, columns, used = gossip(row.reshape(1, 1, 128))
    here = columns[:, 0, 64:].reshape(2, 2, 32)[:, :, : 3 * depth].reshape(2, 2, 3, depth)
    strain_rows = element_strain(jnp.transpose(here, (2, 1, 0, 3)))
    total, shifts, picks, landing = agenda(
        layer.reshape(1), rows[:, 0, :SLOTS].astype(jnp.int32), used[0].astype(jnp.int32)
    )
    updated, means = solve(
        plastic, strain_rows, counts, bulk_modulus, shear_modulus, yield_radius
    )
    force = nodal_forces(means[:, :6], displacement.shape[2], depth)
    moved = migrate(updated.reshape(SLOTS, 96, 256), total[0], shifts, picks, landing)
    return (force, moved.reshape(plastic.shape))


def solution(mesh):
    finer = Mesh(
        mesh.devices.reshape(8, 4, mesh.shape["mic"], mesh.shape["mac"]),
        ("rve_0", "rve_1", "mic", "mac"),
    )
    placed = (
        P(None, RVE, ("mic", "mac"), None),
        P(RVE_MIC_MAC, None, None, None),
        P(),
        P(),
        P(),
        P(RVE_MIC_MAC),
        P(RVE_MIC_MAC),
    )
    return jax.shard_map(
        on_device,
        mesh=finer,
        in_specs=placed,
        out_specs=(P(None, RVE, ("mic", "mac"), None), P(RVE_MIC_MAC, None, None, None)),
        check_vma=False,
    )
```

```python
import functools
import math

import jax
import jax.numpy as jnp
import numpy as np
from jax import lax
from jax.experimental import pallas as pl
from jax.experimental.pallas import tpu as pltpu
from jax.sharding import Mesh
from jax.sharding import PartitionSpec as P

RVE = ("rve_0", "rve_1")
RVE_MIC_MAC = ("rve_0", "rve_1", "mic", "mac")


COUPLING = 0.7
PAIRS = ((0, 0), (1, 1), (2, 2), (1, 2), (0, 2), (0, 1))


def transform_tables(n):
    plane = np.arange(n * n)
    b, c = plane // n, plane % n
    angle = 2.0 * np.pi / n * ((np.outer(b, b) + np.outer(c, c)) % n)
    table = np.concatenate([np.cos(angle), np.sin(angle)], axis=1).astype(np.float32)
    high = table.astype(jnp.bfloat16)
    low = (table - high.astype(np.float32)).astype(jnp.bfloat16)
    return np.concatenate([high, low], axis=0)


def green_table(n):
    index = np.stack(np.meshgrid(np.arange(n), np.arange(n), np.arange(n), indexing="ij"))

    def operator(i):
        k = ((i + n // 2) % n - n // 2).astype(np.float64)
        q = np.sum(k * k, axis=0)
        safe = np.maximum(q, 1.0)
        rows = []
        for m, r in PAIRS:
            row = []
            for p, s in PAIRS:
                eye = lambda u, v: 1.0 if u == v else 0.0
                first = (
                    eye(m, p) * k[r] * k[s] + eye(m, s) * k[r] * k[p] + eye(r, p) * k[m] * k[s] + eye(r, s) * k[m] * k[p]
                ) / (4.0 * safe)
                row.append(first - COUPLING * k[m] * k[r] * k[p] * k[s] / (safe * safe))
            rows.append(row)
        return np.where(q > 0, np.array(rows), 0.0)

    even = 0.5 * (operator(index) + operator((-index) % n)) / float(n**3)
    even = even[:, :, : n // 2 + 1]
    rows = [even[i, j].reshape(n // 2 + 1, n * n) for i in range(6) for j in range(i, 6)]
    table = np.stack(rows, axis=1).reshape(-1, n * n).astype(np.float32)
    return np.pad(table, ((0, -table.shape[0] % 8), (0, 0)))


def turn(k, n, value, sign):
    re, im = value
    if k == 0:
        return value
    if 4 * k == n:
        return (im, -re) if sign < 0 else (-im, re)
    if 8 * k == n:
        r = math.sqrt(0.5)
        return ((re + im) * r, (im - re) * r) if sign < 0 else ((re - im) * r, (re + im) * r)
    c, s = math.cos(2 * math.pi * k / n), sign * math.sin(2 * math.pi * k / n)
    return (re * c - im * s, re * s + im * c)


def real_forward(x):
    n = len(x)
    if n == 2:
        return [(x[0] + x[1], None), (x[0] - x[1], None)]
    even, odd = real_forward(x[0::2]), real_forward(x[1::2])
    out = [None] * (n // 2 + 1)
    out[0] = (even[0][0] + odd[0][0], None)
    out[n // 2] = (even[0][0] - odd[0][0], None)
    for k in range(1, n // 4 + 1):
        if 4 * k == n:
            out[k] = (even[k][0], -odd[k][0])
        else:
            t = turn(k, n, odd[k], -1)
            out[k] = (even[k][0] + t[0], even[k][1] + t[1])
            out[n // 2 - k] = (even[k][0] - t[0], t[1] - even[k][1])
    return out


def real_backward(y):
    n = 2 * (len(y) - 1)
    if n == 2:
        return [y[0][0] + y[1][0], y[0][0] - y[1][0]]
    even, odd = [None] * (n // 4 + 1), [None] * (n // 4 + 1)
    even[0] = (y[0][0] + y[n // 2][0], None)
    odd[0] = (y[0][0] - y[n // 2][0], None)
    for k in range(1, n // 4 + 1):
        if 4 * k == n:
            even[k] = (2.0 * y[k][0], None)
            odd[k] = (-2.0 * y[k][1], None)
        else:
            o = y[n // 2 - k]
            even[k] = (y[k][0] + o[0], y[k][1] - o[1])
            odd[k] = turn(k, n, (y[k][0] - o[0], y[k][1] + o[1]), 1)
    out = [None] * n
    out[0::2] = real_backward(even)
    out[1::2] = real_backward(odd)
    return out


def flow_rule(elastic, shear2, radius):
    volume = elastic[0] + elastic[1] + elastic[2]
    mean = volume * (1.0 / 3.0)
    deviator = [elastic[i] - mean for i in range(3)] + list(elastic[3:])
    trial = [shear2 * d for d in deviator]
    normal = trial[0] * trial[0] + trial[1] * trial[1] + trial[2] * trial[2]
    mixed = trial[3] * trial[3] + trial[4] * trial[4] + trial[5] * trial[5]
    squared = normal + (mixed + mixed)
    factor = radius * lax.rsqrt(jnp.maximum(squared, radius * radius))
    return volume, deviator, trial, factor


HALVES = (slice(0, 128), slice(128, 256))


def solve_kernel(
    order_ref, plastic_ref, macro_ref, counts_ref, bulk_ref, shear_ref, radius_ref, dft_hbm, green_hbm,
    first_ref, second_ref, third_ref, fourth_ref, mean_ref,
    packed_s, packed_sem, halves_s, copy_sem, dft_ref, green_ref, table_sem, material_s, green_s, plastic_s, strain_s, stress_s, update_s, mapped_s, left_s, product_s, left2_s, product2_s,
):
    f32, bf16 = jnp.float32, jnp.bfloat16
    counts = counts_ref[...]
    incoming = [
        pltpu.make_async_copy(plastic_ref.at[:, lanes], halves_s.at[h], copy_sem.at[h]) for h, lanes in enumerate(HALVES)
    ]
    tables = [
        pltpu.make_async_copy(green_hbm, green_ref, table_sem.at[0]),
        pltpu.make_async_copy(dft_hbm.at[:256], dft_ref.at[:256], table_sem.at[1]),
        pltpu.make_async_copy(dft_hbm, dft_ref.at[256:], table_sem.at[2]),
    ]
    for copy in incoming + tables:
        copy.start()
    for a in range(16):
        shear2 = 2.0 * shear_ref[a : a + 1, :]
        for i, row in enumerate((shear2, bulk_ref[a : a + 1, :], radius_ref[a : a + 1, :])):
            material_s[a, i] = jnp.broadcast_to(row, (8, 256))

    for copy in incoming:
        copy.wait()

    @pl.loop(0, 96, unroll=4)
    def _(row):
        for h, lanes in enumerate(HALVES):
            plastic_s[row, :, lanes] = halves_s[h, pl.ds(row, 8, stride=96), :]

    for c in range(6):
        start = jnp.broadcast_to(macro_ref[:, c : c + 1], (8, 256))

        @pl.loop(0, 16)
        def _(a):
            strain_s[c * 16 + a] = start

    def split(value):
        high = value.astype(bf16)
        low = (value - high.astype(f32)).astype(bf16)
        return high, low

    def polarization(step):
        @pl.loop(0, 16)
        def _(a):
            for lanes in HALVES:
                shear2 = material_s[a, 0, :, lanes]
                bulk = material_s[a, 1, :, lanes]
                radius = material_s[a, 2, :, lanes]
                elastic = [strain_s[c * 16 + a, :, lanes] - plastic_s[c * 16 + a, :, lanes] for c in range(6)]
                volume, _, trial, factor = flow_rule(elastic, shear2, radius)
                pressure = bulk * volume
                for c in range(6):
                    value = factor * trial[c]
                    stress_s[c * 16 + a, :, lanes] = value + pressure if c < 3 else value

        @pl.loop(0, 3)
        def _(pair):
            for lanes in HALVES:
                sets = []
                for half in range(2):
                    y = real_forward([stress_s[pair * 32 + half * 16 + a, :, lanes] for a in range(16)])
                    sets.append([y[0][0], y[8][0]] + [part for k in range(1, 8) for part in y[k]])
                rows = pl.ds(pl.multiple_of(pair * 16, 16), 16)
                for r in range(16):
                    high, low = split(jnp.concatenate([sets[0][r], sets[1][r]], axis=0))
                    left_s[r, rows, lanes] = high
                    left_s[r, rows, slice(256 + lanes.start, 256 + lanes.stop)] = low

        @pl.when(step == 0)
        def _():
            tables[1].wait()
            tables[2].wait()
            tables[0].wait()

            @pl.loop(0, 24)
            def _(block):
                rows = green_ref[pl.ds(pl.multiple_of(block * 8, 8), 8), :]
                for r in range(8):
                    green_s[block * 8 + r] = jnp.broadcast_to(rows[r : r + 1, :], (8, 256))

        left = left_s[...].reshape(768, 512)
        product_s[...] = jnp.dot(
            jnp.concatenate([left, left[:, :256]], axis=1), dft_ref[...], preferred_element_type=f32
        ).reshape(16, 48, 512)

        def operate(k, re, im, lanes):
            for t, value in ((2 * k, re), (2 * k + 1, im)):
                value = value[:3] + [v + v for v in value[3:]]
                out = [None] * 6
                j = 0
                for i in range(6):
                    for m in range(i, 6):
                        g = green_s[k * 21 + j, :, lanes]
                        j += 1
                        out[i] = g * value[m] if out[i] is None else out[i] + g * value[m]
                        if m != i:
                            out[m] = g * value[i] if out[m] is None else out[m] + g * value[i]
                for pair in range(3):
                    high, low = split(jnp.concatenate([out[2 * pair], out[2 * pair + 1]], axis=0))
                    left2_s[t, slice(pair * 16, pair * 16 + 16), lanes] = high
                    left2_s[t, slice(pair * 16, pair * 16 + 16), slice(256 + lanes.start, 256 + lanes.stop)] = low

        for k, row in ((0, 0), (8, 1)):
            for lanes in HALVES:
                wide = slice(256 + lanes.start, 256 + lanes.stop)
                re = [product_s[row, slice(c * 8, c * 8 + 8), lanes] for c in range(6)]
                im = [-product_s[row, slice(c * 8, c * 8 + 8), wide] for c in range(6)]
                operate(k, re, im, lanes)

        @pl.loop(1, 8)
        def _(k):
            for lanes in HALVES:
                wide = slice(256 + lanes.start, 256 + lanes.stop)
                re, im = [], []
                for c in range(6):
                    rows = slice(c * 8, c * 8 + 8)
                    re.append(product_s[2 * k, rows, lanes] + product_s[2 * k + 1, rows, wide])
                    im.append(product_s[2 * k + 1, rows, lanes] - product_s[2 * k, rows, wide])
                operate(k, re, im, lanes)

        left2 = left2_s[...].reshape(864, 512)
        product2_s[...] = jnp.dot(
            jnp.concatenate([left2, left2[:, :256]], axis=1), dft_ref[...], preferred_element_type=f32
        ).reshape(18, 48, 512)

    def update_of(c, lanes):
        wide = slice(256 + lanes.start, 256 + lanes.stop)
        rows = pl.ds(pl.multiple_of(c * 8, 8), 8)
        y = []
        for k in range(9):
            re = product2_s[2 * k, rows, lanes] - product2_s[2 * k + 1, rows, wide]
            im = None if k in (0, 8) else product2_s[2 * k, rows, wide] + product2_s[2 * k + 1, rows, lanes]
            y.append((re, im))
        return real_backward(y)

    @pl.loop(0, 96, unroll=4)
    def _(row):
        update_s[row] = jnp.zeros((8, 256), f32)
        mapped_s[row] = strain_s[row]

    @pl.loop(0, 3)
    def _(step):
        polarization(step)
        zero = jnp.zeros((8, 128), f32)

        def gather(c, carry):
            numerator, denominator = carry
            for lanes in HALVES:
                update = update_of(c, lanes)
                for a in range(16):
                    change = update[a] - update_s[c * 16 + a, :, lanes]
                    numerator = numerator + change * update[a]
                    denominator = denominator + change * change
                    update_s[c * 16 + a, :, lanes] = update[a]
            return numerator, denominator

        numerator, denominator = lax.fori_loop(0, 6, gather, (zero, zero))
        scale = 1.0 / float(6 * 16**3)
        numerator = jnp.sum(numerator, axis=1, keepdims=True) * scale
        denominator = jnp.sum(denominator, axis=1, keepdims=True) * scale + 1e-06
        weight = jnp.broadcast_to(jnp.where(step > 0, numerator / denominator, 0.0), (8, 256))
        active = jnp.broadcast_to(step < counts, (8, 256))

        @pl.loop(0, 96, unroll=4)
        def _(row):
            strain = strain_s[row]
            mapped = strain - update_s[row]
            candidate = mapped - weight * (mapped - mapped_s[row])
            mapped_s[row] = mapped
            strain_s[row] = jnp.where(active, candidate, strain)

    def finish(a, sums):
        sums = list(sums)
        for lanes in HALVES:
            shear2 = material_s[a, 0, :, lanes]
            bulk = material_s[a, 1, :, lanes]
            radius = material_s[a, 2, :, lanes]
            plastic = [plastic_s[c * 16 + a, :, lanes] for c in range(6)]
            elastic = [strain_s[c * 16 + a, :, lanes] - plastic[c] for c in range(6)]
            volume, deviator, trial, factor = flow_rule(elastic, shear2, radius)
            pressure = bulk * volume
            for c in range(6):
                value = factor * trial[c]
                sums[c] = sums[c] + (value + pressure if c < 3 else value)
                plastic_s[c * 16 + a, :, lanes] = plastic[c] + (deviator[c] - factor * deviator[c])
        return tuple(sums)

    zero = jnp.zeros((8, 128), f32)
    sums = lax.fori_loop(0, 16, finish, (zero,) * 6)
    lane = lax.broadcasted_iota(jnp.int32, (8, 128), 1)
    means = zero
    for c in range(6):
        means = jnp.where(lane == c, jnp.sum(sums[c], axis=1, keepdims=True) * (1.0 / 4096.0), means)
    mean_ref[...] = means

    @pl.loop(0, 96, unroll=4)
    def _(row):
        for h, lanes in enumerate(HALVES):
            halves_s[h, pl.ds(row, 8, stride=96), :] = plastic_s[row, :, lanes]

    packed = [
        pltpu.make_async_copy(packed_s.at[flow], out_ref, packed_sem.at[flow])
        for flow, out_ref in enumerate((first_ref, second_ref, third_ref, fourth_ref))
    ]
    for flow, copy in enumerate(packed):
        for j in range(2):
            rows = pl.ds(pl.multiple_of(order_ref[2 * flow + j] * 96, 96), 96)
            for h, lanes in enumerate(HALVES):
                packed_s[flow, j, :, lanes] = halves_s[h, rows, :]
        copy.start()
    for copy in packed:
        copy.wait()


def solve(order, plastic, macro, counts, bulk, shear, radius):
    f32, bf16 = jnp.float32, jnp.bfloat16
    vm, sm = pl.BlockSpec(memory_space=pltpu.VMEM), pl.BlockSpec(memory_space=pltpu.SMEM)
    anywhere = pl.BlockSpec(memory_space=pltpu.HBM)
    pair = jax.ShapeDtypeStruct((2, 96, 256), f32)
    return pl.pallas_call(
        solve_kernel,
        out_shape=(pair, pair, pair, pair, jax.ShapeDtypeStruct((8, 128), f32)),
        in_specs=[sm, anywhere] + [vm] * 5 + [anywhere] * 2,
        out_specs=(anywhere,) * 4 + (vm,),
        scratch_shapes=[
            pltpu.VMEM((4, 2, 96, 256), f32),
            pltpu.SemaphoreType.DMA((4,)),
            pltpu.VMEM((2, 768, 128), f32),
            pltpu.SemaphoreType.DMA((2,)),
            pltpu.VMEM((768, 512), bf16),
            pltpu.VMEM((192, 256), f32),
            pltpu.SemaphoreType.DMA((3,)),
            pltpu.VMEM((16, 3, 8, 256), f32),
            pltpu.VMEM((192, 8, 256), f32),
            pltpu.VMEM((96, 8, 256), f32),
            pltpu.VMEM((96, 8, 256), f32),
            pltpu.VMEM((96, 8, 256), f32),
            pltpu.VMEM((96, 8, 256), f32),
            pltpu.VMEM((96, 8, 256), f32),
            pltpu.VMEM((16, 48, 512), bf16),
            pltpu.VMEM((16, 48, 512), f32),
            pltpu.VMEM((18, 48, 512), bf16),
            pltpu.VMEM((18, 48, 512), f32),
        ],
        compiler_params=pltpu.CompilerParams(vmem_limit_bytes=60 << 20),
        name="solve",
    )(
        order,
        plastic.reshape(768, 256),
        macro,
        counts[:, None],
        bulk,
        shear,
        radius,
        jnp.asarray(transform_tables(16)),
        jnp.asarray(green_table(16)),
    )


MESH_ID = pl.DeviceIdType.MESH
GROUP, COLUMNS, SLOTS, PACK = 32, 8, 8, 2


def place(layer, column):
    return {"rve_0": layer // 4, "rve_1": layer % 4, "mic": column // 2, "mac": column % 2}


def own_place():
    layer = lax.axis_index("rve_0") * 4 + lax.axis_index("rve_1")
    return layer, lax.axis_index("mic") * 2 + lax.axis_index("mac")


def gossip_kernel(
    row_ref, rows_ref, columns_ref, used_ref, sent, group, second, across, send_a, recv_a, send_b, recv_b
):
    layer, column = own_place()
    barrier = pltpu.get_barrier_semaphore()

    @pl.loop(1, GROUP)
    def _(step):
        peer = lax.rem(layer + step, GROUP)
        pl.semaphore_signal(barrier, inc=1, device_id=place(peer, column), device_id_type=MESH_ID)

    @pl.loop(1, COLUMNS)
    def _(step):
        peer = lax.rem(column + step, COLUMNS)
        pl.semaphore_signal(barrier, inc=1, device_id=place(layer, peer), device_id_type=MESH_ID)

    sent[...] = row_ref[...]
    group[layer] = row_ref[0]
    pl.semaphore_wait(barrier, GROUP + COLUMNS - 2)

    def to_layer(step):
        peer = lax.rem(layer + step, GROUP)
        return pltpu.make_async_remote_copy(
            src_ref=sent.at[0],
            dst_ref=group.at[layer],
            send_sem=send_a.at[step],
            recv_sem=recv_a.at[step],
            device_id=place(peer, column),
            device_id_type=MESH_ID,
        )

    def to_column(step):
        peer = lax.rem(column + step, COLUMNS)
        return pltpu.make_async_remote_copy(
            src_ref=second.at[0],
            dst_ref=across.at[column],
            send_sem=send_b.at[step],
            recv_sem=recv_b.at[step],
            device_id=place(layer, peer),
            device_id_type=MESH_ID,
        )

    pl.loop(1, GROUP)(lambda step: to_layer(step).start())
    pl.loop(1, GROUP)(lambda step: to_layer(step).wait())
    lane = lax.broadcasted_iota(jnp.int32, (1, 128), 1)
    used = group[0]
    for i in range(1, GROUP):
        used = jnp.maximum(used, group[i])
    upper = pltpu.roll(group[lax.rem(layer + 1, GROUP)], 32, 1)
    upper = jnp.where(layer < GROUP - 1, upper, jnp.zeros_like(upper))
    mixed = jnp.where(lane < 64, used, jnp.where(lane < 96, row_ref[0], upper))
    second[0] = mixed
    across[column] = mixed
    pl.loop(1, COLUMNS)(lambda step: to_column(step).start())
    pl.loop(1, COLUMNS)(lambda step: to_column(step).wait())
    used = across[0]
    for i in range(1, COLUMNS):
        used = jnp.maximum(used, across[i])
    used_ref[...] = used.astype(jnp.int32)
    rows_ref[...] = group[...].astype(jnp.int32)
    right = across[lax.rem(column + 1, COLUMNS)]
    columns_ref[0] = across[column]
    columns_ref[1] = jnp.where(column < COLUMNS - 1, right, jnp.zeros_like(right))


def gossip(row):
    vm = pl.BlockSpec(memory_space=pltpu.VMEM)
    f32 = jnp.float32
    return pl.pallas_call(
        gossip_kernel,
        out_shape=(
            jax.ShapeDtypeStruct((GROUP, 1, 128), jnp.int32),
            jax.ShapeDtypeStruct((2, 1, 128), f32),
            jax.ShapeDtypeStruct((1, 128), jnp.int32),
        ),
        in_specs=[vm],
        out_specs=(vm, vm, vm),
        scratch_shapes=[
            pltpu.VMEM((1, 1, 128), f32),
            pltpu.VMEM((GROUP, 1, 128), f32),
            pltpu.VMEM((1, 1, 128), f32),
            pltpu.VMEM((COLUMNS, 1, 128), f32),
            pltpu.SemaphoreType.DMA((GROUP,)),
            pltpu.SemaphoreType.DMA((GROUP,)),
            pltpu.SemaphoreType.DMA((COLUMNS,)),
            pltpu.SemaphoreType.DMA((COLUMNS,)),
        ],
        compiler_params=pltpu.CompilerParams(collective_id=0, has_side_effects=True),
        name="gossip",
    )(row)


def agenda_kernel(plan_ref, used_ref, total_ref, shift_ref, order_ref, goal_ref, origin_ref, row_ref):
    layer, _ = own_place()
    total = jnp.int32(0)
    for d in range(GROUP):
        shift_ref[total] = jnp.int32(d)
        total = total + jnp.where(used_ref[0, 32 + d] > 0, 1, 0)
    total_ref[0] = total
    mine = [((plan_ref[layer, 0, i] >> 6) - layer) & (GROUP - 1) for i in range(SLOTS)]
    for i in range(SLOTS):
        rank = jnp.int32(0)
        for k in range(SLOTS):
            if k != i:
                rank = rank + jnp.where(mine[k] <= mine[i] if k < i else mine[k] < mine[i], 1, 0)
        order_ref[rank] = jnp.int32(i)
        goal_ref[rank] = PACK * ((layer + mine[i]) & (GROUP - 1)) + (rank & (PACK - 1))

    def step(i, count):
        shift = shift_ref[i]
        source = (layer - shift) & (GROUP - 1)
        for k in range(SLOTS):
            value = plan_ref[source, 0, k]
            row_ref[count] = value & (SLOTS - 1)
            origin_ref[count] = PACK * source + (count & (PACK - 1))
            count = jnp.minimum(count + jnp.where((value >> 6) == layer, 1, 0), SLOTS)
        return count

    lax.fori_loop(0, total, step, jnp.int32(0))


def agenda(plan, used):
    sm = pl.BlockSpec(memory_space=pltpu.SMEM)
    sizes = (1, GROUP + 1, SLOTS, SLOTS, SLOTS + 1, SLOTS + 1)
    return pl.pallas_call(
        agenda_kernel,
        out_shape=tuple(jax.ShapeDtypeStruct((size,), jnp.int32) for size in sizes),
        in_specs=[sm] * 2,
        out_specs=(sm,) * len(sizes),
        name="agenda",
    )(plan, used)


def rotate_kernel(shift, sent_ref, got_ref, send_sem, recv_sem):
    layer, column = own_place()
    target, source = (layer + shift) & (GROUP - 1), (layer - shift) & (GROUP - 1)
    barrier = pltpu.get_barrier_semaphore()
    pl.semaphore_signal(barrier, inc=1, device_id=place(source, column), device_id_type=MESH_ID)
    pl.semaphore_wait(barrier, 1)
    copy = pltpu.make_async_remote_copy(
        src_ref=sent_ref,
        dst_ref=got_ref,
        send_sem=send_sem,
        recv_sem=recv_sem,
        device_id=place(target, column),
        device_id_type=MESH_ID,
    )
    copy.start()
    copy.wait()


def rotate(shift, packets):
    return pl.pallas_call(
        functools.partial(rotate_kernel, shift),
        out_shape=jax.ShapeDtypeStruct(packets.shape, packets.dtype),
        in_specs=[pl.BlockSpec(memory_space=pltpu.HBM)],
        out_specs=pl.BlockSpec(memory_space=pltpu.VMEM),
        scratch_shapes=[pltpu.SemaphoreType.DMA, pltpu.SemaphoreType.DMA],
        compiler_params=pltpu.CompilerParams(collective_id=shift, has_side_effects=True),
        name=f"rotate{shift}",
    )(packets)


def land_kernel(row_ref, *refs):
    held, out_ref, sems = refs[:-2], refs[-2], refs[-1]
    copies = []
    for k in range(SLOTS):
        copies.append(pltpu.make_async_copy(held[k // PACK].at[k % PACK], out_ref.at[row_ref[k]], sems.at[k]))
    for copy in copies:
        copy.start()
    for copy in copies:
        copy.wait()


def land(rows, held):
    vm, sm = pl.BlockSpec(memory_space=pltpu.VMEM), pl.BlockSpec(memory_space=pltpu.SMEM)
    return pl.pallas_call(
        land_kernel,
        out_shape=jax.ShapeDtypeStruct((SLOTS, 96, 256), jnp.float32),
        in_specs=[sm] + [vm] * len(held),
        out_specs=pl.BlockSpec(memory_space=pl.ANY),
        scratch_shapes=[pltpu.SemaphoreType.DMA((SLOTS,))],
        name="land",
    )(rows, *held)


def migrate(packets, total, shifts, goals, origins, rows):
    branches = [lambda pair: pair] + [functools.partial(rotate, d) for d in range(1, GROUP)]
    flows = SLOTS // PACK

    def few(packets):
        return tuple(
            lax.switch(shifts[f] - f, branches[f : GROUP - flows + 1 + f], packets[f]) for f in range(flows)
        )

    def many(packets):
        hits = goals[None, :] == jnp.arange(PACK * GROUP)[:, None]
        source = jnp.sum(jnp.where(hits, jnp.arange(SLOTS)[None, :], 0), axis=1)
        slots = jnp.take(jnp.concatenate(packets, axis=0), source, axis=0)
        arrived = lax.all_to_all(slots, RVE, split_axis=0, concat_axis=0, tiled=True)
        held = jnp.take(arrived, origins[:SLOTS], axis=0)
        return tuple(held[PACK * f : PACK * f + PACK] for f in range(flows))

    return land(rows, lax.cond(total == flows, few, many, packets))


def force_kernel(mean_ref, force_ref, got, send_sem, recv_sem):
    layer, column = own_place()
    barrier = pltpu.get_barrier_semaphore()
    steps = ((1, 0), (0, 1), (1, 1))
    for a, b in steps:
        source = place((layer - a) & (GROUP - 1), (column - b) & (COLUMNS - 1))
        pl.semaphore_signal(barrier, inc=1, device_id=source, device_id_type=MESH_ID)
    pl.semaphore_wait(barrier, len(steps))
    copies = [
        pltpu.make_async_remote_copy(
            src_ref=mean_ref,
            dst_ref=got.at[k],
            send_sem=send_sem.at[k],
            recv_sem=recv_sem.at[k],
            device_id=place((layer + a) & (GROUP - 1), (column + b) & (COLUMNS - 1)),
            device_id_type=MESH_ID,
        )
        for k, (a, b) in enumerate(steps)
    ]
    for copy in copies:
        copy.start()
    for copy in copies:
        copy.wait()
    t00 = mean_ref[...]
    zero = jnp.zeros_like(t00)
    t10 = jnp.where(layer > 0, got[0], zero)
    t01 = jnp.where(column > 0, got[1], zero)
    t11 = jnp.where((layer > 0) & (column > 0), got[2], zero)
    above = lax.broadcasted_iota(jnp.int32, (8, 128), 0) > 0
    lane = lax.broadcasted_iota(jnp.int32, (8, 128), 1)

    def lower(value):
        return jnp.where(above, pltpu.roll(value, 1, 0), zero)

    along_x = 0.25 * ((t10 + t11) - (t00 + t01))
    along_y = 0.25 * ((t01 + t11) - (t00 + t10))
    along_z = 0.25 * ((t00 + t10) + (t01 + t11))
    along_x, along_y, along_z = along_x + lower(along_x), along_y + lower(along_y), lower(along_z) - along_z
    out = zero
    for i, (p, q, r) in enumerate(((0, 5, 4), (5, 1, 3), (4, 3, 2))):
        value = along_x[:, p : p + 1] + along_y[:, q : q + 1] + along_z[:, r : r + 1]
        out = jnp.where(lane == i, value, out)
    force_ref[...] = out


def nodal_forces(means):
    vm = pl.BlockSpec(memory_space=pltpu.VMEM)
    return pl.pallas_call(
        force_kernel,
        out_shape=jax.ShapeDtypeStruct((8, 128), jnp.float32),
        in_specs=[vm],
        out_specs=vm,
        scratch_shapes=[
            pltpu.VMEM((3, 8, 128), jnp.float32),
            pltpu.SemaphoreType.DMA((3,)),
            pltpu.SemaphoreType.DMA((3,)),
        ],
        compiler_params=pltpu.CompilerParams(collective_id=GROUP, has_side_effects=True),
        name="forces",
    )(means)


def element_strain(extended):
    rows_y, depth = extended.shape[2] - 1, extended.shape[3]
    extended = jnp.pad(extended, ((0, 0), (0, 0), (0, 0), (0, 1)))
    gradient = [[0.0, 0.0, 0.0], [0.0, 0.0, 0.0], [0.0, 0.0, 0.0]]
    for shift_a in (0, 1):
        for shift_b in (0, 1):
            for shift_c in (0, 1):
                corner_values = extended[
                    :, shift_a : shift_a + 1, shift_b : shift_b + rows_y, shift_c : shift_c + depth
                ]
                signs = ((2 * shift_a - 1) / 4.0, (2 * shift_b - 1) / 4.0, (2 * shift_c - 1) / 4.0)
                for component in range(3):
                    for direction in range(3):
                        gradient[component][direction] = (
                            gradient[component][direction]
                            + corner_values[component] * signs[direction]
                        )
    strain_field = jnp.stack(
        [
            gradient[0][0],
            gradient[1][1],
            gradient[2][2],
            0.5 * (gradient[1][2] + gradient[2][1]),
            0.5 * (gradient[0][2] + gradient[2][0]),
            0.5 * (gradient[0][1] + gradient[1][0]),
        ],
        axis=0,
    )
    return strain_field.reshape(6, rows_y * depth).T


def on_device(
    displacement, plastic, bulk_modulus, shear_modulus, yield_radius, counts, migration_plan
):
    depth = displacement.shape[3]
    layer, column = own_place()
    shift = (migration_plan // (SLOTS * COLUMNS) - layer + GROUP) % GROUP
    seen = jnp.any(shift[:, None] == jnp.arange(GROUP)[None, :], axis=0)
    row = jnp.concatenate(
        [
            jnp.pad(migration_plan, (0, 24)).astype(jnp.float32),
            seen.astype(jnp.float32),
            jnp.pad(displacement.reshape(3 * depth), (0, 64 - 3 * depth)),
        ]
    )
    rows, columns, used = gossip(row.reshape(1, 1, 128))
    here = columns[:, 0, 64:].reshape(2, 2, 32)[:, :, : 3 * depth].reshape(2, 2, 3, depth)
    strain_rows = element_strain(jnp.transpose(here, (2, 1, 0, 3)))
    total, shifts, order, goals, origins, landing = agenda(rows, used)
    *packets, means = solve(
        order, plastic, strain_rows, counts, bulk_modulus, shear_modulus, yield_radius
    )
    force = nodal_forces(means)[:, :3].T.reshape(displacement.shape)
    moved = migrate(tuple(packets), total[0], shifts, goals, origins, landing)
    return (force, moved.reshape(plastic.shape))


def solution(mesh):
    finer = Mesh(
        mesh.devices.reshape(8, 4, mesh.shape["mic"], mesh.shape["mac"]),
        ("rve_0", "rve_1", "mic", "mac"),
    )
    placed = (
        P(None, RVE, ("mic", "mac"), None),
        P(RVE_MIC_MAC, None, None, None),
        P(),
        P(),
        P(),
        P(RVE_MIC_MAC),
        P(RVE_MIC_MAC),
    )
    return jax.shard_map(
        on_device,
        mesh=finer,
        in_specs=placed,
        out_specs=(P(None, RVE, ("mic", "mac"), None), P(RVE_MIC_MAC, None, None, None)),
        check_vma=False,
    )
```

```python
import functools
import math

import jax
import jax.numpy as jnp
import numpy as np
from jax import lax
from jax.experimental import pallas as pl
from jax.experimental.pallas import tpu as pltpu
from jax.sharding import Mesh
from jax.sharding import PartitionSpec as P

RVE = ("rve_0", "rve_1")
RVE_MIC_MAC = ("rve_0", "rve_1", "mic", "mac")


COUPLING = 0.7
PAIRS = ((0, 0), (1, 1), (2, 2), (1, 2), (0, 2), (0, 1))


def transform_tables(n):
    plane = np.arange(n * n)
    b, c = plane // n, plane % n
    angle = 2.0 * np.pi / n * ((np.outer(b, b) + np.outer(c, c)) % n)
    table = np.concatenate([np.cos(angle), np.sin(angle)], axis=1).astype(np.float32)
    high = table.astype(jnp.bfloat16)
    low = (table - high.astype(np.float32)).astype(jnp.bfloat16)
    return np.concatenate([high, low], axis=0)


def green_table(n):
    index = np.stack(np.meshgrid(np.arange(n), np.arange(n), np.arange(n), indexing="ij"))

    def operator(i):
        k = ((i + n // 2) % n - n // 2).astype(np.float64)
        q = np.sum(k * k, axis=0)
        safe = np.maximum(q, 1.0)
        rows = []
        for m, r in PAIRS:
            row = []
            for p, s in PAIRS:
                eye = lambda u, v: 1.0 if u == v else 0.0
                first = (
                    eye(m, p) * k[r] * k[s] + eye(m, s) * k[r] * k[p] + eye(r, p) * k[m] * k[s] + eye(r, s) * k[m] * k[p]
                ) / (4.0 * safe)
                row.append(first - COUPLING * k[m] * k[r] * k[p] * k[s] / (safe * safe))
            rows.append(row)
        return np.where(q > 0, np.array(rows), 0.0)

    even = 0.5 * (operator(index) + operator((-index) % n)) / float(n**3)
    even = even[:, :, : n // 2 + 1]
    rows = [even[i, j].reshape(n // 2 + 1, n * n) for i in range(6) for j in range(i, 6)]
    table = np.stack(rows, axis=1).reshape(-1, n * n).astype(np.float32)
    return np.pad(table, ((0, -table.shape[0] % 8), (0, 0)))


def turn(k, n, value, sign):
    re, im = value
    if k == 0:
        return value
    if 4 * k == n:
        return (im, -re) if sign < 0 else (-im, re)
    if 8 * k == n:
        r = math.sqrt(0.5)
        return ((re + im) * r, (im - re) * r) if sign < 0 else ((re - im) * r, (re + im) * r)
    c, s = math.cos(2 * math.pi * k / n), sign * math.sin(2 * math.pi * k / n)
    return (re * c - im * s, re * s + im * c)


def real_forward(x):
    n = len(x)
    if n == 2:
        return [(x[0] + x[1], None), (x[0] - x[1], None)]
    even, odd = real_forward(x[0::2]), real_forward(x[1::2])
    out = [None] * (n // 2 + 1)
    out[0] = (even[0][0] + odd[0][0], None)
    out[n // 2] = (even[0][0] - odd[0][0], None)
    for k in range(1, n // 4 + 1):
        if 4 * k == n:
            out[k] = (even[k][0], -odd[k][0])
        else:
            t = turn(k, n, odd[k], -1)
            out[k] = (even[k][0] + t[0], even[k][1] + t[1])
            out[n // 2 - k] = (even[k][0] - t[0], t[1] - even[k][1])
    return out


def real_backward(y):
    n = 2 * (len(y) - 1)
    if n == 2:
        return [y[0][0] + y[1][0], y[0][0] - y[1][0]]
    even, odd = [None] * (n // 4 + 1), [None] * (n // 4 + 1)
    even[0] = (y[0][0] + y[n // 2][0], None)
    odd[0] = (y[0][0] - y[n // 2][0], None)
    for k in range(1, n // 4 + 1):
        if 4 * k == n:
            even[k] = (2.0 * y[k][0], None)
            odd[k] = (-2.0 * y[k][1], None)
        else:
            o = y[n // 2 - k]
            even[k] = (y[k][0] + o[0], y[k][1] - o[1])
            odd[k] = turn(k, n, (y[k][0] - o[0], y[k][1] + o[1]), 1)
    out = [None] * n
    out[0::2] = real_backward(even)
    out[1::2] = real_backward(odd)
    return out


def flow_rule(elastic, shear2, radius):
    volume = elastic[0] + elastic[1] + elastic[2]
    mean = volume * (1.0 / 3.0)
    deviator = [elastic[i] - mean for i in range(3)] + list(elastic[3:])
    trial = [shear2 * d for d in deviator]
    normal = trial[0] * trial[0] + trial[1] * trial[1] + trial[2] * trial[2]
    mixed = trial[3] * trial[3] + trial[4] * trial[4] + trial[5] * trial[5]
    squared = normal + (mixed + mixed)
    factor = radius * lax.rsqrt(jnp.maximum(squared, radius * radius))
    return volume, deviator, trial, factor


HALVES = (slice(0, 128), slice(128, 256))


def step_kernel(
    plan_ref, nodes_ref, counts_ref, plastic_ref, bulk_ref, shear_ref, radius_ref, dft_hbm, green_hbm,
    rows_ref, used_ref, force_ref, updated_ref,
    row_s, group_s, second_s, across_s, group_sem, across_sem, tile_s, nodes_s, means_s, below_s, nodes_sem, below_sem,
    halves_s, copy_sem, dft_ref, green_ref, table_sem, material_s, green_s, plastic_s,
    strain_s, stress_s, update_s, mapped_s, left_s, product_s, left2_s, product2_s,
):
    f32, bf16 = jnp.float32, jnp.bfloat16
    i32 = jnp.int32
    layer, column = own_place()
    incoming = [
        pltpu.make_async_copy(plastic_ref.at[:, lanes], halves_s.at[h], copy_sem.at[h]) for h, lanes in enumerate(HALVES)
    ]
    tables = [
        pltpu.make_async_copy(green_hbm, green_ref, table_sem.at[0]),
        pltpu.make_async_copy(dft_hbm.at[:256], dft_ref.at[:256], table_sem.at[1]),
        pltpu.make_async_copy(dft_hbm, dft_ref.at[256:], table_sem.at[2]),
    ]
    for copy in incoming + tables:
        copy.start()
    barrier = pltpu.get_barrier_semaphore()

    def greet(layers, columns):
        peer = place((layer + layers) & (GROUP - 1), (column + columns) & (COLUMNS - 1))
        pl.semaphore_signal(barrier, inc=1, device_id=peer, device_id_type=MESH_ID)

    pl.loop(1, GROUP)(lambda step: greet(step, 0))
    pl.loop(1, COLUMNS)(lambda step: greet(0, step))
    greet(1, 1)
    greet(-1, -1)

    lane = lax.broadcasted_iota(i32, (1, 128), 1)
    sublane = lax.broadcasted_iota(i32, (8, 128), 0)
    lanes8 = lax.broadcasted_iota(i32, (8, 128), 1)
    plan = [plan_ref[i] for i in range(SLOTS)]
    mine = [((value >> 6) - layer) & (GROUP - 1) for value in plan]
    row = jnp.zeros((1, 128), i32)
    counts = jnp.zeros((8, 128), i32)
    tile = jnp.zeros((8, 128), f32)
    for i in range(SLOTS):
        row = jnp.where(lane == i, plan[i], row)
        row = jnp.where(lane == 32 + mine[i], 1, row)
        counts = jnp.where(sublane == i, counts_ref[i], counts)
        for m in range(3):
            tile = jnp.where((sublane == i) & (lanes8 == m), nodes_ref[m, 0, 0, i], tile)
    row_s[0] = row
    tile_s[...] = tile
    for a in range(16):
        shear2 = 2.0 * shear_ref[a : a + 1, :]
        for i, value in enumerate((shear2, bulk_ref[a : a + 1, :], radius_ref[a : a + 1, :])):
            material_s[a, i] = jnp.broadcast_to(value, (8, 256))

    pl.semaphore_wait(barrier, GROUP + COLUMNS)

    def to(layers, columns):
        return place((layer + layers) & (GROUP - 1), (column + columns) & (COLUMNS - 1))

    def halo(src, dst, sems, sign):
        return [
            pltpu.make_async_remote_copy(
                src_ref=src, dst_ref=dst.at[k], send_sem=sems.at[0, k], recv_sem=sems.at[1, k],
                device_id=to(sign * x, sign * y), device_id_type=MESH_ID,
            )
            for k, (x, y) in enumerate(((1, 0), (0, 1), (1, 1)))
        ]

    def to_layer(step):
        return pltpu.make_async_remote_copy(
            src_ref=row_s.at[0], dst_ref=group_s.at[layer], send_sem=group_sem.at[0, step],
            recv_sem=group_sem.at[1, step], device_id=to(step, 0), device_id_type=MESH_ID,
        )

    def to_column(step):
        return pltpu.make_async_remote_copy(
            src_ref=second_s.at[0], dst_ref=across_s.at[column], send_sem=across_sem.at[0, step],
            recv_sem=across_sem.at[1, step], device_id=to(0, step), device_id_type=MESH_ID,
        )

    nodes_halo = halo(tile_s, nodes_s, nodes_sem, -1)
    for copy in nodes_halo:
        copy.start()
    pl.loop(1, GROUP)(lambda step: to_layer(step).start())
    group_s[layer] = row

    for copy in incoming:
        copy.wait()

    @pl.loop(0, 96, unroll=4)
    def _(row):
        for h, lanes in enumerate(HALVES):
            plastic_s[row, :, lanes] = halves_s[h, pl.ds(row, 8, stride=96), :]

    for copy in nodes_halo:
        copy.wait()
    zero = jnp.zeros((8, 128), f32)

    def gradients(t00, t10, t01, t11, shift):
        along_x = 0.25 * ((t10 + t11) - (t00 + t01))
        along_y = 0.25 * ((t01 + t11) - (t00 + t10))
        along_z = 0.25 * ((t00 + t10) + (t01 + t11))
        return along_x + shift(along_x), along_y + shift(along_y), shift(along_z) - along_z

    inner_x, inner_y = layer < GROUP - 1, column < COLUMNS - 1
    by_x, by_y, by_z = gradients(
        tile,
        jnp.where(inner_x, nodes_s[0], zero),
        jnp.where(inner_y, nodes_s[1], zero),
        jnp.where(inner_x & inner_y, nodes_s[2], zero),
        lambda value: jnp.where(sublane < 7, pltpu.roll(value, 7, 0), zero),
    )
    macro = [
        by_x[:, 0:1],
        by_y[:, 1:2],
        by_z[:, 2:3],
        0.5 * (by_z[:, 1:2] + by_y[:, 2:3]),
        0.5 * (by_z[:, 0:1] + by_x[:, 2:3]),
        0.5 * (by_y[:, 0:1] + by_x[:, 1:2]),
    ]
    for c in range(6):
        start = jnp.broadcast_to(macro[c], (8, 256))

        @pl.loop(0, 16)
        def _(a):
            strain_s[c * 16 + a] = start

    def split(value):
        high = value.astype(bf16)
        low = (value - high.astype(f32)).astype(bf16)
        return high, low

    def polarization(step):
        @pl.loop(0, 16)
        def _(a):
            for lanes in HALVES:
                shear2 = material_s[a, 0, :, lanes]
                bulk = material_s[a, 1, :, lanes]
                radius = material_s[a, 2, :, lanes]
                elastic = [strain_s[c * 16 + a, :, lanes] - plastic_s[c * 16 + a, :, lanes] for c in range(6)]
                volume, _, trial, factor = flow_rule(elastic, shear2, radius)
                pressure = bulk * volume
                for c in range(6):
                    value = factor * trial[c]
                    stress_s[c * 16 + a, :, lanes] = value + pressure if c < 3 else value

        @pl.loop(0, 3)
        def _(pair):
            for lanes in HALVES:
                sets = []
                for half in range(2):
                    y = real_forward([stress_s[pair * 32 + half * 16 + a, :, lanes] for a in range(16)])
                    sets.append([y[0][0], y[8][0]] + [part for k in range(1, 8) for part in y[k]])
                rows = pl.ds(pl.multiple_of(pair * 16, 16), 16)
                for r in range(16):
                    high, low = split(jnp.concatenate([sets[0][r], sets[1][r]], axis=0))
                    left_s[r, rows, lanes] = high
                    left_s[r, rows, slice(256 + lanes.start, 256 + lanes.stop)] = low

        @pl.when(step == 0)
        def _():
            tables[1].wait()
            tables[2].wait()
            tables[0].wait()

            @pl.loop(0, 24)
            def _(block):
                rows = green_ref[pl.ds(pl.multiple_of(block * 8, 8), 8), :]
                for r in range(8):
                    green_s[block * 8 + r] = jnp.broadcast_to(rows[r : r + 1, :], (8, 256))

        left = left_s[...].reshape(768, 512)
        product_s[...] = jnp.dot(
            jnp.concatenate([left, left[:, :256]], axis=1), dft_ref[...], preferred_element_type=f32
        ).reshape(16, 48, 512)

        def operate(k, re, im, lanes):
            for t, value in ((2 * k, re), (2 * k + 1, im)):
                value = value[:3] + [v + v for v in value[3:]]
                out = [None] * 6
                j = 0
                for i in range(6):
                    for m in range(i, 6):
                        g = green_s[k * 21 + j, :, lanes]
                        j += 1
                        out[i] = g * value[m] if out[i] is None else out[i] + g * value[m]
                        if m != i:
                            out[m] = g * value[i] if out[m] is None else out[m] + g * value[i]
                for pair in range(3):
                    high, low = split(jnp.concatenate([out[2 * pair], out[2 * pair + 1]], axis=0))
                    left2_s[t, slice(pair * 16, pair * 16 + 16), lanes] = high
                    left2_s[t, slice(pair * 16, pair * 16 + 16), slice(256 + lanes.start, 256 + lanes.stop)] = low

        for k, row in ((0, 0), (8, 1)):
            for lanes in HALVES:
                wide = slice(256 + lanes.start, 256 + lanes.stop)
                re = [product_s[row, slice(c * 8, c * 8 + 8), lanes] for c in range(6)]
                im = [-product_s[row, slice(c * 8, c * 8 + 8), wide] for c in range(6)]
                operate(k, re, im, lanes)

        @pl.loop(1, 8)
        def _(k):
            for lanes in HALVES:
                wide = slice(256 + lanes.start, 256 + lanes.stop)
                re, im = [], []
                for c in range(6):
                    rows = slice(c * 8, c * 8 + 8)
                    re.append(product_s[2 * k, rows, lanes] + product_s[2 * k + 1, rows, wide])
                    im.append(product_s[2 * k + 1, rows, lanes] - product_s[2 * k, rows, wide])
                operate(k, re, im, lanes)

        left2 = left2_s[...].reshape(864, 512)
        product2_s[...] = jnp.dot(
            jnp.concatenate([left2, left2[:, :256]], axis=1), dft_ref[...], preferred_element_type=f32
        ).reshape(18, 48, 512)

    def update_of(c, lanes):
        wide = slice(256 + lanes.start, 256 + lanes.stop)
        rows = pl.ds(pl.multiple_of(c * 8, 8), 8)
        y = []
        for k in range(9):
            re = product2_s[2 * k, rows, lanes] - product2_s[2 * k + 1, rows, wide]
            im = None if k in (0, 8) else product2_s[2 * k, rows, wide] + product2_s[2 * k + 1, rows, lanes]
            y.append((re, im))
        return real_backward(y)

    @pl.loop(0, 96, unroll=4)
    def _(row):
        update_s[row] = jnp.zeros((8, 256), f32)
        mapped_s[row] = strain_s[row]

    @pl.loop(0, 3)
    def _(step):
        polarization(step)

        @pl.when(step == 1)
        def _():
            pl.loop(1, GROUP)(lambda peer: to_layer(peer).wait())
            union = group_s[0]
            for i in range(1, GROUP):
                union = jnp.maximum(union, group_s[i])
            second_s[0] = union
            across_s[column] = union
            pl.loop(1, COLUMNS)(lambda peer: to_column(peer).start())

        zero = jnp.zeros((8, 128), f32)

        def gather(c, carry):
            numerator, denominator = carry
            for lanes in HALVES:
                update = update_of(c, lanes)
                for a in range(16):
                    change = update[a] - update_s[c * 16 + a, :, lanes]
                    numerator = numerator + change * update[a]
                    denominator = denominator + change * change
                    update_s[c * 16 + a, :, lanes] = update[a]
            return numerator, denominator

        numerator, denominator = lax.fori_loop(0, 6, gather, (zero, zero))
        scale = 1.0 / float(6 * 16**3)
        numerator = jnp.sum(numerator, axis=1, keepdims=True) * scale
        denominator = jnp.sum(denominator, axis=1, keepdims=True) * scale + 1e-06
        weight = jnp.broadcast_to(jnp.where(step > 0, numerator / denominator, 0.0), (8, 256))
        active = step < jnp.concatenate([counts, counts], axis=1)

        @pl.loop(0, 96, unroll=4)
        def _(row):
            strain = strain_s[row]
            mapped = strain - update_s[row]
            candidate = mapped - weight * (mapped - mapped_s[row])
            mapped_s[row] = mapped
            strain_s[row] = jnp.where(active, candidate, strain)

    def finish(a, sums):
        sums = list(sums)
        for lanes in HALVES:
            shear2 = material_s[a, 0, :, lanes]
            bulk = material_s[a, 1, :, lanes]
            radius = material_s[a, 2, :, lanes]
            plastic = [plastic_s[c * 16 + a, :, lanes] for c in range(6)]
            elastic = [strain_s[c * 16 + a, :, lanes] - plastic[c] for c in range(6)]
            volume, deviator, trial, factor = flow_rule(elastic, shear2, radius)
            pressure = bulk * volume
            for c in range(6):
                value = factor * trial[c]
                sums[c] = sums[c] + (value + pressure if c < 3 else value)
                plastic_s[c * 16 + a, :, lanes] = plastic[c] + (deviator[c] - factor * deviator[c])
        return tuple(sums)

    sums = lax.fori_loop(0, 16, finish, (zero,) * 6)
    means = zero
    for c in range(6):
        means = jnp.where(lanes8 == c, jnp.sum(sums[c], axis=1, keepdims=True) * (1.0 / 4096.0), means)
    means_s[...] = means
    stress_halo = halo(means_s, below_s, below_sem, 1)
    for copy in stress_halo:
        copy.start()

    @pl.loop(0, 96, unroll=4)
    def _(row):
        for h, lanes in enumerate(HALVES):
            updated_ref[h, pl.ds(row, 8, stride=96), :] = plastic_s[row, :, lanes]

    for copy in stress_halo:
        copy.wait()
    inner_x, inner_y = layer > 0, column > 0
    by_x, by_y, by_z = gradients(
        means,
        jnp.where(inner_x, below_s[0], zero),
        jnp.where(inner_y, below_s[1], zero),
        jnp.where(inner_x & inner_y, below_s[2], zero),
        lambda value: jnp.where(sublane > 0, pltpu.roll(value, 1, 0), zero),
    )
    force = zero
    for i, (p, q, r) in enumerate(((0, 5, 4), (5, 1, 3), (4, 3, 2))):
        value = by_x[:, p : p + 1] + by_y[:, q : q + 1] + by_z[:, r : r + 1]
        force = jnp.where(lanes8 == i, value, force)
    force_ref[...] = force
    pl.loop(1, COLUMNS)(lambda peer: to_column(peer).wait())
    used = across_s[0]
    for i in range(1, COLUMNS):
        used = jnp.maximum(used, across_s[i])
    used_ref[...] = used
    rows_ref[...] = group_s[...]


def solve(plan, nodes, counts, plastic, bulk, shear, radius):
    f32, bf16, i32 = jnp.float32, jnp.bfloat16, jnp.int32
    vm, sm = pl.BlockSpec(memory_space=pltpu.VMEM), pl.BlockSpec(memory_space=pltpu.SMEM)
    anywhere = pl.BlockSpec(memory_space=pltpu.HBM)
    return pl.pallas_call(
        step_kernel,
        out_shape=(
            jax.ShapeDtypeStruct((GROUP, 1, 128), i32),
            jax.ShapeDtypeStruct((1, 128), i32),
            jax.ShapeDtypeStruct((8, 128), f32),
            jax.ShapeDtypeStruct((2, 768, 128), f32),
        ),
        in_specs=[sm] * 3 + [anywhere] + [vm] * 3 + [anywhere] * 2,
        out_specs=(vm,) * 4,
        scratch_shapes=[
            pltpu.VMEM((1, 1, 128), i32),
            pltpu.VMEM((GROUP, 1, 128), i32),
            pltpu.VMEM((1, 1, 128), i32),
            pltpu.VMEM((COLUMNS, 1, 128), i32),
            pltpu.SemaphoreType.DMA((2, GROUP)),
            pltpu.SemaphoreType.DMA((2, COLUMNS)),
            pltpu.VMEM((8, 128), f32),
            pltpu.VMEM((3, 8, 128), f32),
            pltpu.VMEM((8, 128), f32),
            pltpu.VMEM((3, 8, 128), f32),
            pltpu.SemaphoreType.DMA((2, 3)),
            pltpu.SemaphoreType.DMA((2, 3)),
            pltpu.VMEM((2, 768, 128), f32),
            pltpu.SemaphoreType.DMA((2,)),
            pltpu.VMEM((768, 512), bf16),
            pltpu.VMEM((192, 256), f32),
            pltpu.SemaphoreType.DMA((3,)),
            pltpu.VMEM((16, 3, 8, 256), f32),
            pltpu.VMEM((192, 8, 256), f32),
            pltpu.VMEM((96, 8, 256), f32),
            pltpu.VMEM((96, 8, 256), f32),
            pltpu.VMEM((96, 8, 256), f32),
            pltpu.VMEM((96, 8, 256), f32),
            pltpu.VMEM((96, 8, 256), f32),
            pltpu.VMEM((16, 48, 512), bf16),
            pltpu.VMEM((16, 48, 512), f32),
            pltpu.VMEM((18, 48, 512), bf16),
            pltpu.VMEM((18, 48, 512), f32),
        ],
        compiler_params=pltpu.CompilerParams(
            collective_id=0, has_side_effects=True, vmem_limit_bytes=60 << 20
        ),
        name="step",
    )(
        plan,
        nodes,
        counts,
        plastic.reshape(768, 256),
        bulk,
        shear,
        radius,
        jnp.asarray(transform_tables(16)),
        jnp.asarray(green_table(16)),
    )


MESH_ID = pl.DeviceIdType.MESH
GROUP, COLUMNS, SLOTS, PACK = 32, 8, 8, 2


def place(layer, column):
    return {"rve_0": layer // 4, "rve_1": layer % 4, "mic": column // 2, "mac": column % 2}


def own_place():
    layer = lax.axis_index("rve_0") * 4 + lax.axis_index("rve_1")
    return layer, lax.axis_index("mic") * 2 + lax.axis_index("mac")


def agenda_kernel(
    plan_ref, used_ref, updated_ref, total_ref, shift_ref, goal_ref, origin_ref, row_ref, *packets_and_sems
):
    layer, _ = own_place()
    packets, sems = packets_and_sems[:-1], packets_and_sems[-1]
    mine = [((plan_ref[layer, 0, i] >> 6) - layer) & (GROUP - 1) for i in range(SLOTS)]
    order_rank = []
    for i in range(SLOTS):
        rank = jnp.int32(0)
        for k in range(SLOTS):
            if k != i:
                rank = rank + jnp.where(mine[k] <= mine[i] if k < i else mine[k] < mine[i], 1, 0)
        goal_ref[rank] = PACK * ((layer + mine[i]) & (GROUP - 1)) + (rank & (PACK - 1))
        order_rank.append(rank)
    copies = []
    for k in range(SLOTS):
        index = jnp.int32(0)
        for i in range(SLOTS):
            index = jnp.where(order_rank[i] == k, i, index)
        rows = pl.ds(pl.multiple_of(index * 96, 96), 96)
        for h, lanes in enumerate(HALVES):
            copies.append(
                pltpu.make_async_copy(
                    updated_ref.at[h, rows], packets[k // PACK].at[k % PACK, :, lanes], sems.at[2 * k + h]
                )
            )
    for copy in copies:
        copy.start()
    total = jnp.int32(0)
    for d in range(GROUP):
        shift_ref[total] = jnp.int32(d)
        total = total + jnp.where(used_ref[0, 32 + d] > 0, 1, 0)
    total_ref[0] = total

    def step(i, count):
        shift = shift_ref[i]
        source = (layer - shift) & (GROUP - 1)
        for k in range(SLOTS):
            value = plan_ref[source, 0, k]
            row_ref[count] = value & (SLOTS - 1)
            origin_ref[count] = PACK * source + (count & (PACK - 1))
            count = jnp.minimum(count + jnp.where((value >> 6) == layer, 1, 0), SLOTS)
        return count

    lax.fori_loop(0, total, step, jnp.int32(0))
    for copy in copies:
        copy.wait()


def agenda(plan, used, updated):
    sm, vm = pl.BlockSpec(memory_space=pltpu.SMEM), pl.BlockSpec(memory_space=pltpu.VMEM)
    pair = jax.ShapeDtypeStruct((PACK, 96, 256), jnp.float32)
    flows = SLOTS // PACK
    sizes = (1, GROUP + 1, SLOTS, SLOTS + 1, SLOTS + 1)
    return pl.pallas_call(
        agenda_kernel,
        out_shape=tuple(jax.ShapeDtypeStruct((size,), jnp.int32) for size in sizes) + (pair,) * flows,
        in_specs=[sm, sm, vm],
        out_specs=(sm,) * len(sizes) + (pl.BlockSpec(memory_space=pltpu.HBM),) * flows,
        scratch_shapes=[pltpu.SemaphoreType.DMA((2 * SLOTS,))],
        name="agenda",
    )(plan, used, updated)


def rotate_kernel(shift, sent_ref, got_ref, send_sem, recv_sem):
    layer, column = own_place()
    target, source = (layer + shift) & (GROUP - 1), (layer - shift) & (GROUP - 1)
    barrier = pltpu.get_barrier_semaphore()
    pl.semaphore_signal(barrier, inc=1, device_id=place(source, column), device_id_type=MESH_ID)
    pl.semaphore_wait(barrier, 1)
    copy = pltpu.make_async_remote_copy(
        src_ref=sent_ref,
        dst_ref=got_ref,
        send_sem=send_sem,
        recv_sem=recv_sem,
        device_id=place(target, column),
        device_id_type=MESH_ID,
    )
    copy.start()
    copy.wait()


def rotate(shift, packets):
    return pl.pallas_call(
        functools.partial(rotate_kernel, shift),
        out_shape=jax.ShapeDtypeStruct(packets.shape, packets.dtype),
        in_specs=[pl.BlockSpec(memory_space=pltpu.HBM)],
        out_specs=pl.BlockSpec(memory_space=pltpu.VMEM),
        scratch_shapes=[pltpu.SemaphoreType.DMA, pltpu.SemaphoreType.DMA],
        compiler_params=pltpu.CompilerParams(collective_id=shift, has_side_effects=True),
        name=f"rotate{shift}",
    )(packets)


def land_kernel(row_ref, *refs):
    held, out_ref, sems = refs[:-2], refs[-2], refs[-1]
    copies = []
    for k in range(SLOTS):
        copies.append(pltpu.make_async_copy(held[k // PACK].at[k % PACK], out_ref.at[row_ref[k]], sems.at[k]))
    for copy in copies:
        copy.start()
    for copy in copies:
        copy.wait()


def land(rows, held):
    vm, sm = pl.BlockSpec(memory_space=pltpu.VMEM), pl.BlockSpec(memory_space=pltpu.SMEM)
    return pl.pallas_call(
        land_kernel,
        out_shape=jax.ShapeDtypeStruct((SLOTS, 96, 256), jnp.float32),
        in_specs=[sm] + [vm] * len(held),
        out_specs=pl.BlockSpec(memory_space=pl.ANY),
        scratch_shapes=[pltpu.SemaphoreType.DMA((SLOTS,))],
        name="land",
    )(rows, *held)


def migrate(packets, total, shifts, goals, origins, rows):
    branches = [lambda pair: pair] + [functools.partial(rotate, d) for d in range(1, GROUP)]
    flows = SLOTS // PACK

    def few(packets):
        return tuple(
            lax.switch(shifts[f] - f, branches[f : GROUP - flows + 1 + f], packets[f]) for f in range(flows)
        )

    def many(packets):
        hits = goals[None, :] == jnp.arange(PACK * GROUP)[:, None]
        source = jnp.sum(jnp.where(hits, jnp.arange(SLOTS)[None, :], 0), axis=1)
        slots = jnp.take(jnp.concatenate(packets, axis=0), source, axis=0)
        arrived = lax.all_to_all(slots, RVE, split_axis=0, concat_axis=0, tiled=True)
        held = jnp.take(arrived, origins[:SLOTS], axis=0)
        return tuple(held[PACK * f : PACK * f + PACK] for f in range(flows))

    return land(rows, lax.cond(total == flows, few, many, packets))


def on_device(
    displacement, plastic, bulk_modulus, shear_modulus, yield_radius, counts, migration_plan
):
    plans, used, force, updated = solve(
        migration_plan, displacement, counts, plastic, bulk_modulus, shear_modulus, yield_radius
    )
    total, shifts, goals, origins, landing, *packets = agenda(plans, used, updated)
    force = force[:, :3].T.reshape(displacement.shape)
    moved = migrate(tuple(packets), total[0], shifts, goals, origins, landing)
    return (force, moved.reshape(plastic.shape))


def solution(mesh):
    finer = Mesh(
        mesh.devices.reshape(8, 4, mesh.shape["mic"], mesh.shape["mac"]),
        ("rve_0", "rve_1", "mic", "mac"),
    )
    placed = (
        P(None, RVE, ("mic", "mac"), None),
        P(RVE_MIC_MAC, None, None, None),
        P(),
        P(),
        P(),
        P(RVE_MIC_MAC),
        P(RVE_MIC_MAC),
    )
    return jax.shard_map(
        on_device,
        mesh=finer,
        in_specs=placed,
        out_specs=(P(None, RVE, ("mic", "mac"), None), P(RVE_MIC_MAC, None, None, None)),
        check_vma=False,
    )
```

```python
import functools
import math

import jax
import jax.numpy as jnp
import numpy as np
from jax import lax
from jax.experimental import pallas as pl
from jax.experimental.pallas import tpu as pltpu
from jax.sharding import Mesh
from jax.sharding import PartitionSpec as P

RVE = ("rve_0", "rve_1")
RVE_MIC_MAC = ("rve_0", "rve_1", "mic", "mac")


COUPLING = 0.7
PAIRS = ((0, 0), (1, 1), (2, 2), (1, 2), (0, 2), (0, 1))


def transform_tables(n):
    plane = np.arange(n * n)
    b, c = plane // n, plane % n
    angle = 2.0 * np.pi / n * ((np.outer(b, b) + np.outer(c, c)) % n)
    table = np.concatenate([np.cos(angle), np.sin(angle)], axis=1).astype(np.float32)
    high = table.astype(jnp.bfloat16)
    low = (table - high.astype(np.float32)).astype(jnp.bfloat16)
    return np.concatenate([high, low], axis=0)


def green_table(n):
    index = np.stack(np.meshgrid(np.arange(n), np.arange(n), np.arange(n), indexing="ij"))

    def operator(i):
        k = ((i + n // 2) % n - n // 2).astype(np.float64)
        q = np.sum(k * k, axis=0)
        safe = np.maximum(q, 1.0)
        rows = []
        for m, r in PAIRS:
            row = []
            for p, s in PAIRS:
                eye = lambda u, v: 1.0 if u == v else 0.0
                first = (
                    eye(m, p) * k[r] * k[s] + eye(m, s) * k[r] * k[p] + eye(r, p) * k[m] * k[s] + eye(r, s) * k[m] * k[p]
                ) / (4.0 * safe)
                row.append(first - COUPLING * k[m] * k[r] * k[p] * k[s] / (safe * safe))
            rows.append(row)
        return np.where(q > 0, np.array(rows), 0.0)

    even = 0.5 * (operator(index) + operator((-index) % n)) / float(n**3)
    even = even[:, :, : n // 2 + 1]
    rows = [even[i, j].reshape(n // 2 + 1, n * n) for i in range(6) for j in range(i, 6)]
    table = np.stack(rows, axis=1).reshape(-1, n * n).astype(np.float32)
    return np.pad(table, ((0, -table.shape[0] % 8), (0, 0)))


def turn(k, n, value, sign):
    re, im = value
    if k == 0:
        return value
    if 4 * k == n:
        return (im, -re) if sign < 0 else (-im, re)
    if 8 * k == n:
        r = math.sqrt(0.5)
        return ((re + im) * r, (im - re) * r) if sign < 0 else ((re - im) * r, (re + im) * r)
    c, s = math.cos(2 * math.pi * k / n), sign * math.sin(2 * math.pi * k / n)
    return (re * c - im * s, re * s + im * c)


def real_forward(x):
    n = len(x)
    if n == 2:
        return [(x[0] + x[1], None), (x[0] - x[1], None)]
    even, odd = real_forward(x[0::2]), real_forward(x[1::2])
    out = [None] * (n // 2 + 1)
    out[0] = (even[0][0] + odd[0][0], None)
    out[n // 2] = (even[0][0] - odd[0][0], None)
    for k in range(1, n // 4 + 1):
        if 4 * k == n:
            out[k] = (even[k][0], -odd[k][0])
        else:
            t = turn(k, n, odd[k], -1)
            out[k] = (even[k][0] + t[0], even[k][1] + t[1])
            out[n // 2 - k] = (even[k][0] - t[0], t[1] - even[k][1])
    return out


def real_backward(y):
    n = 2 * (len(y) - 1)
    if n == 2:
        return [y[0][0] + y[1][0], y[0][0] - y[1][0]]
    even, odd = [None] * (n // 4 + 1), [None] * (n // 4 + 1)
    even[0] = (y[0][0] + y[n // 2][0], None)
    odd[0] = (y[0][0] - y[n // 2][0], None)
    for k in range(1, n // 4 + 1):
        if 4 * k == n:
            even[k] = (2.0 * y[k][0], None)
            odd[k] = (-2.0 * y[k][1], None)
        else:
            o = y[n // 2 - k]
            even[k] = (y[k][0] + o[0], y[k][1] - o[1])
            odd[k] = turn(k, n, (y[k][0] - o[0], y[k][1] + o[1]), 1)
    out = [None] * n
    out[0::2] = real_backward(even)
    out[1::2] = real_backward(odd)
    return out


def flow_rule(elastic, shear2, radius):
    volume = elastic[0] + elastic[1] + elastic[2]
    mean = volume * (1.0 / 3.0)
    deviator = [elastic[i] - mean for i in range(3)] + list(elastic[3:])
    trial = [shear2 * d for d in deviator]
    normal = trial[0] * trial[0] + trial[1] * trial[1] + trial[2] * trial[2]
    mixed = trial[3] * trial[3] + trial[4] * trial[4] + trial[5] * trial[5]
    squared = normal + (mixed + mixed)
    factor = radius * lax.rsqrt(jnp.maximum(squared, radius * radius))
    return volume, deviator, trial, factor


HALVES = (slice(0, 128), slice(128, 256))


def step_kernel(
    plan_ref, nodes_ref, counts_ref, plastic_ref, bulk_ref, shear_ref, radius_ref, dft_hbm, green_hbm,
    rows_ref, used_ref, force_ref, updated_ref,
    row_s, group_s, second_s, across_s, group_sem, across_sem, tile_s, nodes_s, means_s, below_s, nodes_sem, below_sem,
    halves_s, copy_sem, dft_ref, green_ref, table_sem, material_s, green_s, plastic_s,
    strain_s, stress_s, update_s, mapped_s, left_s, product_s, left2_s, product2_s,
):
    f32, bf16 = jnp.float32, jnp.bfloat16
    i32 = jnp.int32
    layer, column = own_place()
    incoming = [
        pltpu.make_async_copy(plastic_ref.at[:, lanes], halves_s.at[h], copy_sem.at[h]) for h, lanes in enumerate(HALVES)
    ]
    tables = [
        pltpu.make_async_copy(green_hbm, green_ref, table_sem.at[0]),
        pltpu.make_async_copy(dft_hbm.at[:256], dft_ref.at[:256], table_sem.at[1]),
        pltpu.make_async_copy(dft_hbm, dft_ref.at[256:], table_sem.at[2]),
    ]
    for copy in incoming + tables:
        copy.start()
    barrier = pltpu.get_barrier_semaphore()

    def greet(layers, columns):
        peer = place((layer + layers) & (GROUP - 1), (column + columns) & (COLUMNS - 1))
        pl.semaphore_signal(barrier, inc=1, device_id=peer, device_id_type=MESH_ID)

    z, x = layer // 4, layer % 4

    def at_x(step):
        return z * 4 + ((x + step) & 3)

    for step in range(1, 4):
        peer = place(at_x(step), column)
        pl.semaphore_signal(barrier, inc=1, device_id=peer, device_id_type=MESH_ID)
    for layers, columns in ((1, 0), (-1, 0), (1, 1), (-1, -1)):
        greet(layers, columns)
    pl.loop(1, 8)(lambda step: greet(4 * step, 0))
    pl.loop(1, COLUMNS)(lambda step: greet(0, step))

    lane = lax.broadcasted_iota(i32, (1, 128), 1)
    sublane = lax.broadcasted_iota(i32, (8, 128), 0)
    lanes8 = lax.broadcasted_iota(i32, (8, 128), 1)
    plan = [plan_ref[i] for i in range(SLOTS)]
    mine = [((value >> 6) - layer) & (GROUP - 1) for value in plan]
    row = jnp.zeros((1, 128), i32)
    counts = jnp.zeros((8, 128), i32)
    tile = jnp.zeros((8, 128), f32)
    for i in range(SLOTS):
        row = jnp.where(lane == i, plan[i], row)
        row = jnp.where(lane == 32 + mine[i], 1, row)
        counts = jnp.where(sublane == i, counts_ref[i], counts)
        for m in range(3):
            tile = jnp.where((sublane == i) & (lanes8 == m), nodes_ref[m, 0, 0, i], tile)
    row_s[0] = row
    tile_s[...] = tile
    for a in range(16):
        shear2 = 2.0 * shear_ref[a : a + 1, :]
        for i, value in enumerate((shear2, bulk_ref[a : a + 1, :], radius_ref[a : a + 1, :])):
            material_s[a, i] = jnp.broadcast_to(value, (8, 256))

    pl.semaphore_wait(barrier, 3 + 4 + 7 + COLUMNS - 1)

    def to(layers, columns):
        return place((layer + layers) & (GROUP - 1), (column + columns) & (COLUMNS - 1))

    def halo(src, dst, sems, sign):
        return [
            pltpu.make_async_remote_copy(
                src_ref=src, dst_ref=dst.at[k], send_sem=sems.at[0, k], recv_sem=sems.at[1, k],
                device_id=to(sign * x, sign * y), device_id_type=MESH_ID,
            )
            for k, (x, y) in enumerate(((1, 0), (0, 1), (1, 1)))
        ]

    def along_row(step):
        return pltpu.make_async_remote_copy(
            src_ref=row_s.at[0], dst_ref=group_s.at[layer], send_sem=group_sem.at[0, step],
            recv_sem=group_sem.at[1, step], device_id=place(at_x(step), column), device_id_type=MESH_ID,
        )

    def along_z(step):
        rows = group_s.at[pl.ds(z * 4, 4)]
        return pltpu.make_async_remote_copy(
            src_ref=rows, dst_ref=rows, send_sem=group_sem.at[0, 4 + step],
            recv_sem=group_sem.at[1, 4 + step], device_id=to(4 * step, 0), device_id_type=MESH_ID,
        )

    def to_column(step):
        return pltpu.make_async_remote_copy(
            src_ref=second_s.at[0], dst_ref=across_s.at[column], send_sem=across_sem.at[0, step],
            recv_sem=across_sem.at[1, step], device_id=to(0, step), device_id_type=MESH_ID,
        )

    nodes_halo = halo(tile_s, nodes_s, nodes_sem, -1)
    for copy in nodes_halo:
        copy.start()
    for step in range(1, 4):
        along_row(step).start()
    group_s[layer] = row

    for copy in incoming:
        copy.wait()

    @pl.loop(0, 96, unroll=4)
    def _(row):
        for h, lanes in enumerate(HALVES):
            plastic_s[row, :, lanes] = halves_s[h, pl.ds(row, 8, stride=96), :]

    @pl.loop(0, 96, unroll=8)
    def _(row):
        update_s[row] = jnp.zeros((8, 256), f32)
        mapped_s[row] = jnp.zeros((8, 256), f32)

    for copy in nodes_halo:
        copy.wait()
    zero = jnp.zeros((8, 128), f32)

    def gradients(t00, t10, t01, t11, shift):
        along_x = 0.25 * ((t10 + t11) - (t00 + t01))
        along_y = 0.25 * ((t01 + t11) - (t00 + t10))
        along_z = 0.25 * ((t00 + t10) + (t01 + t11))
        return along_x + shift(along_x), along_y + shift(along_y), shift(along_z) - along_z

    inner_x, inner_y = layer < GROUP - 1, column < COLUMNS - 1
    by_x, by_y, by_z = gradients(
        tile,
        jnp.where(inner_x, nodes_s[0], zero),
        jnp.where(inner_y, nodes_s[1], zero),
        jnp.where(inner_x & inner_y, nodes_s[2], zero),
        lambda value: jnp.where(sublane < 7, pltpu.roll(value, 7, 0), zero),
    )
    macro = [
        by_x[:, 0:1],
        by_y[:, 1:2],
        by_z[:, 2:3],
        0.5 * (by_z[:, 1:2] + by_y[:, 2:3]),
        0.5 * (by_z[:, 0:1] + by_x[:, 2:3]),
        0.5 * (by_y[:, 0:1] + by_x[:, 1:2]),
    ]
    for c in range(6):
        start = jnp.broadcast_to(macro[c], (8, 256))

        @pl.loop(0, 16, unroll=8)
        def _(a):
            strain_s[c * 16 + a] = start

    def split(value):
        high = value.astype(bf16)
        low = (value - high.astype(f32)).astype(bf16)
        return high, low

    def polarization(step):
        @pl.loop(0, 16)
        def _(a):
            for lanes in HALVES:
                shear2 = material_s[a, 0, :, lanes]
                bulk = material_s[a, 1, :, lanes]
                radius = material_s[a, 2, :, lanes]
                elastic = [strain_s[c * 16 + a, :, lanes] - plastic_s[c * 16 + a, :, lanes] for c in range(6)]
                volume, _, trial, factor = flow_rule(elastic, shear2, radius)
                pressure = bulk * volume
                for c in range(6):
                    value = factor * trial[c]
                    stress_s[c * 16 + a, :, lanes] = value + pressure if c < 3 else value

        @pl.loop(0, 3)
        def _(pair):
            for lanes in HALVES:
                sets = []
                for half in range(2):
                    y = real_forward([stress_s[pair * 32 + half * 16 + a, :, lanes] for a in range(16)])
                    sets.append([y[0][0], y[8][0]] + [part for k in range(1, 8) for part in y[k]])
                rows = pl.ds(pl.multiple_of(pair * 16, 16), 16)
                for r in range(16):
                    high, low = split(jnp.concatenate([sets[0][r], sets[1][r]], axis=0))
                    left_s[r, rows, lanes] = high
                    left_s[r, rows, slice(256 + lanes.start, 256 + lanes.stop)] = low

        @pl.when(step == 0)
        def _():
            tables[1].wait()
            tables[2].wait()
            tables[0].wait()

            @pl.loop(0, 24)
            def _(block):
                rows = green_ref[pl.ds(pl.multiple_of(block * 8, 8), 8), :]
                for r in range(8):
                    green_s[block * 8 + r] = jnp.broadcast_to(rows[r : r + 1, :], (8, 256))

        left = left_s[...].reshape(768, 512)
        product_s[...] = jnp.dot(
            jnp.concatenate([left, left[:, :256]], axis=1), dft_ref[...], preferred_element_type=f32
        ).reshape(16, 48, 512)

        def operate(k, re, im, lanes):
            for t, value in ((2 * k, re), (2 * k + 1, im)):
                value = value[:3] + [v + v for v in value[3:]]
                out = [None] * 6
                j = 0
                for i in range(6):
                    for m in range(i, 6):
                        g = green_s[k * 21 + j, :, lanes]
                        j += 1
                        out[i] = g * value[m] if out[i] is None else out[i] + g * value[m]
                        if m != i:
                            out[m] = g * value[i] if out[m] is None else out[m] + g * value[i]
                for pair in range(3):
                    high, low = split(jnp.concatenate([out[2 * pair], out[2 * pair + 1]], axis=0))
                    left2_s[t, slice(pair * 16, pair * 16 + 16), lanes] = high
                    left2_s[t, slice(pair * 16, pair * 16 + 16), slice(256 + lanes.start, 256 + lanes.stop)] = low

        for k, row in ((0, 0), (8, 1)):
            for lanes in HALVES:
                wide = slice(256 + lanes.start, 256 + lanes.stop)
                re = [product_s[row, slice(c * 8, c * 8 + 8), lanes] for c in range(6)]
                im = [-product_s[row, slice(c * 8, c * 8 + 8), wide] for c in range(6)]
                operate(k, re, im, lanes)

        @pl.loop(1, 8)
        def _(k):
            for lanes in HALVES:
                wide = slice(256 + lanes.start, 256 + lanes.stop)
                re, im = [], []
                for c in range(6):
                    rows = slice(c * 8, c * 8 + 8)
                    re.append(product_s[2 * k, rows, lanes] + product_s[2 * k + 1, rows, wide])
                    im.append(product_s[2 * k + 1, rows, lanes] - product_s[2 * k, rows, wide])
                operate(k, re, im, lanes)

        left2 = left2_s[...].reshape(864, 512)
        product2_s[...] = jnp.dot(
            jnp.concatenate([left2, left2[:, :256]], axis=1), dft_ref[...], preferred_element_type=f32
        ).reshape(18, 48, 512)

    def update_of(c, lanes):
        wide = slice(256 + lanes.start, 256 + lanes.stop)
        rows = pl.ds(pl.multiple_of(c * 8, 8), 8)
        y = []
        for k in range(9):
            re = product2_s[2 * k, rows, lanes] - product2_s[2 * k + 1, rows, wide]
            im = None if k in (0, 8) else product2_s[2 * k, rows, wide] + product2_s[2 * k + 1, rows, lanes]
            y.append((re, im))
        return real_backward(y)

    @pl.loop(0, 3)
    def _(step):
        polarization(step)

        @pl.when(step == 0)
        def _():
            for peer in range(1, 4):
                along_row(peer).wait()
            pl.loop(1, 8)(lambda peer: along_z(peer).start())

        @pl.when(step == 1)
        def _():
            pl.loop(1, 8)(lambda peer: along_z(peer).wait())
            union = group_s[0]
            for i in range(1, GROUP):
                union = jnp.maximum(union, group_s[i])
            second_s[0] = union
            across_s[column] = union
            pl.loop(1, COLUMNS)(lambda peer: to_column(peer).start())

        zero = jnp.zeros((8, 128), f32)

        def gather(c, carry):
            numerator, denominator = carry
            for lanes in HALVES:
                update = update_of(c, lanes)
                for a in range(16):
                    change = update[a] - update_s[c * 16 + a, :, lanes]
                    numerator = numerator + change * update[a]
                    denominator = denominator + change * change
                    update_s[c * 16 + a, :, lanes] = update[a]
            return numerator, denominator

        numerator, denominator = lax.fori_loop(0, 6, gather, (zero, zero))
        scale = 1.0 / float(6 * 16**3)
        numerator = jnp.sum(numerator, axis=1, keepdims=True) * scale
        denominator = jnp.sum(denominator, axis=1, keepdims=True) * scale + 1e-06
        weight = jnp.broadcast_to(jnp.where(step > 0, numerator / denominator, 0.0), (8, 256))
        active = step < jnp.concatenate([counts, counts], axis=1)

        @pl.loop(0, 96, unroll=4)
        def _(row):
            strain = strain_s[row]
            mapped = strain - update_s[row]
            candidate = mapped - weight * (mapped - mapped_s[row])
            mapped_s[row] = mapped
            strain_s[row] = jnp.where(active, candidate, strain)

    def finish(a, sums):
        sums = list(sums)
        for lanes in HALVES:
            shear2 = material_s[a, 0, :, lanes]
            bulk = material_s[a, 1, :, lanes]
            radius = material_s[a, 2, :, lanes]
            plastic = [plastic_s[c * 16 + a, :, lanes] for c in range(6)]
            elastic = [strain_s[c * 16 + a, :, lanes] - plastic[c] for c in range(6)]
            volume, deviator, trial, factor = flow_rule(elastic, shear2, radius)
            pressure = bulk * volume
            for c in range(6):
                value = factor * trial[c]
                sums[c] = sums[c] + (value + pressure if c < 3 else value)
                plastic_s[c * 16 + a, :, lanes] = plastic[c] + (deviator[c] - factor * deviator[c])
        return tuple(sums)

    sums = lax.fori_loop(0, 16, finish, (zero,) * 6)
    means = zero
    for c in range(6):
        means = jnp.where(lanes8 == c, jnp.sum(sums[c], axis=1, keepdims=True) * (1.0 / 4096.0), means)
    means_s[...] = means
    stress_halo = halo(means_s, below_s, below_sem, 1)
    for copy in stress_halo:
        copy.start()

    @pl.loop(0, 96, unroll=4)
    def _(row):
        for h, lanes in enumerate(HALVES):
            updated_ref[h, pl.ds(row, 8, stride=96), :] = plastic_s[row, :, lanes]

    for copy in stress_halo:
        copy.wait()
    inner_x, inner_y = layer > 0, column > 0
    by_x, by_y, by_z = gradients(
        means,
        jnp.where(inner_x, below_s[0], zero),
        jnp.where(inner_y, below_s[1], zero),
        jnp.where(inner_x & inner_y, below_s[2], zero),
        lambda value: jnp.where(sublane > 0, pltpu.roll(value, 1, 0), zero),
    )
    force = zero
    for i, (p, q, r) in enumerate(((0, 5, 4), (5, 1, 3), (4, 3, 2))):
        value = by_x[:, p : p + 1] + by_y[:, q : q + 1] + by_z[:, r : r + 1]
        force = jnp.where(lanes8 == i, value, force)
    force_ref[...] = force
    pl.loop(1, COLUMNS)(lambda peer: to_column(peer).wait())
    used = across_s[0]
    for i in range(1, COLUMNS):
        used = jnp.maximum(used, across_s[i])
    used_ref[...] = used
    rows_ref[...] = group_s[...]


def solve(plan, nodes, counts, plastic, bulk, shear, radius):
    f32, bf16, i32 = jnp.float32, jnp.bfloat16, jnp.int32
    vm, sm = pl.BlockSpec(memory_space=pltpu.VMEM), pl.BlockSpec(memory_space=pltpu.SMEM)
    anywhere = pl.BlockSpec(memory_space=pltpu.HBM)
    return pl.pallas_call(
        step_kernel,
        out_shape=(
            jax.ShapeDtypeStruct((GROUP, 1, 128), i32),
            jax.ShapeDtypeStruct((1, 128), i32),
            jax.ShapeDtypeStruct((8, 128), f32),
            jax.ShapeDtypeStruct((2, 768, 128), f32),
        ),
        in_specs=[sm] * 3 + [anywhere] + [vm] * 3 + [anywhere] * 2,
        out_specs=(vm,) * 4,
        scratch_shapes=[
            pltpu.VMEM((1, 1, 128), i32),
            pltpu.VMEM((GROUP, 1, 128), i32),
            pltpu.VMEM((1, 1, 128), i32),
            pltpu.VMEM((COLUMNS, 1, 128), i32),
            pltpu.SemaphoreType.DMA((2, 12)),
            pltpu.SemaphoreType.DMA((2, COLUMNS)),
            pltpu.VMEM((8, 128), f32),
            pltpu.VMEM((3, 8, 128), f32),
            pltpu.VMEM((8, 128), f32),
            pltpu.VMEM((3, 8, 128), f32),
            pltpu.SemaphoreType.DMA((2, 3)),
            pltpu.SemaphoreType.DMA((2, 3)),
            pltpu.VMEM((2, 768, 128), f32),
            pltpu.SemaphoreType.DMA((2,)),
            pltpu.VMEM((768, 512), bf16),
            pltpu.VMEM((192, 256), f32),
            pltpu.SemaphoreType.DMA((3,)),
            pltpu.VMEM((16, 3, 8, 256), f32),
            pltpu.VMEM((192, 8, 256), f32),
            pltpu.VMEM((96, 8, 256), f32),
            pltpu.VMEM((96, 8, 256), f32),
            pltpu.VMEM((96, 8, 256), f32),
            pltpu.VMEM((96, 8, 256), f32),
            pltpu.VMEM((96, 8, 256), f32),
            pltpu.VMEM((16, 48, 512), bf16),
            pltpu.VMEM((16, 48, 512), f32),
            pltpu.VMEM((18, 48, 512), bf16),
            pltpu.VMEM((18, 48, 512), f32),
        ],
        compiler_params=pltpu.CompilerParams(
            collective_id=0, has_side_effects=True, vmem_limit_bytes=60 << 20
        ),
        name="step",
    )(
        plan,
        nodes,
        counts,
        plastic.reshape(768, 256),
        bulk,
        shear,
        radius,
        jnp.asarray(transform_tables(16)),
        jnp.asarray(green_table(16)),
    )


MESH_ID = pl.DeviceIdType.MESH
GROUP, COLUMNS, SLOTS, PACK = 32, 8, 8, 2


def place(layer, column):
    return {"rve_0": layer // 4, "rve_1": layer % 4, "mic": column // 2, "mac": column % 2}


def own_place():
    layer = lax.axis_index("rve_0") * 4 + lax.axis_index("rve_1")
    return layer, lax.axis_index("mic") * 2 + lax.axis_index("mac")


def agenda_kernel(
    plan_ref, used_ref, updated_ref, total_ref, shift_ref, goal_ref, origin_ref, row_ref, *packets_and_sems
):
    layer, _ = own_place()
    packets, sems = packets_and_sems[:-1], packets_and_sems[-1]
    mine = [((plan_ref[layer, 0, i] >> 6) - layer) & (GROUP - 1) for i in range(SLOTS)]
    order_rank = []
    for i in range(SLOTS):
        rank = jnp.int32(0)
        for k in range(SLOTS):
            if k != i:
                rank = rank + jnp.where(mine[k] <= mine[i] if k < i else mine[k] < mine[i], 1, 0)
        goal_ref[rank] = PACK * ((layer + mine[i]) & (GROUP - 1)) + (rank & (PACK - 1))
        order_rank.append(rank)
    copies = []
    for k in range(SLOTS):
        index = jnp.int32(0)
        for i in range(SLOTS):
            index = jnp.where(order_rank[i] == k, i, index)
        rows = pl.ds(pl.multiple_of(index * 96, 96), 96)
        for h, lanes in enumerate(HALVES):
            copies.append(
                pltpu.make_async_copy(
                    updated_ref.at[h, rows], packets[k // PACK].at[k % PACK, :, lanes], sems.at[2 * k + h]
                )
            )
    for copy in copies:
        copy.start()
    total = jnp.int32(0)
    for d in range(GROUP):
        shift_ref[total] = jnp.int32(d)
        total = total + jnp.where(used_ref[0, 32 + d] > 0, 1, 0)
    total_ref[0] = total

    def step(i, count):
        shift = shift_ref[i]
        source = (layer - shift) & (GROUP - 1)
        for k in range(SLOTS):
            value = plan_ref[source, 0, k]
            row_ref[count] = value & (SLOTS - 1)
            origin_ref[count] = PACK * source + (count & (PACK - 1))
            count = jnp.minimum(count + jnp.where((value >> 6) == layer, 1, 0), SLOTS)
        return count

    lax.fori_loop(0, total, step, jnp.int32(0))
    for copy in copies:
        copy.wait()


def agenda(plan, used, updated):
    sm, vm = pl.BlockSpec(memory_space=pltpu.SMEM), pl.BlockSpec(memory_space=pltpu.VMEM)
    pair = jax.ShapeDtypeStruct((PACK, 96, 256), jnp.float32)
    flows = SLOTS // PACK
    sizes = (1, GROUP + 1, SLOTS, SLOTS + 1, SLOTS + 1)
    return pl.pallas_call(
        agenda_kernel,
        out_shape=tuple(jax.ShapeDtypeStruct((size,), jnp.int32) for size in sizes) + (pair,) * flows,
        in_specs=[sm, sm, vm],
        out_specs=(sm,) * len(sizes) + (pl.BlockSpec(memory_space=pltpu.HBM),) * flows,
        scratch_shapes=[pltpu.SemaphoreType.DMA((2 * SLOTS,))],
        name="agenda",
    )(plan, used, updated)


def rotate_kernel(shift, sent_ref, got_ref, send_sem, recv_sem):
    layer, column = own_place()
    target, source = (layer + shift) & (GROUP - 1), (layer - shift) & (GROUP - 1)
    barrier = pltpu.get_barrier_semaphore()
    pl.semaphore_signal(barrier, inc=1, device_id=place(source, column), device_id_type=MESH_ID)
    pl.semaphore_wait(barrier, 1)
    copy = pltpu.make_async_remote_copy(
        src_ref=sent_ref,
        dst_ref=got_ref,
        send_sem=send_sem,
        recv_sem=recv_sem,
        device_id=place(target, column),
        device_id_type=MESH_ID,
    )
    copy.start()
    copy.wait()


def rotate(shift, packets):
    return pl.pallas_call(
        functools.partial(rotate_kernel, shift),
        out_shape=jax.ShapeDtypeStruct(packets.shape, packets.dtype),
        in_specs=[pl.BlockSpec(memory_space=pltpu.HBM)],
        out_specs=pl.BlockSpec(memory_space=pltpu.VMEM),
        scratch_shapes=[pltpu.SemaphoreType.DMA, pltpu.SemaphoreType.DMA],
        compiler_params=pltpu.CompilerParams(collective_id=shift, has_side_effects=True),
        name=f"rotate{shift}",
    )(packets)


def stay_kernel(sent_ref, got_ref, sem):
    copy = pltpu.make_async_copy(sent_ref, got_ref, sem)
    copy.start()
    copy.wait()


def stay(packets):
    return pl.pallas_call(
        stay_kernel,
        out_shape=jax.ShapeDtypeStruct(packets.shape, packets.dtype),
        in_specs=[pl.BlockSpec(memory_space=pltpu.HBM)],
        out_specs=pl.BlockSpec(memory_space=pltpu.VMEM),
        scratch_shapes=[pltpu.SemaphoreType.DMA],
        name="stay",
    )(packets)


def land_kernel(row_ref, *refs):
    held, out_ref, sems = refs[:-2], refs[-2], refs[-1]
    copies = []
    for k in range(SLOTS):
        copies.append(pltpu.make_async_copy(held[k // PACK].at[k % PACK], out_ref.at[row_ref[k]], sems.at[k]))
    for copy in copies:
        copy.start()
    for copy in copies:
        copy.wait()


def land(rows, held):
    vm, sm = pl.BlockSpec(memory_space=pltpu.VMEM), pl.BlockSpec(memory_space=pltpu.SMEM)
    return pl.pallas_call(
        land_kernel,
        out_shape=jax.ShapeDtypeStruct((SLOTS, 96, 256), jnp.float32),
        in_specs=[sm] + [vm] * len(held),
        out_specs=pl.BlockSpec(memory_space=pl.ANY),
        scratch_shapes=[pltpu.SemaphoreType.DMA((SLOTS,))],
        name="land",
    )(rows, *held)


def migrate(packets, total, shifts, goals, origins, rows):
    branches = [stay] + [functools.partial(rotate, d) for d in range(1, GROUP)]
    flows = SLOTS // PACK

    def few(packets):
        return tuple(
            lax.switch(shifts[f] - f, branches[f : GROUP - flows + 1 + f], packets[f]) for f in range(flows)
        )

    def many(packets):
        hits = goals[None, :] == jnp.arange(PACK * GROUP)[:, None]
        source = jnp.sum(jnp.where(hits, jnp.arange(SLOTS)[None, :], 0), axis=1)
        slots = jnp.take(jnp.concatenate(packets, axis=0), source, axis=0)
        arrived = lax.all_to_all(slots, RVE, split_axis=0, concat_axis=0, tiled=True)
        held = jnp.take(arrived, origins[:SLOTS], axis=0)
        return tuple(held[PACK * f : PACK * f + PACK] for f in range(flows))

    return land(rows, lax.cond(total == flows, few, many, packets))


def on_device(
    displacement, plastic, bulk_modulus, shear_modulus, yield_radius, counts, migration_plan
):
    plans, used, force, updated = solve(
        migration_plan, displacement, counts, plastic, bulk_modulus, shear_modulus, yield_radius
    )
    total, shifts, goals, origins, landing, *packets = agenda(plans, used, updated)
    force = force[:, :3].T.reshape(displacement.shape)
    moved = migrate(tuple(packets), total[0], shifts, goals, origins, landing)
    return (force, moved.reshape(plastic.shape))


def solution(mesh):
    finer = Mesh(
        mesh.devices.reshape(8, 4, mesh.shape["mic"], mesh.shape["mac"]),
        ("rve_0", "rve_1", "mic", "mac"),
    )
    placed = (
        P(None, RVE, ("mic", "mac"), None),
        P(RVE_MIC_MAC, None, None, None),
        P(),
        P(),
        P(),
        P(RVE_MIC_MAC),
        P(RVE_MIC_MAC),
    )
    return jax.shard_map(
        on_device,
        mesh=finer,
        in_specs=placed,
        out_specs=(P(None, RVE, ("mic", "mac"), None), P(RVE_MIC_MAC, None, None, None)),
        check_vma=False,
    )
```

```python
import functools
import math

import jax
import jax.numpy as jnp
import numpy as np
from jax import lax
from jax.experimental import pallas as pl
from jax.experimental.pallas import tpu as pltpu
from jax.sharding import Mesh
from jax.sharding import PartitionSpec as P

RVE = ("rve_0", "rve_1")
RVE_MIC_MAC = ("rve_0", "rve_1", "mic", "mac")


COUPLING = 0.7
PAIRS = ((0, 0), (1, 1), (2, 2), (1, 2), (0, 2), (0, 1))


def transform_tables(n):
    plane = np.arange(n * n)
    b, c = plane // n, plane % n
    angle = 2.0 * np.pi / n * ((np.outer(b, b) + np.outer(c, c)) % n)
    table = np.concatenate([np.cos(angle), np.sin(angle)], axis=1).astype(np.float32)
    high = table.astype(jnp.bfloat16)
    low = (table - high.astype(np.float32)).astype(jnp.bfloat16)
    return np.concatenate([high, low], axis=0)


def green_table(n):
    index = np.stack(np.meshgrid(np.arange(n), np.arange(n), np.arange(n), indexing="ij"))

    def operator(i):
        k = ((i + n // 2) % n - n // 2).astype(np.float64)
        q = np.sum(k * k, axis=0)
        safe = np.maximum(q, 1.0)
        rows = []
        for m, r in PAIRS:
            row = []
            for p, s in PAIRS:
                eye = lambda u, v: 1.0 if u == v else 0.0
                first = (
                    eye(m, p) * k[r] * k[s] + eye(m, s) * k[r] * k[p] + eye(r, p) * k[m] * k[s] + eye(r, s) * k[m] * k[p]
                ) / (4.0 * safe)
                row.append(first - COUPLING * k[m] * k[r] * k[p] * k[s] / (safe * safe))
            rows.append(row)
        return np.where(q > 0, np.array(rows), 0.0)

    even = 0.5 * (operator(index) + operator((-index) % n)) / float(n**3)
    even = even[:, :, : n // 2 + 1]
    rows = [even[i, j].reshape(n // 2 + 1, n * n) for i in range(6) for j in range(i, 6)]
    table = np.stack(rows, axis=1).reshape(-1, n * n).astype(np.float32)
    return np.pad(table, ((0, -table.shape[0] % 8), (0, 0)))


def turn(k, n, value, sign):
    re, im = value
    if k == 0:
        return value
    if 4 * k == n:
        return (im, -re) if sign < 0 else (-im, re)
    if 8 * k == n:
        r = math.sqrt(0.5)
        return ((re + im) * r, (im - re) * r) if sign < 0 else ((re - im) * r, (re + im) * r)
    c, s = math.cos(2 * math.pi * k / n), sign * math.sin(2 * math.pi * k / n)
    return (re * c - im * s, re * s + im * c)


def real_forward(x):
    n = len(x)
    if n == 2:
        return [(x[0] + x[1], None), (x[0] - x[1], None)]
    even, odd = real_forward(x[0::2]), real_forward(x[1::2])
    out = [None] * (n // 2 + 1)
    out[0] = (even[0][0] + odd[0][0], None)
    out[n // 2] = (even[0][0] - odd[0][0], None)
    for k in range(1, n // 4 + 1):
        if 4 * k == n:
            out[k] = (even[k][0], -odd[k][0])
        else:
            t = turn(k, n, odd[k], -1)
            out[k] = (even[k][0] + t[0], even[k][1] + t[1])
            out[n // 2 - k] = (even[k][0] - t[0], t[1] - even[k][1])
    return out


def real_backward(y):
    n = 2 * (len(y) - 1)
    if n == 2:
        return [y[0][0] + y[1][0], y[0][0] - y[1][0]]
    even, odd = [None] * (n // 4 + 1), [None] * (n // 4 + 1)
    even[0] = (y[0][0] + y[n // 2][0], None)
    odd[0] = (y[0][0] - y[n // 2][0], None)
    for k in range(1, n // 4 + 1):
        if 4 * k == n:
            even[k] = (2.0 * y[k][0], None)
            odd[k] = (-2.0 * y[k][1], None)
        else:
            o = y[n // 2 - k]
            even[k] = (y[k][0] + o[0], y[k][1] - o[1])
            odd[k] = turn(k, n, (y[k][0] - o[0], y[k][1] + o[1]), 1)
    out = [None] * n
    out[0::2] = real_backward(even)
    out[1::2] = real_backward(odd)
    return out


def flow_rule(elastic, shear2, radius):
    volume = elastic[0] + elastic[1] + elastic[2]
    mean = volume * (1.0 / 3.0)
    deviator = [elastic[i] - mean for i in range(3)] + list(elastic[3:])
    trial = [shear2 * d for d in deviator]
    normal = trial[0] * trial[0] + trial[1] * trial[1] + trial[2] * trial[2]
    mixed = trial[3] * trial[3] + trial[4] * trial[4] + trial[5] * trial[5]
    squared = normal + (mixed + mixed)
    factor = radius * lax.rsqrt(jnp.maximum(squared, radius * radius))
    return volume, deviator, trial, factor


HALVES = (slice(0, 128), slice(128, 256))


def step_kernel(
    plan_ref, nodes_ref, counts_ref, plastic_ref, bulk_ref, shear_ref, radius_ref, dft_hbm, green_hbm,
    rows_ref, used_ref, force_ref, updated_ref,
    row_s, group_s, second_s, across_s, group_sem, across_sem, tile_s, nodes_s, means_s, below_s, nodes_sem, below_sem,
    halves_s, copy_sem, dft_ref, green_ref, table_sem, material_s, green_s, plastic_s,
    strain_s, stress_s, update_s, mapped_s, left_s, product_s, left2_s, product2_s,
):
    f32, bf16 = jnp.float32, jnp.bfloat16
    i32 = jnp.int32
    layer, column = own_place()
    incoming = [
        pltpu.make_async_copy(plastic_ref.at[:, lanes], halves_s.at[h], copy_sem.at[h]) for h, lanes in enumerate(HALVES)
    ]
    tables = [
        pltpu.make_async_copy(green_hbm, green_ref, table_sem.at[0]),
        pltpu.make_async_copy(dft_hbm.at[:256], dft_ref.at[:256], table_sem.at[1]),
        pltpu.make_async_copy(dft_hbm, dft_ref.at[256:], table_sem.at[2]),
    ]
    for copy in incoming + tables:
        copy.start()
    barrier = pltpu.get_barrier_semaphore()

    def greet(layers, columns):
        peer = place((layer + layers) & (GROUP - 1), (column + columns) & (COLUMNS - 1))
        pl.semaphore_signal(barrier, inc=1, device_id=peer, device_id_type=MESH_ID)

    z, x = layer // 4, layer % 4

    def at_x(step):
        return z * 4 + ((x + step) & 3)

    for step in range(1, 4):
        peer = place(at_x(step), column)
        pl.semaphore_signal(barrier, inc=1, device_id=peer, device_id_type=MESH_ID)
    for layers, columns in ((1, 0), (-1, 0), (1, 1), (-1, -1)):
        greet(layers, columns)
    pl.loop(1, 8)(lambda step: greet(4 * step, 0))
    pl.loop(1, COLUMNS)(lambda step: greet(0, step))

    lane = lax.broadcasted_iota(i32, (1, 128), 1)
    sublane = lax.broadcasted_iota(i32, (8, 128), 0)
    lanes8 = lax.broadcasted_iota(i32, (8, 128), 1)
    plan = [plan_ref[i] for i in range(SLOTS)]
    mine = [((value >> 6) - layer) & (GROUP - 1) for value in plan]
    row = jnp.zeros((1, 128), i32)
    counts = jnp.zeros((8, 128), i32)
    tile = jnp.zeros((8, 128), f32)
    for i in range(SLOTS):
        row = jnp.where(lane == i, plan[i], row)
        row = jnp.where(lane == 32 + mine[i], 1, row)
        counts = jnp.where(sublane == i, counts_ref[i], counts)
        for m in range(3):
            tile = jnp.where((sublane == i) & (lanes8 == m), nodes_ref[m, 0, 0, i], tile)
    row_s[0] = row
    tile_s[...] = tile
    for a in range(16):
        shear2 = 2.0 * shear_ref[a : a + 1, :]
        for i, value in enumerate((shear2, bulk_ref[a : a + 1, :], radius_ref[a : a + 1, :])):
            material_s[a, i] = jnp.broadcast_to(value, (8, 256))

    pl.semaphore_wait(barrier, 3 + 4 + 7 + COLUMNS - 1)

    def to(layers, columns):
        return place((layer + layers) & (GROUP - 1), (column + columns) & (COLUMNS - 1))

    def halo(src, dst, sems, sign):
        return [
            pltpu.make_async_remote_copy(
                src_ref=src, dst_ref=dst.at[k], send_sem=sems.at[0, k], recv_sem=sems.at[1, k],
                device_id=to(sign * x, sign * y), device_id_type=MESH_ID,
            )
            for k, (x, y) in enumerate(((1, 0), (0, 1), (1, 1)))
        ]

    def along_row(step):
        return pltpu.make_async_remote_copy(
            src_ref=row_s.at[0], dst_ref=group_s.at[layer], send_sem=group_sem.at[0, step],
            recv_sem=group_sem.at[1, step], device_id=place(at_x(step), column), device_id_type=MESH_ID,
        )

    def along_z(step):
        rows = group_s.at[pl.ds(z * 4, 4)]
        return pltpu.make_async_remote_copy(
            src_ref=rows, dst_ref=rows, send_sem=group_sem.at[0, 4 + step],
            recv_sem=group_sem.at[1, 4 + step], device_id=to(4 * step, 0), device_id_type=MESH_ID,
        )

    def to_column(step):
        return pltpu.make_async_remote_copy(
            src_ref=second_s.at[0], dst_ref=across_s.at[column], send_sem=across_sem.at[0, step],
            recv_sem=across_sem.at[1, step], device_id=to(0, step), device_id_type=MESH_ID,
        )

    nodes_halo = halo(tile_s, nodes_s, nodes_sem, -1)
    for copy in nodes_halo:
        copy.start()
    for step in range(1, 4):
        along_row(step).start()
    group_s[layer] = row

    for copy in incoming:
        copy.wait()

    @pl.loop(0, 96, unroll=4)
    def _(row):
        for h, lanes in enumerate(HALVES):
            plastic_s[row, :, lanes] = halves_s[h, pl.ds(row, 8, stride=96), :]

    @pl.loop(0, 96, unroll=8)
    def _(row):
        update_s[row] = jnp.zeros((8, 256), f32)
        mapped_s[row] = jnp.zeros((8, 256), f32)

    for copy in nodes_halo:
        copy.wait()
    zero = jnp.zeros((8, 128), f32)

    def gradients(t00, t10, t01, t11, shift):
        along_x = 0.25 * ((t10 + t11) - (t00 + t01))
        along_y = 0.25 * ((t01 + t11) - (t00 + t10))
        along_z = 0.25 * ((t00 + t10) + (t01 + t11))
        return along_x + shift(along_x), along_y + shift(along_y), shift(along_z) - along_z

    inner_x, inner_y = layer < GROUP - 1, column < COLUMNS - 1
    by_x, by_y, by_z = gradients(
        tile,
        jnp.where(inner_x, nodes_s[0], zero),
        jnp.where(inner_y, nodes_s[1], zero),
        jnp.where(inner_x & inner_y, nodes_s[2], zero),
        lambda value: jnp.where(sublane < 7, pltpu.roll(value, 7, 0), zero),
    )
    macro = [
        by_x[:, 0:1],
        by_y[:, 1:2],
        by_z[:, 2:3],
        0.5 * (by_z[:, 1:2] + by_y[:, 2:3]),
        0.5 * (by_z[:, 0:1] + by_x[:, 2:3]),
        0.5 * (by_y[:, 0:1] + by_x[:, 1:2]),
    ]
    for c in range(6):
        start = jnp.broadcast_to(macro[c], (8, 256))

        @pl.loop(0, 16, unroll=8)
        def _(a):
            strain_s[c * 16 + a] = start

    def split(value):
        high = value.astype(bf16)
        low = (value - high.astype(f32)).astype(bf16)
        return high, low

    def polarization(step):
        @pl.loop(0, 16)
        def _(a):
            for lanes in HALVES:
                shear2 = material_s[a, 0, :, lanes]
                bulk = material_s[a, 1, :, lanes]
                radius = material_s[a, 2, :, lanes]
                elastic = [strain_s[c * 16 + a, :, lanes] - plastic_s[c * 16 + a, :, lanes] for c in range(6)]
                volume, _, trial, factor = flow_rule(elastic, shear2, radius)
                pressure = bulk * volume
                for c in range(6):
                    value = factor * trial[c]
                    stress_s[c * 16 + a, :, lanes] = value + pressure if c < 3 else value

        @pl.loop(0, 3)
        def _(pair):
            for lanes in HALVES:
                sets = []
                for half in range(2):
                    y = real_forward([stress_s[pair * 32 + half * 16 + a, :, lanes] for a in range(16)])
                    sets.append([y[0][0], y[8][0]] + [part for k in range(1, 8) for part in y[k]])
                rows = pl.ds(pl.multiple_of(pair * 16, 16), 16)
                for r in range(16):
                    high, low = split(jnp.concatenate([sets[0][r], sets[1][r]], axis=0))
                    left_s[r, rows, lanes] = high
                    left_s[r, rows, slice(256 + lanes.start, 256 + lanes.stop)] = low

        @pl.when(step == 0)
        def _():
            tables[1].wait()
            tables[2].wait()
            tables[0].wait()

            @pl.loop(0, 24)
            def _(block):
                rows = green_ref[pl.ds(pl.multiple_of(block * 8, 8), 8), :]
                for r in range(8):
                    green_s[block * 8 + r] = jnp.broadcast_to(rows[r : r + 1, :], (8, 256))

        left = left_s[...].reshape(768, 512)
        product_s[...] = jnp.dot(
            jnp.concatenate([left, left[:, :256]], axis=1), dft_ref[...], preferred_element_type=f32
        ).reshape(16, 48, 512)

        def operate(k, re, im, lanes):
            for t, value in ((2 * k, re), (2 * k + 1, im)):
                value = value[:3] + [v + v for v in value[3:]]
                out = [None] * 6
                j = 0
                for i in range(6):
                    for m in range(i, 6):
                        g = green_s[k * 21 + j, :, lanes]
                        j += 1
                        out[i] = g * value[m] if out[i] is None else out[i] + g * value[m]
                        if m != i:
                            out[m] = g * value[i] if out[m] is None else out[m] + g * value[i]
                for pair in range(3):
                    high, low = split(jnp.concatenate([out[2 * pair], out[2 * pair + 1]], axis=0))
                    left2_s[t, slice(pair * 16, pair * 16 + 16), lanes] = high
                    left2_s[t, slice(pair * 16, pair * 16 + 16), slice(256 + lanes.start, 256 + lanes.stop)] = low

        for k, row in ((0, 0), (8, 1)):
            for lanes in HALVES:
                wide = slice(256 + lanes.start, 256 + lanes.stop)
                re = [product_s[row, slice(c * 8, c * 8 + 8), lanes] for c in range(6)]
                im = [-product_s[row, slice(c * 8, c * 8 + 8), wide] for c in range(6)]
                operate(k, re, im, lanes)

        @pl.loop(1, 8)
        def _(k):
            for lanes in HALVES:
                wide = slice(256 + lanes.start, 256 + lanes.stop)
                re, im = [], []
                for c in range(6):
                    rows = slice(c * 8, c * 8 + 8)
                    re.append(product_s[2 * k, rows, lanes] + product_s[2 * k + 1, rows, wide])
                    im.append(product_s[2 * k + 1, rows, lanes] - product_s[2 * k, rows, wide])
                operate(k, re, im, lanes)

        left2 = left2_s[...].reshape(864, 512)
        product2_s[...] = jnp.dot(
            jnp.concatenate([left2, left2[:, :256]], axis=1), dft_ref[...], preferred_element_type=f32
        ).reshape(18, 48, 512)

    def update_of(c, lanes):
        wide = slice(256 + lanes.start, 256 + lanes.stop)
        rows = pl.ds(pl.multiple_of(c * 8, 8), 8)
        y = []
        for k in range(9):
            re = product2_s[2 * k, rows, lanes] - product2_s[2 * k + 1, rows, wide]
            im = None if k in (0, 8) else product2_s[2 * k, rows, wide] + product2_s[2 * k + 1, rows, lanes]
            y.append((re, im))
        return real_backward(y)

    @pl.loop(0, 3)
    def _(step):
        polarization(step)

        @pl.when(step == 0)
        def _():
            for peer in range(1, 4):
                along_row(peer).wait()
            pl.loop(1, 8)(lambda peer: along_z(peer).start())

        @pl.when(step == 1)
        def _():
            pl.loop(1, 8)(lambda peer: along_z(peer).wait())
            union = group_s[0]
            for i in range(1, GROUP):
                union = jnp.maximum(union, group_s[i])
            second_s[0] = union
            across_s[column] = union
            pl.loop(1, COLUMNS)(lambda peer: to_column(peer).start())

        zero = jnp.zeros((8, 128), f32)

        def gather(c, carry):
            numerator, denominator = carry
            for lanes in HALVES:
                update = update_of(c, lanes)
                for a in range(16):
                    change = update[a] - update_s[c * 16 + a, :, lanes]
                    numerator = numerator + change * update[a]
                    denominator = denominator + change * change
                    update_s[c * 16 + a, :, lanes] = update[a]
            return numerator, denominator

        numerator, denominator = lax.fori_loop(0, 6, gather, (zero, zero))
        scale = 1.0 / float(6 * 16**3)
        numerator = jnp.sum(numerator, axis=1, keepdims=True) * scale
        denominator = jnp.sum(denominator, axis=1, keepdims=True) * scale + 1e-06
        weight = jnp.broadcast_to(jnp.where(step > 0, numerator / denominator, 0.0), (8, 256))
        active = step < jnp.concatenate([counts, counts], axis=1)

        @pl.loop(0, 96, unroll=4)
        def _(row):
            strain = strain_s[row]
            mapped = strain - update_s[row]
            candidate = mapped - weight * (mapped - mapped_s[row])
            mapped_s[row] = mapped
            strain_s[row] = jnp.where(active, candidate, strain)

    def finish(a, sums):
        sums = list(sums)
        for lanes in HALVES:
            shear2 = material_s[a, 0, :, lanes]
            bulk = material_s[a, 1, :, lanes]
            radius = material_s[a, 2, :, lanes]
            plastic = [plastic_s[c * 16 + a, :, lanes] for c in range(6)]
            elastic = [strain_s[c * 16 + a, :, lanes] - plastic[c] for c in range(6)]
            volume, deviator, trial, factor = flow_rule(elastic, shear2, radius)
            pressure = bulk * volume
            for c in range(6):
                value = factor * trial[c]
                sums[c] = sums[c] + (value + pressure if c < 3 else value)
                plastic_s[c * 16 + a, :, lanes] = plastic[c] + (deviator[c] - factor * deviator[c])
        return tuple(sums)

    sums = lax.fori_loop(0, 16, finish, (zero,) * 6)
    means = zero
    for c in range(6):
        means = jnp.where(lanes8 == c, jnp.sum(sums[c], axis=1, keepdims=True) * (1.0 / 4096.0), means)
    means_s[...] = means
    stress_halo = halo(means_s, below_s, below_sem, 1)
    for copy in stress_halo:
        copy.start()

    @pl.loop(0, 96, unroll=4)
    def _(row):
        for h, lanes in enumerate(HALVES):
            updated_ref[h, pl.ds(row, 8, stride=96), :] = plastic_s[row, :, lanes]

    for copy in stress_halo:
        copy.wait()
    inner_x, inner_y = layer > 0, column > 0
    by_x, by_y, by_z = gradients(
        means,
        jnp.where(inner_x, below_s[0], zero),
        jnp.where(inner_y, below_s[1], zero),
        jnp.where(inner_x & inner_y, below_s[2], zero),
        lambda value: jnp.where(sublane > 0, pltpu.roll(value, 1, 0), zero),
    )
    force = zero
    for i, (p, q, r) in enumerate(((0, 5, 4), (5, 1, 3), (4, 3, 2))):
        value = by_x[:, p : p + 1] + by_y[:, q : q + 1] + by_z[:, r : r + 1]
        force = jnp.where(lanes8 == i, value, force)
    force_ref[...] = force
    pl.loop(1, COLUMNS)(lambda peer: to_column(peer).wait())
    used = across_s[0]
    for i in range(1, COLUMNS):
        used = jnp.maximum(used, across_s[i])
    used_ref[...] = used
    rows_ref[...] = group_s[...]


def solve(plan, nodes, counts, plastic, bulk, shear, radius):
    f32, bf16, i32 = jnp.float32, jnp.bfloat16, jnp.int32
    vm, sm = pl.BlockSpec(memory_space=pltpu.VMEM), pl.BlockSpec(memory_space=pltpu.SMEM)
    anywhere = pl.BlockSpec(memory_space=pltpu.HBM)
    return pl.pallas_call(
        step_kernel,
        out_shape=(
            jax.ShapeDtypeStruct((GROUP, 1, 128), i32),
            jax.ShapeDtypeStruct((1, 128), i32),
            jax.ShapeDtypeStruct((8, 128), f32),
            jax.ShapeDtypeStruct((2, 768, 128), f32),
        ),
        in_specs=[sm] * 3 + [anywhere] + [vm] * 3 + [anywhere] * 2,
        out_specs=(vm,) * 4,
        scratch_shapes=[
            pltpu.VMEM((1, 1, 128), i32),
            pltpu.VMEM((GROUP, 1, 128), i32),
            pltpu.VMEM((1, 1, 128), i32),
            pltpu.VMEM((COLUMNS, 1, 128), i32),
            pltpu.SemaphoreType.DMA((2, 12)),
            pltpu.SemaphoreType.DMA((2, COLUMNS)),
            pltpu.VMEM((8, 128), f32),
            pltpu.VMEM((3, 8, 128), f32),
            pltpu.VMEM((8, 128), f32),
            pltpu.VMEM((3, 8, 128), f32),
            pltpu.SemaphoreType.DMA((2, 3)),
            pltpu.SemaphoreType.DMA((2, 3)),
            pltpu.VMEM((2, 768, 128), f32),
            pltpu.SemaphoreType.DMA((2,)),
            pltpu.VMEM((768, 512), bf16),
            pltpu.VMEM((192, 256), f32),
            pltpu.SemaphoreType.DMA((3,)),
            pltpu.VMEM((16, 3, 8, 256), f32),
            pltpu.VMEM((192, 8, 256), f32),
            pltpu.VMEM((96, 8, 256), f32),
            pltpu.VMEM((96, 8, 256), f32),
            pltpu.VMEM((96, 8, 256), f32),
            pltpu.VMEM((96, 8, 256), f32),
            pltpu.VMEM((96, 8, 256), f32),
            pltpu.VMEM((16, 48, 512), bf16),
            pltpu.VMEM((16, 48, 512), f32),
            pltpu.VMEM((18, 48, 512), bf16),
            pltpu.VMEM((18, 48, 512), f32),
        ],
        compiler_params=pltpu.CompilerParams(
            collective_id=0, has_side_effects=True, vmem_limit_bytes=60 << 20
        ),
        name="step",
    )(
        plan,
        nodes,
        counts,
        plastic.reshape(768, 256),
        bulk,
        shear,
        radius,
        jnp.asarray(transform_tables(16)),
        jnp.asarray(green_table(16)),
    )


MESH_ID = pl.DeviceIdType.MESH
GROUP, COLUMNS, SLOTS, PACK = 32, 8, 8, 2


def place(layer, column):
    return {"rve_0": layer // 4, "rve_1": layer % 4, "mic": column // 2, "mac": column % 2}


def own_place():
    layer = lax.axis_index("rve_0") * 4 + lax.axis_index("rve_1")
    return layer, lax.axis_index("mic") * 2 + lax.axis_index("mac")


def agenda_kernel(
    plan_ref, used_ref, updated_ref, force_ref, total_ref, goal_ref, origin_ref, row_ref, nodal_ref, *rest
):
    layer, _ = own_place()
    flows = SLOTS // PACK
    branch_refs, packets, (sems, shift_ref) = rest[:flows], rest[flows : 2 * flows], rest[2 * flows :]
    mine = [((plan_ref[layer, 0, i] >> 6) - layer) & (GROUP - 1) for i in range(SLOTS)]
    order_rank = []
    for i in range(SLOTS):
        rank = jnp.int32(0)
        for k in range(SLOTS):
            if k != i:
                rank = rank + jnp.where(mine[k] <= mine[i] if k < i else mine[k] < mine[i], 1, 0)
        goal_ref[rank] = PACK * ((layer + mine[i]) & (GROUP - 1)) + (rank & (PACK - 1))
        order_rank.append(rank)
    copies = []
    for k in range(SLOTS):
        index = jnp.int32(0)
        for i in range(SLOTS):
            index = jnp.where(order_rank[i] == k, i, index)
        rows = pl.ds(pl.multiple_of(index * 96, 96), 96)
        for h, lanes in enumerate(HALVES):
            copies.append(
                pltpu.make_async_copy(
                    updated_ref.at[h, rows], packets[k // PACK].at[k % PACK, :, lanes], sems.at[2 * k + h]
                )
            )
    for copy in copies:
        copy.start()
    total = jnp.int32(0)
    for d in range(GROUP):
        shift_ref[total] = jnp.int32(d)
        total = total + jnp.where(used_ref[0, 32 + d] > 0, 1, 0)
    total_ref[0] = total
    for f in range(flows):
        branch_refs[f][0] = jnp.clip(shift_ref[f] - f, 0, GROUP - flows)
    turned = jnp.transpose(force_ref[...])
    for i in range(3):
        nodal_ref[i, 0] = turned[i : i + 1]

    def step(i, count):
        shift = shift_ref[i]
        source = (layer - shift) & (GROUP - 1)
        for k in range(SLOTS):
            value = plan_ref[source, 0, k]
            row_ref[count] = value & (SLOTS - 1)
            origin_ref[count] = PACK * source + (count & (PACK - 1))
            count = jnp.minimum(count + jnp.where((value >> 6) == layer, 1, 0), SLOTS)
        return count

    lax.fori_loop(0, total, step, jnp.int32(0))
    for copy in copies:
        copy.wait()


def agenda(plan, used, updated, force):
    sm, vm = pl.BlockSpec(memory_space=pltpu.SMEM), pl.BlockSpec(memory_space=pltpu.VMEM)
    pair = jax.ShapeDtypeStruct((PACK, 96, 256), jnp.float32)
    flows = SLOTS // PACK
    sizes = (1, SLOTS, SLOTS + 1, SLOTS + 1)
    scalar, nodal = jax.ShapeDtypeStruct((1,), jnp.int32), jax.ShapeDtypeStruct((3, 1, 1, 8), jnp.float32)
    return pl.pallas_call(
        agenda_kernel,
        out_shape=tuple(jax.ShapeDtypeStruct((size,), jnp.int32) for size in sizes)
        + (nodal,) + (scalar,) * flows + (pair,) * flows,
        in_specs=[sm, sm, vm, vm],
        out_specs=(sm,) * len(sizes) + (vm,) + (sm,) * flows + (pl.BlockSpec(memory_space=pltpu.HBM),) * flows,
        scratch_shapes=[pltpu.SemaphoreType.DMA((2 * SLOTS,)), pltpu.SMEM((GROUP + 1,), jnp.int32)],
        name="agenda",
    )(plan, used, updated, force)


def rotate_kernel(shift, sent_ref, got_ref, send_sem, recv_sem):
    layer, column = own_place()
    target, source = (layer + shift) & (GROUP - 1), (layer - shift) & (GROUP - 1)
    barrier = pltpu.get_barrier_semaphore()
    pl.semaphore_signal(barrier, inc=1, device_id=place(source, column), device_id_type=MESH_ID)
    pl.semaphore_wait(barrier, 1)
    copy = pltpu.make_async_remote_copy(
        src_ref=sent_ref,
        dst_ref=got_ref,
        send_sem=send_sem,
        recv_sem=recv_sem,
        device_id=place(target, column),
        device_id_type=MESH_ID,
    )
    copy.start()
    copy.wait()


def rotate(shift, packets):
    return pl.pallas_call(
        functools.partial(rotate_kernel, shift),
        out_shape=jax.ShapeDtypeStruct(packets.shape, packets.dtype),
        in_specs=[pl.BlockSpec(memory_space=pltpu.HBM)],
        out_specs=pl.BlockSpec(memory_space=pltpu.VMEM),
        scratch_shapes=[pltpu.SemaphoreType.DMA, pltpu.SemaphoreType.DMA],
        compiler_params=pltpu.CompilerParams(collective_id=shift, has_side_effects=True),
        name=f"rotate{shift}",
    )(packets)


def stay_kernel(sent_ref, got_ref, sem):
    copy = pltpu.make_async_copy(sent_ref, got_ref, sem)
    copy.start()
    copy.wait()


def stay(packets):
    return pl.pallas_call(
        stay_kernel,
        out_shape=jax.ShapeDtypeStruct(packets.shape, packets.dtype),
        in_specs=[pl.BlockSpec(memory_space=pltpu.HBM)],
        out_specs=pl.BlockSpec(memory_space=pltpu.VMEM),
        scratch_shapes=[pltpu.SemaphoreType.DMA],
        name="stay",
    )(packets)


def land_kernel(row_ref, *refs):
    held, out_ref, sems = refs[:-2], refs[-2], refs[-1]
    copies = []
    for k in range(SLOTS):
        copies.append(pltpu.make_async_copy(held[k // PACK].at[k % PACK], out_ref.at[row_ref[k]], sems.at[k]))
    for copy in copies:
        copy.start()
    for copy in copies:
        copy.wait()


def land(rows, held):
    vm, sm = pl.BlockSpec(memory_space=pltpu.VMEM), pl.BlockSpec(memory_space=pltpu.SMEM)
    return pl.pallas_call(
        land_kernel,
        out_shape=jax.ShapeDtypeStruct((SLOTS, 96, 256), jnp.float32),
        in_specs=[sm] + [vm] * len(held),
        out_specs=pl.BlockSpec(memory_space=pl.ANY),
        scratch_shapes=[pltpu.SemaphoreType.DMA((SLOTS,))],
        name="land",
    )(rows, *held)


def migrate(packets, total, choices, goals, origins, rows):
    branches = [stay] + [functools.partial(rotate, d) for d in range(1, GROUP)]
    flows = SLOTS // PACK

    def few(packets):
        return tuple(
            lax.switch(choices[f][0], branches[f : GROUP - flows + 1 + f], packets[f]) for f in range(flows)
        )

    def many(packets):
        hits = goals[None, :] == jnp.arange(PACK * GROUP)[:, None]
        source = jnp.sum(jnp.where(hits, jnp.arange(SLOTS)[None, :], 0), axis=1)
        slots = jnp.take(jnp.concatenate(packets, axis=0), source, axis=0)
        arrived = lax.all_to_all(slots, RVE, split_axis=0, concat_axis=0, tiled=True)
        held = jnp.take(arrived, origins[:SLOTS], axis=0)
        return tuple(held[PACK * f : PACK * f + PACK] for f in range(flows))

    return land(rows, lax.cond(total == flows, few, many, packets))


def on_device(
    displacement, plastic, bulk_modulus, shear_modulus, yield_radius, counts, migration_plan
):
    plans, used, force, updated = solve(
        migration_plan, displacement, counts, plastic, bulk_modulus, shear_modulus, yield_radius
    )
    total, goals, origins, landing, force, *rest = agenda(plans, used, updated, force)
    flows = SLOTS // PACK
    moved = migrate(tuple(rest[flows:]), total[0], rest[:flows], goals, origins, landing)
    return (force, moved.reshape(plastic.shape))


def solution(mesh):
    finer = Mesh(
        mesh.devices.reshape(8, 4, mesh.shape["mic"], mesh.shape["mac"]),
        ("rve_0", "rve_1", "mic", "mac"),
    )
    placed = (
        P(None, RVE, ("mic", "mac"), None),
        P(RVE_MIC_MAC, None, None, None),
        P(),
        P(),
        P(),
        P(RVE_MIC_MAC),
        P(RVE_MIC_MAC),
    )
    return jax.shard_map(
        on_device,
        mesh=finer,
        in_specs=placed,
        out_specs=(P(None, RVE, ("mic", "mac"), None), P(RVE_MIC_MAC, None, None, None)),
        check_vma=False,
    )
```

```python
import functools
import math

import jax
import jax.numpy as jnp
import numpy as np
from jax import lax
from jax.experimental import pallas as pl
from jax.experimental.pallas import tpu as pltpu
from jax.sharding import Mesh
from jax.sharding import PartitionSpec as P

RVE = ("rve_0", "rve_1")
RVE_MIC_MAC = ("rve_0", "rve_1", "mic", "mac")


COUPLING = 0.7
PAIRS = ((0, 0), (1, 1), (2, 2), (1, 2), (0, 2), (0, 1))


def transform_tables(n):
    plane = np.arange(n * n)
    b, c = plane // n, plane % n
    angle = 2.0 * np.pi / n * ((np.outer(b, b) + np.outer(c, c)) % n)
    table = np.concatenate([np.cos(angle), np.sin(angle)], axis=1).astype(np.float32)
    high = table.astype(jnp.bfloat16)
    low = (table - high.astype(np.float32)).astype(jnp.bfloat16)
    return np.concatenate([high, low], axis=0)


def green_table(n):
    index = np.stack(np.meshgrid(np.arange(n), np.arange(n), np.arange(n), indexing="ij"))

    def operator(i):
        k = ((i + n // 2) % n - n // 2).astype(np.float64)
        q = np.sum(k * k, axis=0)
        safe = np.maximum(q, 1.0)
        rows = []
        for m, r in PAIRS:
            row = []
            for p, s in PAIRS:
                eye = lambda u, v: 1.0 if u == v else 0.0
                first = (
                    eye(m, p) * k[r] * k[s] + eye(m, s) * k[r] * k[p] + eye(r, p) * k[m] * k[s] + eye(r, s) * k[m] * k[p]
                ) / (4.0 * safe)
                row.append(first - COUPLING * k[m] * k[r] * k[p] * k[s] / (safe * safe))
            rows.append(row)
        return np.where(q > 0, np.array(rows), 0.0)

    even = 0.5 * (operator(index) + operator((-index) % n)) / float(n**3)
    even = even[:, :, : n // 2 + 1]
    rows = [even[i, j].reshape(n // 2 + 1, n * n) for i in range(6) for j in range(i, 6)]
    table = np.stack(rows, axis=1).reshape(-1, n * n).astype(np.float32)
    return np.pad(table, ((0, -table.shape[0] % 8), (0, 0)))


def turn(k, n, value, sign):
    re, im = value
    if k == 0:
        return value
    if 4 * k == n:
        return (im, -re) if sign < 0 else (-im, re)
    if 8 * k == n:
        r = math.sqrt(0.5)
        return ((re + im) * r, (im - re) * r) if sign < 0 else ((re - im) * r, (re + im) * r)
    c, s = math.cos(2 * math.pi * k / n), sign * math.sin(2 * math.pi * k / n)
    return (re * c - im * s, re * s + im * c)


def real_forward(x):
    n = len(x)
    if n == 2:
        return [(x[0] + x[1], None), (x[0] - x[1], None)]
    even, odd = real_forward(x[0::2]), real_forward(x[1::2])
    out = [None] * (n // 2 + 1)
    out[0] = (even[0][0] + odd[0][0], None)
    out[n // 2] = (even[0][0] - odd[0][0], None)
    for k in range(1, n // 4 + 1):
        if 4 * k == n:
            out[k] = (even[k][0], -odd[k][0])
        else:
            t = turn(k, n, odd[k], -1)
            out[k] = (even[k][0] + t[0], even[k][1] + t[1])
            out[n // 2 - k] = (even[k][0] - t[0], t[1] - even[k][1])
    return out


def real_backward(y):
    n = 2 * (len(y) - 1)
    if n == 2:
        return [y[0][0] + y[1][0], y[0][0] - y[1][0]]
    even, odd = [None] * (n // 4 + 1), [None] * (n // 4 + 1)
    even[0] = (y[0][0] + y[n // 2][0], None)
    odd[0] = (y[0][0] - y[n // 2][0], None)
    for k in range(1, n // 4 + 1):
        if 4 * k == n:
            even[k] = (2.0 * y[k][0], None)
            odd[k] = (-2.0 * y[k][1], None)
        else:
            o = y[n // 2 - k]
            even[k] = (y[k][0] + o[0], y[k][1] - o[1])
            odd[k] = turn(k, n, (y[k][0] - o[0], y[k][1] + o[1]), 1)
    out = [None] * n
    out[0::2] = real_backward(even)
    out[1::2] = real_backward(odd)
    return out


def flow_rule(elastic, shear2, radius):
    volume = elastic[0] + elastic[1] + elastic[2]
    mean = volume * (1.0 / 3.0)
    deviator = [elastic[i] - mean for i in range(3)] + list(elastic[3:])
    trial = [shear2 * d for d in deviator]
    normal = trial[0] * trial[0] + trial[1] * trial[1] + trial[2] * trial[2]
    mixed = trial[3] * trial[3] + trial[4] * trial[4] + trial[5] * trial[5]
    squared = normal + (mixed + mixed)
    factor = radius * lax.rsqrt(jnp.maximum(squared, radius * radius))
    return volume, deviator, trial, factor


HALVES = (slice(0, 128), slice(128, 256))


def step_kernel(
    plan_ref, nodes_ref, counts_ref, plastic_ref, bulk_ref, shear_ref, radius_ref, dft_hbm, green_hbm,
    rows_ref, used_ref, force_ref, updated_ref,
    row_s, group_s, second_s, across_s, group_sem, across_sem, tile_s, nodes_s, means_s, below_s, nodes_sem, below_sem,
    halves_s, copy_sem, dft_ref, green_ref, table_sem, material_s, green_s, plastic_s,
    strain_s, stress_s, update_s, mapped_s, left_s, product_s, left2_s, product2_s,
):
    f32, bf16 = jnp.float32, jnp.bfloat16
    i32 = jnp.int32
    layer, column = own_place()
    incoming = [
        pltpu.make_async_copy(plastic_ref.at[:, lanes], halves_s.at[h], copy_sem.at[h]) for h, lanes in enumerate(HALVES)
    ]
    tables = [
        pltpu.make_async_copy(green_hbm, green_ref, table_sem.at[0]),
        pltpu.make_async_copy(dft_hbm.at[:256], dft_ref.at[:256], table_sem.at[1]),
        pltpu.make_async_copy(dft_hbm, dft_ref.at[256:], table_sem.at[2]),
    ]
    for copy in incoming + tables:
        copy.start()
    barrier = pltpu.get_barrier_semaphore()

    def greet(layers, columns):
        peer = place((layer + layers) & (GROUP - 1), (column + columns) & (COLUMNS - 1))
        pl.semaphore_signal(barrier, inc=1, device_id=peer, device_id_type=MESH_ID)

    z, x = layer // 4, layer % 4

    def at_x(step):
        return z * 4 + ((x + step) & 3)

    for step in range(1, 4):
        peer = place(at_x(step), column)
        pl.semaphore_signal(barrier, inc=1, device_id=peer, device_id_type=MESH_ID)
    for layers, columns in ((1, 0), (-1, 0), (1, 1), (-1, -1)):
        greet(layers, columns)
    pl.loop(1, 8)(lambda step: greet(4 * step, 0))
    pl.loop(1, COLUMNS)(lambda step: greet(0, step))

    lane = lax.broadcasted_iota(i32, (1, 128), 1)
    sublane = lax.broadcasted_iota(i32, (8, 128), 0)
    lanes8 = lax.broadcasted_iota(i32, (8, 128), 1)
    plan = [plan_ref[i] for i in range(SLOTS)]
    mine = [((value >> 6) - layer) & (GROUP - 1) for value in plan]
    row = jnp.zeros((1, 128), i32)
    counts = jnp.zeros((8, 128), i32)
    tile = jnp.zeros((8, 128), f32)
    for i in range(SLOTS):
        row = jnp.where(lane == i, plan[i], row)
        row = jnp.where(lane == 32 + mine[i], 1, row)
        counts = jnp.where(sublane == i, counts_ref[i], counts)
        for m in range(3):
            tile = jnp.where((sublane == i) & (lanes8 == m), nodes_ref[m, 0, 0, i], tile)
    row_s[0] = row
    tile_s[...] = tile
    for a in range(16):
        shear2 = 2.0 * shear_ref[a : a + 1, :]
        for i, value in enumerate((shear2, bulk_ref[a : a + 1, :], radius_ref[a : a + 1, :])):
            material_s[a, i] = jnp.broadcast_to(value, (8, 256))

    pl.semaphore_wait(barrier, 3 + 4 + 7 + COLUMNS - 1)

    def to(layers, columns):
        return place((layer + layers) & (GROUP - 1), (column + columns) & (COLUMNS - 1))

    def halo(src, dst, sems, sign):
        return [
            pltpu.make_async_remote_copy(
                src_ref=src, dst_ref=dst.at[k], send_sem=sems.at[0, k], recv_sem=sems.at[1, k],
                device_id=to(sign * x, sign * y), device_id_type=MESH_ID,
            )
            for k, (x, y) in enumerate(((1, 0), (0, 1), (1, 1)))
        ]

    def along_row(step):
        return pltpu.make_async_remote_copy(
            src_ref=row_s.at[0], dst_ref=group_s.at[layer], send_sem=group_sem.at[0, step],
            recv_sem=group_sem.at[1, step], device_id=place(at_x(step), column), device_id_type=MESH_ID,
        )

    def along_z(step):
        rows = group_s.at[pl.ds(z * 4, 4)]
        return pltpu.make_async_remote_copy(
            src_ref=rows, dst_ref=rows, send_sem=group_sem.at[0, 4 + step],
            recv_sem=group_sem.at[1, 4 + step], device_id=to(4 * step, 0), device_id_type=MESH_ID,
        )

    def to_column(step):
        return pltpu.make_async_remote_copy(
            src_ref=second_s.at[0], dst_ref=across_s.at[column], send_sem=across_sem.at[0, step],
            recv_sem=across_sem.at[1, step], device_id=to(0, step), device_id_type=MESH_ID,
        )

    nodes_halo = halo(tile_s, nodes_s, nodes_sem, -1)
    for copy in nodes_halo:
        copy.start()
    for step in range(1, 4):
        along_row(step).start()
    group_s[layer] = row

    for copy in incoming:
        copy.wait()

    @pl.loop(0, 96, unroll=4)
    def _(row):
        for h, lanes in enumerate(HALVES):
            plastic_s[row, :, lanes] = halves_s[h, pl.ds(row, 8, stride=96), :]

    @pl.loop(0, 96, unroll=8)
    def _(row):
        update_s[row] = jnp.zeros((8, 256), f32)
        mapped_s[row] = jnp.zeros((8, 256), f32)

    for copy in nodes_halo:
        copy.wait()
    zero = jnp.zeros((8, 128), f32)

    def gradients(t00, t10, t01, t11, shift):
        along_x = 0.25 * ((t10 + t11) - (t00 + t01))
        along_y = 0.25 * ((t01 + t11) - (t00 + t10))
        along_z = 0.25 * ((t00 + t10) + (t01 + t11))
        return along_x + shift(along_x), along_y + shift(along_y), shift(along_z) - along_z

    inner_x, inner_y = layer < GROUP - 1, column < COLUMNS - 1
    by_x, by_y, by_z = gradients(
        tile,
        jnp.where(inner_x, nodes_s[0], zero),
        jnp.where(inner_y, nodes_s[1], zero),
        jnp.where(inner_x & inner_y, nodes_s[2], zero),
        lambda value: jnp.where(sublane < 7, pltpu.roll(value, 7, 0), zero),
    )
    macro = [
        by_x[:, 0:1],
        by_y[:, 1:2],
        by_z[:, 2:3],
        0.5 * (by_z[:, 1:2] + by_y[:, 2:3]),
        0.5 * (by_z[:, 0:1] + by_x[:, 2:3]),
        0.5 * (by_y[:, 0:1] + by_x[:, 1:2]),
    ]
    for c in range(6):
        start = jnp.broadcast_to(macro[c], (8, 256))

        @pl.loop(0, 16, unroll=8)
        def _(a):
            strain_s[c * 16 + a] = start

    def split(value):
        high = value.astype(bf16)
        low = (value - high.astype(f32)).astype(bf16)
        return high, low

    def polarization(step):
        @pl.loop(0, 16)
        def _(a):
            for lanes in HALVES:
                shear2 = material_s[a, 0, :, lanes]
                bulk = material_s[a, 1, :, lanes]
                radius = material_s[a, 2, :, lanes]
                elastic = [strain_s[c * 16 + a, :, lanes] - plastic_s[c * 16 + a, :, lanes] for c in range(6)]
                volume, _, trial, factor = flow_rule(elastic, shear2, radius)
                pressure = bulk * volume
                for c in range(6):
                    value = factor * trial[c]
                    stress_s[c * 16 + a, :, lanes] = value + pressure if c < 3 else value

        @pl.loop(0, 3)
        def _(pair):
            for lanes in HALVES:
                sets = []
                for half in range(2):
                    y = real_forward([stress_s[pair * 32 + half * 16 + a, :, lanes] for a in range(16)])
                    sets.append([y[0][0], y[8][0]] + [part for k in range(1, 8) for part in y[k]])
                rows = pl.ds(pl.multiple_of(pair * 16, 16), 16)
                for r in range(16):
                    high, low = split(jnp.concatenate([sets[0][r], sets[1][r]], axis=0))
                    left_s[r, rows, lanes] = high
                    left_s[r, rows, slice(256 + lanes.start, 256 + lanes.stop)] = low

        @pl.when(step == 0)
        def _():
            tables[1].wait()
            tables[2].wait()
            tables[0].wait()

            @pl.loop(0, 24)
            def _(block):
                rows = green_ref[pl.ds(pl.multiple_of(block * 8, 8), 8), :]
                for r in range(8):
                    green_s[block * 8 + r] = jnp.broadcast_to(rows[r : r + 1, :], (8, 256))

        left = left_s[...].reshape(768, 512)
        product_s[...] = jnp.dot(
            jnp.concatenate([left, left[:, :256]], axis=1), dft_ref[...], preferred_element_type=f32
        ).reshape(16, 48, 512)

        def operate(k, re, im, lanes):
            for t, value in ((2 * k, re), (2 * k + 1, im)):
                value = value[:3] + [v + v for v in value[3:]]
                out = [None] * 6
                j = 0
                for i in range(6):
                    for m in range(i, 6):
                        g = green_s[k * 21 + j, :, lanes]
                        j += 1
                        out[i] = g * value[m] if out[i] is None else out[i] + g * value[m]
                        if m != i:
                            out[m] = g * value[i] if out[m] is None else out[m] + g * value[i]
                for pair in range(3):
                    high, low = split(jnp.concatenate([out[2 * pair], out[2 * pair + 1]], axis=0))
                    left2_s[t, slice(pair * 16, pair * 16 + 16), lanes] = high
                    left2_s[t, slice(pair * 16, pair * 16 + 16), slice(256 + lanes.start, 256 + lanes.stop)] = low

        for k, row in ((0, 0), (8, 1)):
            for lanes in HALVES:
                wide = slice(256 + lanes.start, 256 + lanes.stop)
                re = [product_s[row, slice(c * 8, c * 8 + 8), lanes] for c in range(6)]
                im = [-product_s[row, slice(c * 8, c * 8 + 8), wide] for c in range(6)]
                operate(k, re, im, lanes)

        @pl.loop(1, 8)
        def _(k):
            for lanes in HALVES:
                wide = slice(256 + lanes.start, 256 + lanes.stop)
                re, im = [], []
                for c in range(6):
                    rows = slice(c * 8, c * 8 + 8)
                    re.append(product_s[2 * k, rows, lanes] + product_s[2 * k + 1, rows, wide])
                    im.append(product_s[2 * k + 1, rows, lanes] - product_s[2 * k, rows, wide])
                operate(k, re, im, lanes)

        left2 = left2_s[...].reshape(864, 512)
        product2_s[...] = jnp.dot(
            jnp.concatenate([left2, left2[:, :256]], axis=1), dft_ref[...], preferred_element_type=f32
        ).reshape(18, 48, 512)

    def update_of(c, lanes):
        wide = slice(256 + lanes.start, 256 + lanes.stop)
        rows = pl.ds(pl.multiple_of(c * 8, 8), 8)
        y = []
        for k in range(9):
            re = product2_s[2 * k, rows, lanes] - product2_s[2 * k + 1, rows, wide]
            im = None if k in (0, 8) else product2_s[2 * k, rows, wide] + product2_s[2 * k + 1, rows, lanes]
            y.append((re, im))
        return real_backward(y)

    @pl.loop(0, 3)
    def _(step):
        polarization(step)

        @pl.when(step == 0)
        def _():
            for peer in range(1, 4):
                along_row(peer).wait()
            pl.loop(1, 8)(lambda peer: along_z(peer).start())

        @pl.when(step == 1)
        def _():
            pl.loop(1, 8)(lambda peer: along_z(peer).wait())
            union = group_s[0]
            for i in range(1, GROUP):
                union = jnp.maximum(union, group_s[i])
            second_s[0] = union
            across_s[column] = union
            pl.loop(1, COLUMNS)(lambda peer: to_column(peer).start())

        zero = jnp.zeros((8, 128), f32)

        def gather(c, carry):
            numerator, denominator = carry
            for lanes in HALVES:
                update = update_of(c, lanes)
                for a in range(16):
                    change = update[a] - update_s[c * 16 + a, :, lanes]
                    numerator = numerator + change * update[a]
                    denominator = denominator + change * change
                    update_s[c * 16 + a, :, lanes] = update[a]
            return numerator, denominator

        numerator, denominator = lax.fori_loop(0, 6, gather, (zero, zero))
        scale = 1.0 / float(6 * 16**3)
        numerator = jnp.sum(numerator, axis=1, keepdims=True) * scale
        denominator = jnp.sum(denominator, axis=1, keepdims=True) * scale + 1e-06
        weight = jnp.broadcast_to(jnp.where(step > 0, numerator / denominator, 0.0), (8, 256))
        active = step < jnp.concatenate([counts, counts], axis=1)

        @pl.loop(0, 96, unroll=4)
        def _(row):
            strain = strain_s[row]
            mapped = strain - update_s[row]
            candidate = mapped - weight * (mapped - mapped_s[row])
            mapped_s[row] = mapped
            strain_s[row] = jnp.where(active, candidate, strain)

    def finish(a, sums):
        sums = list(sums)
        for lanes in HALVES:
            shear2 = material_s[a, 0, :, lanes]
            bulk = material_s[a, 1, :, lanes]
            radius = material_s[a, 2, :, lanes]
            plastic = [plastic_s[c * 16 + a, :, lanes] for c in range(6)]
            elastic = [strain_s[c * 16 + a, :, lanes] - plastic[c] for c in range(6)]
            volume, deviator, trial, factor = flow_rule(elastic, shear2, radius)
            pressure = bulk * volume
            for c in range(6):
                value = factor * trial[c]
                sums[c] = sums[c] + (value + pressure if c < 3 else value)
                plastic_s[c * 16 + a, :, lanes] = plastic[c] + (deviator[c] - factor * deviator[c])
        return tuple(sums)

    sums = lax.fori_loop(0, 16, finish, (zero,) * 6)
    means = zero
    for c in range(6):
        means = jnp.where(lanes8 == c, jnp.sum(sums[c], axis=1, keepdims=True) * (1.0 / 4096.0), means)
    means_s[...] = means
    stress_halo = halo(means_s, below_s, below_sem, 1)
    for copy in stress_halo:
        copy.start()

    @pl.loop(0, 96, unroll=4)
    def _(row):
        for h, lanes in enumerate(HALVES):
            updated_ref[h, pl.ds(row, 8, stride=96), :] = plastic_s[row, :, lanes]

    for copy in stress_halo:
        copy.wait()
    inner_x, inner_y = layer > 0, column > 0
    by_x, by_y, by_z = gradients(
        means,
        jnp.where(inner_x, below_s[0], zero),
        jnp.where(inner_y, below_s[1], zero),
        jnp.where(inner_x & inner_y, below_s[2], zero),
        lambda value: jnp.where(sublane > 0, pltpu.roll(value, 1, 0), zero),
    )
    force = zero
    for i, (p, q, r) in enumerate(((0, 5, 4), (5, 1, 3), (4, 3, 2))):
        value = by_x[:, p : p + 1] + by_y[:, q : q + 1] + by_z[:, r : r + 1]
        force = jnp.where(lanes8 == i, value, force)
    force_ref[...] = force
    pl.loop(1, COLUMNS)(lambda peer: to_column(peer).wait())
    used = across_s[0]
    for i in range(1, COLUMNS):
        used = jnp.maximum(used, across_s[i])
    used_ref[...] = used
    rows_ref[...] = group_s[...]


def solve(plan, nodes, counts, plastic, bulk, shear, radius):
    f32, bf16, i32 = jnp.float32, jnp.bfloat16, jnp.int32
    vm, sm = pl.BlockSpec(memory_space=pltpu.VMEM), pl.BlockSpec(memory_space=pltpu.SMEM)
    anywhere = pl.BlockSpec(memory_space=pltpu.HBM)
    return pl.pallas_call(
        step_kernel,
        out_shape=(
            jax.ShapeDtypeStruct((GROUP, 1, 128), i32),
            jax.ShapeDtypeStruct((1, 128), i32),
            jax.ShapeDtypeStruct((8, 128), f32),
            jax.ShapeDtypeStruct((2, 768, 128), f32),
        ),
        in_specs=[sm] * 3 + [anywhere] + [vm] * 3 + [anywhere] * 2,
        out_specs=(vm,) * 4,
        scratch_shapes=[
            pltpu.VMEM((1, 1, 128), i32),
            pltpu.VMEM((GROUP, 1, 128), i32),
            pltpu.VMEM((1, 1, 128), i32),
            pltpu.VMEM((COLUMNS, 1, 128), i32),
            pltpu.SemaphoreType.DMA((2, 12)),
            pltpu.SemaphoreType.DMA((2, COLUMNS)),
            pltpu.VMEM((8, 128), f32),
            pltpu.VMEM((3, 8, 128), f32),
            pltpu.VMEM((8, 128), f32),
            pltpu.VMEM((3, 8, 128), f32),
            pltpu.SemaphoreType.DMA((2, 3)),
            pltpu.SemaphoreType.DMA((2, 3)),
            pltpu.VMEM((2, 768, 128), f32),
            pltpu.SemaphoreType.DMA((2,)),
            pltpu.VMEM((768, 512), bf16),
            pltpu.VMEM((192, 256), f32),
            pltpu.SemaphoreType.DMA((3,)),
            pltpu.VMEM((16, 3, 8, 256), f32),
            pltpu.VMEM((192, 8, 256), f32),
            pltpu.VMEM((96, 8, 256), f32),
            pltpu.VMEM((96, 8, 256), f32),
            pltpu.VMEM((96, 8, 256), f32),
            pltpu.VMEM((96, 8, 256), f32),
            pltpu.VMEM((96, 8, 256), f32),
            pltpu.VMEM((16, 48, 512), bf16),
            pltpu.VMEM((16, 48, 512), f32),
            pltpu.VMEM((18, 48, 512), bf16),
            pltpu.VMEM((18, 48, 512), f32),
        ],
        compiler_params=pltpu.CompilerParams(
            collective_id=0, has_side_effects=True, vmem_limit_bytes=60 << 20
        ),
        name="step",
    )(
        plan,
        nodes,
        counts,
        plastic.reshape(768, 256),
        bulk,
        shear,
        radius,
        jnp.asarray(transform_tables(16)),
        jnp.asarray(green_table(16)),
    )


MESH_ID = pl.DeviceIdType.MESH
GROUP, COLUMNS, SLOTS, PACK = 32, 8, 8, 2


def place(layer, column):
    return {"rve_0": layer // 4, "rve_1": layer % 4, "mic": column // 2, "mac": column % 2}


def own_place():
    layer = lax.axis_index("rve_0") * 4 + lax.axis_index("rve_1")
    return layer, lax.axis_index("mic") * 2 + lax.axis_index("mac")


def agenda_kernel(
    plan_ref, used_ref, updated_ref, force_ref, total_ref, goal_ref, origin_ref, row_ref, nodal_ref, *rest
):
    layer, _ = own_place()
    flows = SLOTS // PACK
    branch_refs, packets, (sems, shift_ref) = rest[:flows], rest[flows : 2 * flows], rest[2 * flows :]
    mine = [((plan_ref[layer, 0, i] >> 6) - layer) & (GROUP - 1) for i in range(SLOTS)]
    order_rank = []
    for i in range(SLOTS):
        rank = jnp.int32(0)
        for k in range(SLOTS):
            if k != i:
                rank = rank + jnp.where(mine[k] <= mine[i] if k < i else mine[k] < mine[i], 1, 0)
        goal_ref[rank] = PACK * ((layer + mine[i]) & (GROUP - 1)) + (rank & (PACK - 1))
        order_rank.append(rank)
    copies = []
    for k in range(SLOTS):
        index = jnp.int32(0)
        for i in range(SLOTS):
            index = jnp.where(order_rank[i] == k, i, index)
        rows = pl.ds(pl.multiple_of(index * 96, 96), 96)
        for h, lanes in enumerate(HALVES):
            copies.append(
                pltpu.make_async_copy(
                    updated_ref.at[h, rows], packets[k // PACK].at[k % PACK, :, lanes], sems.at[2 * k + h]
                )
            )
    for copy in copies:
        copy.start()
    total = jnp.int32(0)
    for d in range(GROUP):
        shift_ref[total] = jnp.int32(d)
        total = total + jnp.where(used_ref[0, 32 + d] > 0, 1, 0)
    total_ref[0] = total
    for f in range(flows):
        branch_refs[f][0] = jnp.clip(shift_ref[f] - f, 0, GROUP - flows)
    turned = jnp.transpose(force_ref[...])
    for i in range(3):
        nodal_ref[i, 0] = turned[i : i + 1]

    def step(i, count):
        shift = shift_ref[i]
        source = (layer - shift) & (GROUP - 1)
        for k in range(SLOTS):
            value = plan_ref[source, 0, k]
            row_ref[count] = value & (SLOTS - 1)
            origin_ref[count] = PACK * source + (count & (PACK - 1))
            count = jnp.minimum(count + jnp.where((value >> 6) == layer, 1, 0), SLOTS)
        return count

    lax.fori_loop(0, total, step, jnp.int32(0))
    for copy in copies:
        copy.wait()


def agenda(plan, used, updated, force):
    sm, vm = pl.BlockSpec(memory_space=pltpu.SMEM), pl.BlockSpec(memory_space=pltpu.VMEM)
    pair = jax.ShapeDtypeStruct((PACK, 96, 256), jnp.float32)
    flows = SLOTS // PACK
    sizes = (1, SLOTS, SLOTS + 1, SLOTS + 1)
    scalar, nodal = jax.ShapeDtypeStruct((1,), jnp.int32), jax.ShapeDtypeStruct((3, 1, 1, 8), jnp.float32)
    return pl.pallas_call(
        agenda_kernel,
        out_shape=tuple(jax.ShapeDtypeStruct((size,), jnp.int32) for size in sizes)
        + (nodal,) + (scalar,) * flows + (pair,) * flows,
        in_specs=[sm, sm, vm, vm],
        out_specs=(sm,) * len(sizes) + (vm,) + (sm,) * flows + (pl.BlockSpec(memory_space=pltpu.HBM),) * flows,
        scratch_shapes=[pltpu.SemaphoreType.DMA((2 * SLOTS,)), pltpu.SMEM((GROUP + 1,), jnp.int32)],
        name="agenda",
    )(plan, used, updated, force)


def rotate_kernel(shift, sent_ref, got_ref, send_sem, recv_sem):
    layer, column = own_place()
    target, source = (layer + shift) & (GROUP - 1), (layer - shift) & (GROUP - 1)
    barrier = pltpu.get_barrier_semaphore()
    pl.semaphore_signal(barrier, inc=1, device_id=place(source, column), device_id_type=MESH_ID)
    pl.semaphore_wait(barrier, 1)
    copies = [
        pltpu.make_async_remote_copy(
            src_ref=sent_ref.at[j],
            dst_ref=got_ref.at[j],
            send_sem=send_sem.at[j],
            recv_sem=recv_sem.at[j],
            device_id=place(target, column),
            device_id_type=MESH_ID,
        )
        for j in range(PACK)
    ]
    for copy in copies:
        copy.start()
    for copy in copies:
        copy.wait()


def rotate(shift, packets):
    return pl.pallas_call(
        functools.partial(rotate_kernel, shift),
        out_shape=jax.ShapeDtypeStruct(packets.shape, packets.dtype),
        in_specs=[pl.BlockSpec(memory_space=pltpu.HBM)],
        out_specs=pl.BlockSpec(memory_space=pltpu.VMEM),
        scratch_shapes=[pltpu.SemaphoreType.DMA((PACK,)), pltpu.SemaphoreType.DMA((PACK,))],
        compiler_params=pltpu.CompilerParams(collective_id=shift, has_side_effects=True),
        name=f"rotate{shift}",
    )(packets)


def stay_kernel(sent_ref, got_ref, sem):
    copy = pltpu.make_async_copy(sent_ref, got_ref, sem)
    copy.start()
    copy.wait()


def stay(packets):
    return pl.pallas_call(
        stay_kernel,
        out_shape=jax.ShapeDtypeStruct(packets.shape, packets.dtype),
        in_specs=[pl.BlockSpec(memory_space=pltpu.HBM)],
        out_specs=pl.BlockSpec(memory_space=pltpu.VMEM),
        scratch_shapes=[pltpu.SemaphoreType.DMA],
        name="stay",
    )(packets)


def land_kernel(row_ref, *refs):
    held, out_ref, sems = refs[:-2], refs[-2], refs[-1]
    copies = []
    for k in range(SLOTS):
        copies.append(pltpu.make_async_copy(held[k // PACK].at[k % PACK], out_ref.at[row_ref[k]], sems.at[k]))
    for copy in copies:
        copy.start()
    for copy in copies:
        copy.wait()


def land(rows, held):
    vm, sm = pl.BlockSpec(memory_space=pltpu.VMEM), pl.BlockSpec(memory_space=pltpu.SMEM)
    return pl.pallas_call(
        land_kernel,
        out_shape=jax.ShapeDtypeStruct((SLOTS, 96, 256), jnp.float32),
        in_specs=[sm] + [vm] * len(held),
        out_specs=pl.BlockSpec(memory_space=pl.ANY),
        scratch_shapes=[pltpu.SemaphoreType.DMA((SLOTS,))],
        name="land",
    )(rows, *held)


def migrate(packets, total, choices, goals, origins, rows):
    branches = [stay] + [functools.partial(rotate, d) for d in range(1, GROUP)]
    flows = SLOTS // PACK

    def few(packets):
        return tuple(
            lax.switch(choices[f][0], branches[f : GROUP - flows + 1 + f], packets[f]) for f in range(flows)
        )

    def many(packets):
        hits = goals[None, :] == jnp.arange(PACK * GROUP)[:, None]
        source = jnp.sum(jnp.where(hits, jnp.arange(SLOTS)[None, :], 0), axis=1)
        slots = jnp.take(jnp.concatenate(packets, axis=0), source, axis=0)
        arrived = lax.all_to_all(slots, RVE, split_axis=0, concat_axis=0, tiled=True)
        held = jnp.take(arrived, origins[:SLOTS], axis=0)
        return tuple(held[PACK * f : PACK * f + PACK] for f in range(flows))

    return land(rows, lax.cond(total == flows, few, many, packets))


def on_device(
    displacement, plastic, bulk_modulus, shear_modulus, yield_radius, counts, migration_plan
):
    plans, used, force, updated = solve(
        migration_plan, displacement, counts, plastic, bulk_modulus, shear_modulus, yield_radius
    )
    total, goals, origins, landing, force, *rest = agenda(plans, used, updated, force)
    flows = SLOTS // PACK
    moved = migrate(tuple(rest[flows:]), total[0], rest[:flows], goals, origins, landing)
    return (force, moved.reshape(plastic.shape))


def solution(mesh):
    finer = Mesh(
        mesh.devices.reshape(8, 4, mesh.shape["mic"], mesh.shape["mac"]),
        ("rve_0", "rve_1", "mic", "mac"),
    )
    placed = (
        P(None, RVE, ("mic", "mac"), None),
        P(RVE_MIC_MAC, None, None, None),
        P(),
        P(),
        P(),
        P(RVE_MIC_MAC),
        P(RVE_MIC_MAC),
    )
    return jax.shard_map(
        on_device,
        mesh=finer,
        in_specs=placed,
        out_specs=(P(None, RVE, ("mic", "mac"), None), P(RVE_MIC_MAC, None, None, None)),
        check_vma=False,
    )
```
